512 devices in a mesh: ctx: 32 (over z_hi, y, core), tp: 16 (over x, z_lo).
Axes of the slice: x: 4, y: 8, z: 8 (z_hi: 2, z_lo: 4; z = z_hi * 4 + z_lo), core: 2. Of those that a mesh axis runs over, the one named last changes fastest.
Arguments:
- residual: bfloat16 [4352, 8192], P('ctx', 'tp'), may hold values from -64 to 64
- gate_first: bfloat16 [4352, 8192], P('ctx', 'tp'), may hold values from -6 to 6
- gate_second: bfloat16 [4352, 8192], P('ctx', 'tp'), may hold values from -6 to 6
- hyena_value: bfloat16 [4352, 8192], P('ctx', 'tp'), may hold values from -6 to 6
- short_taps: float32 [3, 3, 8192], P(None, None, 'tp'), may hold values from -3.5 to 3.5
- long_taps: bfloat16 [128, 8192], P(None, 'tp'), may hold values from -0.5 to 0.5
- norm_gain: float32 [8192], P('tp'), may hold values from 0.1 to 1.9
- queries: bfloat16 [4352, 8192], P('ctx', 'tp'), may hold values from -8 to 8
- attn_keys: bfloat16 [4352, 8192], P('ctx', 'tp'), may hold values from -8 to 8
Outputs:
- stream: bfloat16 [4352, 8192], P('ctx', 'tp')
- attended: bfloat16 [4352, 8192], P('ctx', 'tp')
The draws below stay inside these ranges and needn't reach their ends.
All inputs are finite; a program needn't handle non-finite values.
Results may differ from the reference program's by a relative error of at most 0.007.
Values may be sent and summed in bfloat16 or wider, within the bound.
No kernel may reach another device: no remote copies, remote signals or barrier semaphores. Data moves between devices by JAX's collectives and lax.ppermute only.
A program may use at most 64 MiB of HBM per device.

```python
import math
import jax
import jax.numpy as jnp
from jax import lax

HEADS = 64
HD = 128
D = 8192
FILT = 128
SHORT = 3
SEQ = 4352


def draw_residual(key, part):
    base_key = jax.random.fold_in(key, 3)
    key_base, key_row, key_col = jax.random.split(base_key, 3)
    position = jnp.arange(D, dtype=jnp.float32) / D - 0.5
    base = jnp.clip(jax.random.normal(key_base, (SEQ, D), jnp.float32), -4.0, 4.0)
    row_scale = jnp.exp(jax.random.uniform(key_row, (SEQ, 1), jnp.float32, math.log(0.3), math.log(3.0)))
    col_scale = jnp.exp(jax.random.uniform(key_col, (1, D), jnp.float32, math.log(0.3), math.log(3.0)) + math.log(3.0) * position[None, :])
    return (base * row_scale * col_scale).astype(jnp.bfloat16)


def query_key_pair(key):
    base_key = jax.random.fold_in(key, 11)
    key_query, key_key = jax.random.split(base_key, 2)
    query_vals = jnp.clip(2.0 * jax.random.normal(key_query, (SEQ, D), jnp.float32), -8.0, 8.0)
    key_vals = jnp.clip(2.0 * jax.random.normal(key_key, (SEQ, D), jnp.float32), -8.0, 8.0)
    return (query_vals.astype(jnp.bfloat16), key_vals.astype(jnp.bfloat16))


def draw_queries(key, part):
    return query_key_pair(key)[0]


def draw_attn_keys(key, part):
    return query_key_pair(key)[1]


def block_levels(rng, dims, cuts, smallest, top_value):
    def one(axis_at, parts):
        draws = jax.random.uniform(jax.random.fold_in(jax.random.fold_in(rng, 6), axis_at), (parts,), jnp.float32, smallest / len(cuts), top_value / len(cuts))
        return jnp.repeat(jnp.exp(draws), dims[axis_at] // parts).reshape((-1,) + (1,) * (len(dims) - axis_at - 1))

    loudness = one(*cuts[0])
    for cut in cuts[1:]:
        loudness = loudness * one(*cut)
    return loudness


def scatter_about(rng, dims, width, most, cuts=(), kind=jnp.bfloat16):
    loudness = block_levels(rng, dims, cuts, -0.22, 0.18) if cuts else 1.0
    drawn = jax.random.normal(rng, dims, jnp.float32) * width * loudness
    return jnp.minimum(jnp.maximum(drawn, -most), most).astype(kind)


def setup_inputs(seed: int = 0) -> dict:
    key_of = jax.random.split(jax.random.key(seed), 10)
    residual = draw_residual(jax.random.fold_in(key_of[9], 71), 0)
    gate_first = scatter_about(key_of[1], (SEQ, D), 1.0, 6.0, ((0, 32), (1, 16)))
    gate_second = scatter_about(key_of[2], (SEQ, D), 1.0, 6.0, ((0, 32), (1, 16)))
    hyena_value = scatter_about(key_of[3], (SEQ, D), 1.0, 6.0, ((0, 32), (1, 16)))
    short_taps = scatter_about(key_of[4], (3, SHORT, D), SHORT ** -0.5, 3.5, ((2, 16),), jnp.float32)
    long_taps = scatter_about(key_of[5], (FILT, D), FILT ** -0.5, 0.5, ((1, 16),))
    norm_gain = jnp.clip(1.0 + 0.18 * jax.random.normal(key_of[6], (D,), jnp.float32), 0.1, 1.9)
    queries = draw_queries(jax.random.fold_in(key_of[9], 71), 0)
    attn_keys = draw_attn_keys(jax.random.fold_in(key_of[9], 71), 0)
    return dict(residual=residual, gate_first=gate_first, gate_second=gate_second, hyena_value=hyena_value, short_taps=short_taps, long_taps=long_taps, norm_gain=norm_gain, queries=queries, attn_keys=attn_keys)


def featurize(source, tap_weights):
    count = tap_weights.shape[0]
    length = source.shape[0]
    padded = jnp.pad(source.astype(jnp.float32), ((count - 1, 0), (0, 0)))
    result = jnp.zeros(source.shape, jnp.float32)
    for lag_index in range(count):
        begin = count - 1 - lag_index
        result = result + tap_weights[lag_index] * padded[begin:begin + length]
    return result

def reference(residual, gate_first, gate_second, hyena_value, short_taps, long_taps, norm_gain, queries, attn_keys):
    feat_first = featurize(gate_first, short_taps[0])
    feat_second = featurize(gate_second, short_taps[1])
    feat_value = featurize(hyena_value, short_taps[2])
    product = (feat_first * feat_value).astype(jnp.bfloat16)
    length = SEQ + FILT
    spectrum = jnp.fft.rfft(product.astype(jnp.float32), n=length, axis=0) * jnp.fft.rfft(long_taps.astype(jnp.float32), n=length, axis=0)
    filtered = jnp.fft.irfft(spectrum, n=length, axis=0)[:SEQ].astype(jnp.float32)
    stream = (residual.astype(jnp.float32) + feat_second * filtered).astype(jnp.bfloat16)
    stream_f = stream.astype(jnp.float32)
    inverse = 1.0 / jnp.sqrt(lax.optimization_barrier(jnp.mean(stream_f * stream_f, axis=1)) + 1e-06)
    values = (stream_f * inverse[:, None] * norm_gain).astype(jnp.bfloat16)
    scale = 1.0 / math.sqrt(HD)
    query_heads = queries.reshape(SEQ, HEADS, HD).transpose(1, 0, 2)
    key_heads = attn_keys.reshape(SEQ, HEADS, HD).transpose(1, 0, 2)
    value_heads = values.reshape(SEQ, HEADS, HD).transpose(1, 0, 2)
    positions = jnp.arange(SEQ)
    allowed = positions[None, :] <= positions[:, None]

    def one_head(operands):
        query_h, key_h, value_h = operands
        scores = jnp.dot(query_h, key_h.T, preferred_element_type=jnp.float32) * scale
        masked = jnp.where(allowed, scores, -1e+30)
        top_score = lax.optimization_barrier(jnp.max(masked, axis=1, keepdims=True))
        expo = jnp.where(allowed, jnp.exp(scores - top_score), 0.0)
        denom = lax.optimization_barrier(jnp.sum(expo, axis=1, keepdims=True))
        weights = expo.astype(jnp.bfloat16)
        numer = jnp.dot(weights, value_h, preferred_element_type=jnp.float32)
        return numer / denom
    outputs = lax.map(one_head, (query_heads, key_heads, value_heads))
    attended = outputs.transpose(1, 0, 2).reshape(SEQ, HEADS * HD).astype(jnp.bfloat16)
    return (stream, attended)
```

```python
import functools
import math

import jax
import jax.numpy as jnp
from jax import lax
from jax.experimental import pallas as pl
from jax.experimental.pallas import tpu as pltpu
from jax.sharding import Mesh, PartitionSpec as P

HD = 128
ROWS_AXES = ("zh", "s", "h", "c")
CHAN_AXES = ("x", "zl")
PEERS = ("zh", "s", "h")
HIGHEST = lax.Precision.HIGHEST


def front_kernel(gf, gs, hv, res, halo, taps, long_taps, stream, packed, squares, ext, prod, copies):
    rows = gf.shape[0]
    lanes = gf.shape[1]

    def extended(own, prev):
        ext[0:rows, :] = prev.astype(jnp.float32)
        ext[rows : 2 * rows, :] = own.astype(jnp.float32)

    def featurize(index, begin, count):
        total = taps[index, 0:1, :] * ext[begin : begin + count, :]
        total = total + taps[index, 1:2, :] * ext[begin - 1 : begin - 1 + count, :]
        return total + taps[index, 2:3, :] * ext[begin - 2 : begin - 2 + count, :]

    span = 2 * rows - 8
    extended(gf[...], halo[0:rows, :])
    prod[8:, :] = featurize(0, 8, span)
    extended(hv[...], halo[rows : 2 * rows, :])
    value = (prod[8:, :] * featurize(2, 8, span)).astype(jnp.bfloat16)
    prod[0:8, :] = jnp.zeros((8, lanes), jnp.float32)
    prod[8:, :] = value.astype(jnp.float32)
    for lag in range(8):
        copies[lag, 8:, :] = prod[8 - lag : 2 * rows - lag, :]

    tiles = rows // 8

    def lag_group(group, totals):
        weights = long_taps[pl.ds(pl.multiple_of(group * 8, 8), 8), :].astype(jnp.float32)
        base = rows - group * 8
        totals = list(totals)
        for lag in range(8):
            weight = jnp.broadcast_to(weights[lag : lag + 1, :], (8, lanes))
            for tile in range(tiles):
                window = copies[lag, pl.ds(pl.multiple_of(base + tile * 8, 8), 8), :]
                totals[tile] = totals[tile] + weight * window
        return tuple(totals)

    zero = jnp.zeros((8, lanes), jnp.float32)
    totals = lax.fori_loop(0, long_taps.shape[0] // 8, lag_group, (zero,) * tiles)
    filtered = jnp.concatenate(totals, axis=0)

    ext[rows - 8 : rows, :] = halo[2 * rows : 2 * rows + 8, :].astype(jnp.float32)
    ext[rows : 2 * rows, :] = gs[...].astype(jnp.float32)
    out = (res[...].astype(jnp.float32) + featurize(1, rows, rows) * filtered).astype(jnp.bfloat16)
    stream[...] = out
    for copy in range(packed.shape[0]):
        packed[copy, 0] = out
    wide = out.astype(jnp.float32)
    part = lax.dot_general(
        jnp.ones((squares.shape[0], lanes), jnp.float32),
        wide * wide,
        (((1,), (1,)), ((), ())),
        precision=HIGHEST,
        preferred_element_type=jnp.float32,
    )

    @pl.when(pl.program_id(0) == 0)
    def _():
        squares[...] = part

    @pl.when(pl.program_id(0) > 0)
    def _():
        squares[...] = squares[...] + part


def front(gf, gs, hv, res, halo, taps, long_taps):
    rows, chans = gf.shape
    heads = chans // HD
    column = lambda n: pl.BlockSpec((n, HD), lambda i: (0, i))
    return pl.pallas_call(
        front_kernel,
        grid=(heads,),
        in_specs=[
            column(rows),
            column(rows),
            column(rows),
            column(rows),
            column(halo.shape[0]),
            pl.BlockSpec((3, 3, HD), lambda i: (0, 0, i)),
            column(long_taps.shape[0]),
        ],
        out_specs=[
            column(rows),
            pl.BlockSpec((4, 1, rows, HD), lambda i: (0, i, 0, 0)),
            pl.BlockSpec((16, rows), lambda i: (0, 0)),
        ],
        out_shape=[
            jax.ShapeDtypeStruct((rows, chans), jnp.bfloat16),
            jax.ShapeDtypeStruct((4, heads, rows, HD), jnp.bfloat16),
            jax.ShapeDtypeStruct((16, rows), jnp.float32),
        ],
        scratch_shapes=[
            pltpu.VMEM((2 * rows, HD), jnp.float32),
            pltpu.VMEM((2 * rows, HD), jnp.float32),
            pltpu.VMEM((8, 2 * rows, HD), jnp.float32),
        ],
        compiler_params=pltpu.CompilerParams(vmem_limit_bytes=32 << 20),
        cost_estimate=pl.CostEstimate(flops=40_000_000, bytes_accessed=2_000_000, transcendentals=0),
        name="front",
    )(gf, gs, hv, res, halo, taps, long_taps)


def score_kernel(place, q, k_own, k_other, weights, denom, scores):
    rows = q.shape[1]
    keys = k_own.shape[0]
    unit = math.log2(math.e) / math.sqrt(HD)
    chunks = [(begin, min(256, keys - begin)) for begin in range(0, keys, 256)]

    def query_block(index, carry):
        query = q[index]
        query_pos = place[0] + index * 2 * rows + lax.broadcasted_iota(jnp.int32, (rows, 1), 0)
        top = None
        for half, ref in enumerate((k_own, k_other)):
            for begin, width in chunks:
                score = lax.dot_general(
                    query,
                    ref[begin : begin + width, :],
                    (((1,), (1,)), ((), ())),
                    preferred_element_type=jnp.float32,
                )
                lane = begin + lax.broadcasted_iota(jnp.int32, (1, width), 1)
                key_pos = place[1 + half] + lane
                for edge in range(rows, keys, rows):
                    if edge < begin + width:
                        key_pos = key_pos + jnp.where(lane >= edge, rows, 0)
                score = jnp.where(key_pos <= query_pos, score * unit, -1e30)
                scores[:, half * keys + begin : half * keys + begin + width] = score
                for part in range(0, width, 128):
                    piece = score[:, part : part + 128]
                    top = piece if top is None else jnp.maximum(top, piece)
        top = jnp.max(top, axis=1, keepdims=True)
        total = jnp.zeros((rows, 128), jnp.float32)
        for begin in range(0, 2 * keys, 128):
            expo = jnp.exp2(scores[:, begin : begin + 128] - top)
            total = total + expo
            weights[index, :, begin : begin + 128] = expo.astype(jnp.bfloat16)
        total = jnp.sum(total, axis=1, keepdims=True)
        denom[index] = jnp.broadcast_to(total, (rows, 128))
        return carry

    lax.fori_loop(0, q.shape[0], query_block, 0)


def score(place, q, k_own, k_other):
    blocks, rows, _ = q.shape
    keys = k_own.shape[0]
    vmem = pl.BlockSpec(memory_space=pltpu.VMEM)
    return pl.pallas_call(
        score_kernel,
        in_specs=[pl.BlockSpec(memory_space=pltpu.SMEM), vmem, vmem, vmem],
        out_specs=[vmem, vmem],
        out_shape=[
            jax.ShapeDtypeStruct((blocks, rows, 2 * keys), jnp.bfloat16),
            jax.ShapeDtypeStruct((blocks, rows, 128), jnp.float32),
        ],
        scratch_shapes=[pltpu.VMEM((rows, 2 * keys), jnp.float32)],
        compiler_params=pltpu.CompilerParams(vmem_limit_bytes=32 << 20),
        cost_estimate=pl.CostEstimate(
            flops=2 * blocks * rows * 2 * keys * HD,
            bytes_accessed=8_000_000,
            transcendentals=blocks * rows * 2 * keys,
        ),
        name="score",
    )(place, q, k_own, k_other)


def attend_kernel(weights, denom, v_own, v_other, inv_own, inv_other, gain, out, values):
    blocks, rows, _ = out.shape
    keys = v_own.shape[0] * rows
    for half, (v, inv) in enumerate(((v_own, inv_own), (v_other, inv_other))):
        for block in range(v.shape[0]):
            scaled = v[block].astype(jnp.float32) * inv[:, block : block + 1] * gain[...]
            begin = half * keys + block * rows
            values[begin : begin + rows, :] = scaled.astype(jnp.bfloat16)

    def query_block(index, carry):
        total = jnp.dot(weights[index], values[...], preferred_element_type=jnp.float32)
        out[index] = (total / denom[index]).astype(jnp.bfloat16)
        return carry

    lax.fori_loop(0, blocks, query_block, 0)


def attend(weights, denom, v_own, v_other, inv_own, inv_other, gain):
    blocks, rows, keys = weights.shape
    vmem = pl.BlockSpec(memory_space=pltpu.VMEM)
    return pl.pallas_call(
        attend_kernel,
        in_specs=[vmem] * 7,
        out_specs=vmem,
        out_shape=jax.ShapeDtypeStruct((blocks, rows, HD), jnp.bfloat16),
        scratch_shapes=[pltpu.VMEM((keys, HD), jnp.bfloat16)],
        compiler_params=pltpu.CompilerParams(vmem_limit_bytes=32 << 20),
        cost_estimate=pl.CostEstimate(
            flops=2 * blocks * rows * keys * HD, bytes_accessed=7_000_000, transcendentals=0
        ),
        name="attend",
    )(weights, denom, v_own, v_other, inv_own, inv_other, gain)


def exchange(value, axes):
    return lax.all_to_all(value, axes, 0, 0, tiled=True)


def swap_cores(value):
    return lax.ppermute(value, "c", [(0, 1), (1, 0)])


def shards(residual, gate_first, gate_second, hyena_value, short_taps, long_taps, norm_gain, queries, attn_keys):
    rows, chans = residual.shape
    heads = chans // HD
    count = 32
    width = chans * 16

    halo = lax.ppermute(
        jnp.concatenate([gate_first, hyena_value, gate_second[rows - 8 :]], axis=0),
        ROWS_AXES,
        [(source, source + 1) for source in range(count - 1)],
    )
    keys_by_head = attn_keys.reshape(rows, heads, HD).transpose(1, 0, 2)
    keys_own = exchange(jnp.concatenate([keys_by_head] * 4, axis=0), PEERS)
    queries_own = exchange(queries.reshape(rows, heads, HD).transpose(1, 0, 2), "h")

    stream, packed, squares = front(gate_first, gate_second, hyena_value, residual, halo, short_taps, long_taps)
    values_own = exchange(packed.reshape(16, rows, HD), PEERS)
    totals = jnp.sum(exchange(squares, CHAN_AXES), axis=0)
    inverse = 1.0 / jnp.sqrt(totals / width + 1e-06)
    inverse_own = exchange(jnp.broadcast_to(inverse, (16, rows)), PEERS)

    keys_other = swap_cores(keys_own)
    values_other = swap_cores(values_own)
    inverse_other = swap_cores(inverse_own)

    core = lax.axis_index("c")
    block = lax.axis_index("zh") * 16 + lax.axis_index("s") * 8 + core
    place = jnp.stack([block * rows, core * rows, (1 - core) * rows]).astype(jnp.int32)
    weights, denom = score(
        place, queries_own, keys_own.reshape(16 * rows, HD), keys_other.reshape(16 * rows, HD)
    )
    gain = lax.dynamic_slice_in_dim(norm_gain, lax.axis_index("h") * HD, HD, 0).reshape(1, HD)
    result = attend(weights, denom, values_own, values_other, inverse_own.T, inverse_other.T, gain)
    attended = exchange(result, "h").transpose(1, 0, 2).reshape(rows, chans)
    return stream, attended


def solution(mesh):
    inner = Mesh(mesh.devices.reshape(2, 2, 4, 2, 4, 4), ROWS_AXES + CHAN_AXES)
    both = P(ROWS_AXES, CHAN_AXES)
    return jax.shard_map(
        shards,
        mesh=inner,
        in_specs=(both, both, both, both, P(None, None, CHAN_AXES), P(None, CHAN_AXES), P(CHAN_AXES), both, both),
        out_specs=(both, both),
        check_vma=False,
    )
```

```python
import functools
import math

import jax
import jax.numpy as jnp
from jax import lax
from jax.experimental import pallas as pl
from jax.experimental.pallas import tpu as pltpu
from jax.sharding import Mesh, PartitionSpec as P

HD = 128
ROWS_AXES = ("zh", "s", "h", "c")
CHAN_AXES = ("x", "zl")
PEERS = ("zh", "s", "h")
HIGHEST = lax.Precision.HIGHEST


def shift_copies(prod, copies):
    length = prod.shape[0]
    for lag in range(8):
        copies[lag, 8:length, :] = prod[8 - lag : length - lag, :]


def lag_sums(weights, copies, base, pairs):
    totals = {}
    for group in range(weights.shape[0] // 8):
        wanted = [tile for tile, other in pairs if other == group]
        rows = weights[group * 8 : group * 8 + 8, :].astype(jnp.float32)
        for lag in range(8):
            weight = jnp.broadcast_to(rows[lag : lag + 1, :], rows.shape)
            for tile in wanted:
                begin = base + 8 * (tile - group)
                term = weight * copies[lag, begin : begin + 8, :]
                totals[tile] = totals[tile] + term if tile in totals else term
    return [totals[tile] for tile in sorted(totals)]


def featurize(taps, index, ext, begin, count):
    total = taps[index, 0:1, :] * ext[begin : begin + count, :]
    total = total + taps[index, 1:2, :] * ext[begin - 1 : begin - 1 + count, :]
    return total + taps[index, 2:3, :] * ext[begin - 2 : begin - 2 + count, :]


def head_lanes(head):
    return pl.ds(pl.multiple_of(head * HD, HD), HD)


def early_kernel(
    packed, gs, res, taps_in, long_in, keys, partial, feat, res_out, edge, taps_out, long_out, keys_out,
    gs_v, ext, prod, copies, sems,
):
    rows, chans = gs.shape
    loads = [(taps_in, taps_out), (long_in, long_out), (gs, gs_v), (res, res_out)]
    moves = [pltpu.make_async_copy(src, dst, sems.at[i]) for i, (src, dst) in enumerate(loads)]
    for copy in range(keys_out.shape[0]):
        for head in range(keys_out.shape[1]):
            src = keys.at[:, head * HD : (head + 1) * HD]
            moves.append(pltpu.make_async_copy(src, keys_out.at[copy, head], sems.at[len(moves)]))
    for move in moves:
        move.start()
    for move in moves[:4]:
        move.wait()
    tiles = rows // 8
    pairs = [(tile, group) for group in range(long_in.shape[0] // 8) for tile in range(group, tiles)]
    top = lax.broadcasted_iota(jnp.int32, (rows, HD), 0) < 2
    ext[0:8, :] = jnp.zeros((8, HD), jnp.float32)
    prod[0:8, :] = jnp.zeros((8, HD), jnp.float32)

    def one_head(head, carry):
        lanes = head_lanes(head)
        taps = taps_out[:, :, lanes]

        def feature(index, raw):
            wide = raw.astype(jnp.float32)
            ext[8:, :] = wide
            edge[index, :, lanes] = wide[0:8, :]
            return featurize(taps, index, ext, 8, rows)

        first = feature(0, packed[0:rows, lanes])
        product = (first * feature(2, packed[rows : 2 * rows, lanes])).astype(jnp.bfloat16).astype(jnp.float32)
        feat[:, lanes] = feature(1, gs_v[:, lanes])
        prod[8:, :] = jnp.where(top, 0.0, product)
        shift_copies(prod, copies)
        totals = lag_sums(long_out[:, lanes], copies, 8, pairs)
        partial[:, lanes] = jnp.concatenate(totals, axis=0)
        return carry

    lax.fori_loop(0, chans // HD, one_head, 0)
    for move in moves[4:]:
        move.wait()


def in_hbm(*arrays):
    return [pltpu.with_memory_space_constraint(array, pltpu.HBM) for array in arrays]


def early(packed, gs, res, taps, long_taps, keys):
    rows, chans = gs.shape
    heads = chans // HD
    hbm = pl.BlockSpec(memory_space=pltpu.HBM)
    vmem = pl.BlockSpec(memory_space=pltpu.VMEM)
    return pl.pallas_call(
        early_kernel,
        in_specs=[vmem] + [hbm] * 5,
        out_specs=[vmem] * 7,
        out_shape=[
            jax.ShapeDtypeStruct((rows, chans), jnp.float32),
            jax.ShapeDtypeStruct((rows, chans), jnp.float32),
            jax.ShapeDtypeStruct((rows, chans), jnp.bfloat16),
            jax.ShapeDtypeStruct((3, 8, chans), jnp.float32),
            jax.ShapeDtypeStruct(taps.shape, jnp.float32),
            jax.ShapeDtypeStruct(long_taps.shape, jnp.bfloat16),
            jax.ShapeDtypeStruct((2, heads, rows, HD), jnp.bfloat16),
        ],
        scratch_shapes=[
            pltpu.VMEM((rows, chans), jnp.bfloat16),
            pltpu.VMEM((rows + 8, HD), jnp.float32),
            pltpu.VMEM((rows + 8, HD), jnp.float32),
            pltpu.VMEM((8, rows + 8, HD), jnp.float32),
            pltpu.SemaphoreType.DMA((4 + 2 * heads,)),
        ],
        compiler_params=pltpu.CompilerParams(vmem_limit_bytes=32 << 20),
        cost_estimate=pl.CostEstimate(flops=6_000_000_000, bytes_accessed=2_000_000, transcendentals=0),
        name="early",
    )(packed, *in_hbm(gs, res, taps, long_taps, keys))


def late_kernel(halo, partial, feat, res, edge, taps_in, long_in, stream, squares, ext, prod, copies):
    rows, chans = res.shape
    tiles = rows // 8
    pairs = [(tile, group) for group in range(long_in.shape[0] // 8) for tile in range(min(group + 2, tiles))]
    inside = lax.broadcasted_iota(jnp.int32, (rows, HD), 0) < rows - 6
    first_row = (lax.broadcasted_iota(jnp.int32, (8, HD), 0) == 0).astype(jnp.float32)
    prod[0:8, :] = jnp.zeros((8, HD), jnp.float32)
    prod[rows + 8 :, :] = jnp.zeros((8, HD), jnp.float32)
    squares[...] = jnp.zeros_like(squares)

    def one_head(head, carry):
        lanes = head_lanes(head)
        taps = taps_in[:, :, lanes]

        def feature(index, begin):
            ext[0:rows, :] = halo[begin : begin + rows, lanes].astype(jnp.float32)
            ext[rows : rows + 8, :] = edge[index, :, lanes]
            return featurize(taps, index, ext, 8, rows)

        first = feature(0, 0)
        product = (first * feature(2, rows)).astype(jnp.bfloat16).astype(jnp.float32)
        prod[8 : rows + 8, :] = jnp.where(inside, product, 0.0)
        shift_copies(prod, copies)
        totals = lag_sums(long_in[:, lanes], copies, rows, pairs)
        filtered = partial[:, lanes] + jnp.concatenate(totals, axis=0)
        ext[0:8, :] = halo[2 * rows : 2 * rows + 8, lanes].astype(jnp.float32)
        ext[8:16, :] = edge[1, :, lanes]
        gate = jnp.concatenate([featurize(taps, 1, ext, 8, 8), feat[8:, lanes]], axis=0)
        out = (res[:, lanes].astype(jnp.float32) + gate * filtered).astype(jnp.bfloat16)
        stream[:, lanes] = out
        wide = out.astype(jnp.float32)
        squares[...] += lax.dot_general(
            first_row,
            wide * wide,
            (((1,), (1,)), ((), ())),
            precision=HIGHEST,
            preferred_element_type=jnp.float32,
        )
        return carry

    lax.fori_loop(0, chans // HD, one_head, 0)


def late(halo, partial, feat, res, edge, taps, long_taps):
    rows, chans = res.shape
    vmem = pl.BlockSpec(memory_space=pltpu.VMEM)
    return pl.pallas_call(
        late_kernel,
        in_specs=[vmem] * 7,
        out_specs=[vmem] * 2,
        out_shape=[
            jax.ShapeDtypeStruct((rows, chans), jnp.bfloat16),
            jax.ShapeDtypeStruct((8, rows), jnp.float32),
        ],
        scratch_shapes=[
            pltpu.VMEM((rows + 8, HD), jnp.float32),
            pltpu.VMEM((rows + 16, HD), jnp.float32),
            pltpu.VMEM((8, rows + 16, HD), jnp.float32),
        ],
        compiler_params=pltpu.CompilerParams(vmem_limit_bytes=32 << 20),
        cost_estimate=pl.CostEstimate(flops=30_000_000_000, bytes_accessed=2_000_000, transcendentals=0),
        name="late",
    )(halo, partial, feat, res, edge, taps, long_taps)


def pack_kernel(gf, hv, gs, out, sems):
    rows = gf.shape[0]
    moves = [
        pltpu.make_async_copy(gf, out.at[0:rows], sems.at[0]),
        pltpu.make_async_copy(hv, out.at[rows : 2 * rows], sems.at[1]),
        pltpu.make_async_copy(gs.at[rows - 8 : rows], out.at[2 * rows : 2 * rows + 8], sems.at[2]),
    ]
    for move in moves:
        move.start()
    for move in moves:
        move.wait()


def pack(gf, hv, gs):
    rows, chans = gf.shape
    return pl.pallas_call(
        pack_kernel,
        in_specs=[pl.BlockSpec(memory_space=pltpu.HBM)] * 3,
        out_specs=pl.BlockSpec(memory_space=pltpu.VMEM),
        out_shape=jax.ShapeDtypeStruct((2 * rows + 8, chans), jnp.bfloat16),
        scratch_shapes=[pltpu.SemaphoreType.DMA((3,))],
        compiler_params=pltpu.CompilerParams(vmem_limit_bytes=16 << 20),
        cost_estimate=pl.CostEstimate(flops=0, bytes_accessed=600_000, transcendentals=0),
        name="pack",
    )(*in_hbm(gf, hv, gs))


def normalize_kernel(width, gathered, stream, gain, packed):
    parts = gathered.shape[0]
    total = lax.dot_general(
        gathered[...],
        jnp.ones((parts, HD), jnp.float32),
        (((0,), (0,)), ((), ())),
        precision=HIGHEST,
        preferred_element_type=jnp.float32,
    )
    inverse = 1.0 / jnp.sqrt(total / width + 1e-06)
    for head in range(packed.shape[1]):
        lanes = slice(head * HD, (head + 1) * HD)
        value = stream[:, lanes].astype(jnp.float32) * inverse * gain[:, lanes]
        value = value.astype(jnp.bfloat16)
        for copy in range(packed.shape[0]):
            packed[copy, head] = value


def normalize(width, gathered, stream, gain):
    rows, chans = stream.shape
    vmem = pl.BlockSpec(memory_space=pltpu.VMEM)
    return pl.pallas_call(
        functools.partial(normalize_kernel, width),
        in_specs=[vmem] * 3,
        out_specs=vmem,
        out_shape=jax.ShapeDtypeStruct((4, chans // HD, rows, HD), jnp.bfloat16),
        cost_estimate=pl.CostEstimate(flops=1_000_000, bytes_accessed=800_000, transcendentals=20_000),
        name="normalize",
    )(gathered, stream, gain)


def score_kernel(place, q0, q1, q2, q3, k0, k1, k2, k3, out, denom, scores, weights, sems):
    rows = q0.shape[0]
    keys = k0.shape[0]
    unit = math.log2(math.e) / math.sqrt(HD)
    chunks = [(begin, min(256, keys - begin)) for begin in range(0, keys, 256)]
    for index, query_ref in enumerate((q0, q1, q2, q3)):
        query = query_ref[...]
        query_pos = place[4 + index] + lax.broadcasted_iota(jnp.int32, (rows, 1), 0)
        top = None
        for part, ref in enumerate((k0, k1, k2, k3)):
            for begin, width in chunks:
                score = lax.dot_general(
                    query,
                    ref[begin : begin + width, :],
                    (((1,), (1,)), ((), ())),
                    preferred_element_type=jnp.float32,
                )
                lane = begin + lax.broadcasted_iota(jnp.int32, (1, width), 1)
                key_pos = place[part] + lane
                for edge in range(rows, keys, rows):
                    if edge < begin + width:
                        key_pos = key_pos + jnp.where(lane >= edge, rows, 0)
                score = jnp.where(key_pos <= query_pos, score * unit, -1e30)
                scores[:, part * keys + begin : part * keys + begin + width] = score
                for piece in range(0, width, 128):
                    piece = score[:, piece : min(piece + 128, width)]
                    if piece.shape[1] < 128:
                        piece = jnp.concatenate(
                            [piece, jnp.full((rows, 128 - piece.shape[1]), -1e30, jnp.float32)], axis=1
                        )
                    top = piece if top is None else jnp.maximum(top, piece)
        top = jnp.max(top, axis=1, keepdims=True)
        total = jnp.zeros((rows, 128), jnp.float32)
        for begin in range(0, 4 * keys, 128):
            expo = jnp.exp2(scores[:, begin : begin + 128] - top)
            total = total + expo
            weights[index, :, begin : begin + 128] = expo.astype(jnp.bfloat16)
        total = jnp.sum(total, axis=1, keepdims=True)
        denom[index] = jnp.broadcast_to(total, (rows, 128))
        pltpu.make_async_copy(weights.at[index], out.at[index], sems.at[index]).start()
    for index in range(4):
        pltpu.make_async_copy(weights.at[index], out.at[index], sems.at[index]).wait()


def score(place, queries, keys):
    rows = queries[0].shape[0]
    blocks = len(queries)
    count = sum(part.shape[0] for part in keys)
    vmem = pl.BlockSpec(memory_space=pltpu.VMEM)
    return pl.pallas_call(
        score_kernel,
        in_specs=[pl.BlockSpec(memory_space=pltpu.SMEM)] + [vmem] * 8,
        out_specs=[pl.BlockSpec(memory_space=pltpu.HBM), vmem],
        out_shape=[
            pltpu.HBM((blocks, rows, count), jnp.bfloat16),
            jax.ShapeDtypeStruct((blocks, rows, 128), jnp.float32),
        ],
        scratch_shapes=[
            pltpu.VMEM((rows, count), jnp.float32),
            pltpu.VMEM((blocks, rows, count), jnp.bfloat16),
            pltpu.SemaphoreType.DMA((blocks,)),
        ],
        compiler_params=pltpu.CompilerParams(vmem_limit_bytes=32 << 20),
        cost_estimate=pl.CostEstimate(
            flops=2 * blocks * rows * count * HD,
            bytes_accessed=8_000_000,
            transcendentals=blocks * rows * count,
        ),
        name="score",
    )(place, *queries, *keys)


def attend_kernel(place, weights_in, denom, v_own, v_other, out, weights, sems):
    blocks, rows, _ = out.shape
    half = v_own.shape[0] // 2
    moves = [
        pltpu.make_async_copy(weights_in.at[index], weights.at[index], sems.at[index]) for index in range(blocks)
    ]
    for move in moves:
        move.start()
    for index, move in enumerate(moves):
        move.wait()
        total = jnp.zeros((rows, HD), jnp.float32)
        for part in range(4):
            begin = pl.multiple_of(place[12 + part // 2] * half, 16)
            ref = v_other if part % 2 else v_own
            total = total + jnp.dot(
                weights[index, :, part * half : (part + 1) * half],
                ref[pl.ds(begin, half), :],
                preferred_element_type=jnp.float32,
            )
        out[place[8 + index]] = (total / denom[index]).astype(jnp.bfloat16)


def attend(place, weights, denom, v_own, v_other):
    blocks, rows, keys = weights.shape
    vmem = pl.BlockSpec(memory_space=pltpu.VMEM)
    return pl.pallas_call(
        attend_kernel,
        in_specs=[pl.BlockSpec(memory_space=pltpu.SMEM), pl.BlockSpec(memory_space=pltpu.HBM), vmem, vmem, vmem],
        out_specs=vmem,
        out_shape=jax.ShapeDtypeStruct((blocks, rows, HD), jnp.bfloat16),
        scratch_shapes=[pltpu.VMEM((blocks, rows, keys), jnp.bfloat16), pltpu.SemaphoreType.DMA((blocks,))],
        compiler_params=pltpu.CompilerParams(vmem_limit_bytes=16 << 20),
        cost_estimate=pl.CostEstimate(
            flops=2 * blocks * rows * keys * HD, bytes_accessed=7_000_000, transcendentals=0
        ),
        name="attend",
    )(place, *in_hbm(weights), denom, v_own, v_other)


def exchange(value, axes):
    return lax.all_to_all(value, axes, 0, 0, tiled=True)


def swap_cores(value):
    return lax.ppermute(value, "c", [(0, 1), (1, 0)])


def shards(residual, gate_first, gate_second, hyena_value, short_taps, long_taps, norm_gain, queries, attn_keys):
    rows, chans = residual.shape
    heads = chans // HD
    count = 32
    width = chans * 16

    core = lax.axis_index("c")
    head = lax.axis_index("h")
    side = lax.axis_index("zh")
    group = side * 16 + lax.axis_index("s") * 8 + core
    owners = [head ^ flip for flip in range(heads)]
    place = [side * 16 + core, side * 16 + 1 - core, (1 - side) * 16 + core, (1 - side) * 16 + 1 - core]
    place = place + [group + owner * 2 for owner in owners]
    place = jnp.concatenate([jnp.stack(place) * rows, jnp.stack(owners + [side, 1 - side])]).astype(jnp.int32)

    last = pack(gate_first, hyena_value, gate_second)
    halo = lax.ppermute(
        last,
        ROWS_AXES,
        [(source, source + 1) for source in range(count - 1)],
    )
    *early_parts, keys_by_head = early(
        last, gate_second, residual, short_taps, long_taps, attn_keys
    )
    keys_near = exchange(keys_by_head.reshape(8, rows, HD), ("s", "h"))

    stream, squares = late(halo, *early_parts)
    gathered = lax.all_gather(squares, CHAN_AXES, axis=0, tiled=True)
    packed = normalize(width, gathered, stream, norm_gain.reshape(1, chans))
    keys_near, packed = lax.optimization_barrier((keys_near, packed))
    values_own = exchange(packed.reshape(16, rows, HD), PEERS)

    keys_far = lax.ppermute(keys_near, "zh", [(0, 1)])
    parts = [keys_near, swap_cores(keys_near), keys_far, swap_cores(keys_far)]
    blocks = []
    for flip, owner in enumerate(owners):
        block = lax.dynamic_slice_in_dim(queries, owner * HD, HD, 1)
        if flip:
            block = lax.ppermute(block, "h", [(source, source ^ flip) for source in range(heads)])
        blocks.append(block)
    weights, denom = score(place, blocks, [part.reshape(8 * rows, HD) for part in parts])
    values_own, denom = lax.optimization_barrier((values_own, denom))
    values_other = swap_cores(values_own)
    result = attend(
        place, weights, denom, values_own.reshape(16 * rows, HD), values_other.reshape(16 * rows, HD)
    )
    attended = exchange(result, "h").transpose(1, 0, 2).reshape(rows, chans)
    return stream, attended


def solution(mesh):
    inner = Mesh(mesh.devices.reshape(2, 2, 4, 2, 4, 4), ROWS_AXES + CHAN_AXES)
    both = P(ROWS_AXES, CHAN_AXES)
    return jax.shard_map(
        shards,
        mesh=inner,
        in_specs=(both, both, both, both, P(None, None, CHAN_AXES), P(None, CHAN_AXES), P(CHAN_AXES), both, both),
        out_specs=(both, both),
        check_vma=False,
    )
```

```python
import functools
import math

import jax
import jax.numpy as jnp
from jax import lax
from jax.experimental import pallas as pl
from jax.experimental.pallas import tpu as pltpu
from jax.sharding import Mesh, PartitionSpec as P

HD = 128
ROWS_AXES = ("zh", "s", "h", "c")
CHAN_AXES = ("x", "zl")
PEERS = ("zh", "s", "h")
HIGHEST = lax.Precision.HIGHEST


def shift_copies(prod, copies):
    length = prod.shape[0]
    for lag in range(8):
        copies[lag, 8:length, :] = prod[8 - lag : length - lag, :]


def lag_sums(weights, copies, base, pairs):
    totals = {}
    for group in range(weights.shape[0] // 8):
        wanted = [tile for tile, other in pairs if other == group]
        rows = weights[group * 8 : group * 8 + 8, :].astype(jnp.float32)
        for lag in range(8):
            weight = jnp.broadcast_to(rows[lag : lag + 1, :], rows.shape)
            for tile in wanted:
                begin = base + 8 * (tile - group)
                term = weight * copies[lag, begin : begin + 8, :]
                totals[tile] = totals[tile] + term if tile in totals else term
    return [totals[tile] for tile in sorted(totals)]


def featurize(taps, index, ext, begin, count):
    total = taps[index, 0:1, :] * ext[begin : begin + count, :]
    total = total + taps[index, 1:2, :] * ext[begin - 1 : begin - 1 + count, :]
    return total + taps[index, 2:3, :] * ext[begin - 2 : begin - 2 + count, :]


def head_lanes(head):
    return pl.ds(pl.multiple_of(head * HD, HD), HD)


def early_kernel(
    packed, gs, res, taps_in, long_in, partial, feat, res_out, edge, taps_out, long_out,
    gs_v, ext, prod, copies, sems,
):
    rows, chans = gs.shape
    loads = [(taps_in, taps_out), (long_in, long_out), (gs, gs_v), (res, res_out)]
    moves = [pltpu.make_async_copy(src, dst, sems.at[i]) for i, (src, dst) in enumerate(loads)]
    for move in moves:
        move.start()
    for move in moves:
        move.wait()
    tiles = rows // 8
    pairs = [(tile, group) for group in range(long_in.shape[0] // 8) for tile in range(group, tiles)]
    top = lax.broadcasted_iota(jnp.int32, (rows, HD), 0) < 2
    ext[0:8, :] = jnp.zeros((8, HD), jnp.float32)
    prod[0:8, :] = jnp.zeros((8, HD), jnp.float32)

    def one_head(head, carry):
        lanes = head_lanes(head)
        taps = taps_out[:, :, lanes]

        def feature(index, raw):
            wide = raw.astype(jnp.float32)
            ext[8:, :] = wide
            edge[index, :, lanes] = wide[0:8, :]
            return featurize(taps, index, ext, 8, rows)

        first = feature(0, packed[0:rows, lanes])
        product = (first * feature(2, packed[rows : 2 * rows, lanes])).astype(jnp.bfloat16).astype(jnp.float32)
        feat[:, lanes] = feature(1, gs_v[:, lanes])
        prod[8:, :] = jnp.where(top, 0.0, product)
        shift_copies(prod, copies)
        totals = lag_sums(long_out[:, lanes], copies, 8, pairs)
        partial[:, lanes] = jnp.concatenate(totals, axis=0)
        return carry

    lax.fori_loop(0, chans // HD, one_head, 0)


def in_hbm(*arrays):
    return [pltpu.with_memory_space_constraint(array, pltpu.HBM) for array in arrays]


def early(packed, gs, res, taps, long_taps):
    rows, chans = gs.shape
    hbm = pl.BlockSpec(memory_space=pltpu.HBM)
    vmem = pl.BlockSpec(memory_space=pltpu.VMEM)
    return pl.pallas_call(
        early_kernel,
        in_specs=[vmem] + [hbm] * 4,
        out_specs=[vmem] * 6,
        out_shape=[
            jax.ShapeDtypeStruct((rows, chans), jnp.float32),
            jax.ShapeDtypeStruct((rows, chans), jnp.float32),
            jax.ShapeDtypeStruct((rows, chans), jnp.bfloat16),
            jax.ShapeDtypeStruct((3, 8, chans), jnp.float32),
            jax.ShapeDtypeStruct(taps.shape, jnp.float32),
            jax.ShapeDtypeStruct(long_taps.shape, jnp.bfloat16),
        ],
        scratch_shapes=[
            pltpu.VMEM((rows, chans), jnp.bfloat16),
            pltpu.VMEM((rows + 8, HD), jnp.float32),
            pltpu.VMEM((rows + 8, HD), jnp.float32),
            pltpu.VMEM((8, rows + 8, HD), jnp.float32),
            pltpu.SemaphoreType.DMA((4,)),
        ],
        compiler_params=pltpu.CompilerParams(vmem_limit_bytes=32 << 20),
        cost_estimate=pl.CostEstimate(flops=6_000_000_000, bytes_accessed=2_000_000, transcendentals=0),
        name="early",
    )(packed, *in_hbm(gs, res, taps, long_taps))


def late_kernel(halo, partial, feat, res, edge, taps_in, long_in, stream, squares, ext, prod, copies):
    rows, chans = res.shape
    tiles = rows // 8
    pairs = [(tile, group) for group in range(long_in.shape[0] // 8) for tile in range(min(group + 2, tiles))]
    inside = lax.broadcasted_iota(jnp.int32, (rows, HD), 0) < rows - 6
    prod[0:8, :] = jnp.zeros((8, HD), jnp.float32)
    prod[rows + 8 :, :] = jnp.zeros((8, HD), jnp.float32)
    total = jnp.zeros((8, rows), jnp.float32)

    def one_head(head, total):
        lanes = head_lanes(head)
        taps = taps_in[:, :, lanes]

        def feature(index, begin):
            ext[0:rows, :] = halo[begin : begin + rows, lanes].astype(jnp.float32)
            ext[rows : rows + 8, :] = edge[index, :, lanes]
            return featurize(taps, index, ext, 8, rows)

        first = feature(0, 0)
        product = (first * feature(2, rows)).astype(jnp.bfloat16).astype(jnp.float32)
        prod[8 : rows + 8, :] = jnp.where(inside, product, 0.0)
        shift_copies(prod, copies)
        totals = lag_sums(long_in[:, lanes], copies, rows, pairs)
        filtered = partial[:, lanes] + jnp.concatenate(totals, axis=0)
        ext[0:8, :] = halo[2 * rows : 2 * rows + 8, lanes].astype(jnp.float32)
        ext[8:16, :] = edge[1, :, lanes]
        gate = jnp.concatenate([featurize(taps, 1, ext, 8, 8), feat[8:, lanes]], axis=0)
        out = (res[:, lanes].astype(jnp.float32) + gate * filtered).astype(jnp.bfloat16)
        stream[:, lanes] = out
        wide = out.astype(jnp.float32)
        total = total + lax.dot_general(
            jnp.ones((8, HD), jnp.float32),
            wide * wide,
            (((1,), (1,)), ((), ())),
            precision=HIGHEST,
            preferred_element_type=jnp.float32,
        )
        return total

    total = lax.fori_loop(0, chans // HD, one_head, total)
    for peer in range(squares.shape[0]):
        squares[peer] = total[0:1, :]


def late(halo, partial, feat, res, edge, taps, long_taps):
    rows, chans = res.shape
    vmem = pl.BlockSpec(memory_space=pltpu.VMEM)
    return pl.pallas_call(
        late_kernel,
        in_specs=[vmem] * 7,
        out_specs=[vmem] * 2,
        out_shape=[
            jax.ShapeDtypeStruct((rows, chans), jnp.bfloat16),
            jax.ShapeDtypeStruct((16, 1, rows), jnp.float32),
        ],
        scratch_shapes=[
            pltpu.VMEM((rows + 8, HD), jnp.float32),
            pltpu.VMEM((rows + 16, HD), jnp.float32),
            pltpu.VMEM((8, rows + 16, HD), jnp.float32),
        ],
        compiler_params=pltpu.CompilerParams(vmem_limit_bytes=32 << 20),
        cost_estimate=pl.CostEstimate(flops=30_000_000_000, bytes_accessed=2_000_000, transcendentals=0),
        name="late",
    )(halo, partial, feat, res, edge, taps, long_taps)


def pack_kernel(gf, hv, gs, keys, queries, halo, keys_out, queries_out, sems):
    rows = gf.shape[0]
    pairs = []
    for copy in range(keys_out.shape[0]):
        for head in range(keys_out.shape[1]):
            pairs.append((keys.at[:, head * HD : (head + 1) * HD], keys_out.at[copy, head]))
    pairs += [
        (gf, halo.at[0:rows]),
        (hv, halo.at[rows : 2 * rows]),
        (gs.at[rows - 8 : rows], halo.at[2 * rows : 2 * rows + 8]),
        (queries, queries_out.at[0:rows]),
        (queries, queries_out.at[rows : 2 * rows]),
    ]
    moves = [pltpu.make_async_copy(src, dst, sems.at[i]) for i, (src, dst) in enumerate(pairs)]
    for move in moves:
        move.start()
    for move in moves:
        move.wait()


def pack(gf, hv, gs, keys, queries):
    rows, chans = gf.shape
    heads = chans // HD
    vmem = pl.BlockSpec(memory_space=pltpu.VMEM)
    hbm = pl.BlockSpec(memory_space=pltpu.HBM)
    return pl.pallas_call(
        pack_kernel,
        in_specs=[hbm] * 5,
        out_specs=[vmem, vmem, hbm],
        out_shape=[
            jax.ShapeDtypeStruct((2 * rows + 8, chans), jnp.bfloat16),
            jax.ShapeDtypeStruct((2, heads, rows, HD), jnp.bfloat16),
            pltpu.HBM((2 * rows, chans), jnp.bfloat16),
        ],
        scratch_shapes=[pltpu.SemaphoreType.DMA((2 * heads + 5,))],
        compiler_params=pltpu.CompilerParams(vmem_limit_bytes=16 << 20),
        cost_estimate=pl.CostEstimate(flops=0, bytes_accessed=600_000, transcendentals=0),
        name="pack",
    )(*in_hbm(gf, hv, gs, keys, queries))


def normalize_kernel(width, gathered, stream, gain, packed):
    total = gathered[0]
    for peer in range(1, gathered.shape[0]):
        total = total + gathered[peer]
    total = jnp.broadcast_to(total, (8, total.shape[1]))
    total = lax.dot_general(
        jnp.where(lax.broadcasted_iota(jnp.int32, total.shape, 0) == 0, total, 0.0),
        jnp.ones((8, HD), jnp.float32),
        (((0,), (0,)), ((), ())),
        precision=HIGHEST,
        preferred_element_type=jnp.float32,
    )
    inverse = 1.0 / jnp.sqrt(total / width + 1e-06)
    for head in range(packed.shape[1]):
        lanes = slice(head * HD, (head + 1) * HD)
        value = stream[:, lanes].astype(jnp.float32) * inverse * gain[:, lanes]
        value = value.astype(jnp.bfloat16)
        for copy in range(packed.shape[0]):
            packed[copy, head] = value


def normalize(width, gathered, stream, gain):
    rows, chans = stream.shape
    vmem = pl.BlockSpec(memory_space=pltpu.VMEM)
    return pl.pallas_call(
        functools.partial(normalize_kernel, width),
        in_specs=[vmem] * 3,
        out_specs=vmem,
        out_shape=jax.ShapeDtypeStruct((4, chans // HD, rows, HD), jnp.bfloat16),
        cost_estimate=pl.CostEstimate(flops=1_000_000, bytes_accessed=800_000, transcendentals=20_000),
        name="normalize",
    )(gathered, stream, gain)


def score_kernel(place, gathered, k0, k1, k2, k3, out, denom, scores, weights, q, sems):
    rows = q.shape[1]
    keys = k0.shape[0]
    unit = math.log2(math.e) / math.sqrt(HD)
    chunks = [(begin, min(256, keys - begin)) for begin in range(0, keys, 256)]
    blocks = q.shape[0]
    begin = pl.multiple_of(place[8] * HD, HD)
    moves = []
    for index in range(blocks):
        src = gathered.at[index * 2 * rows : index * 2 * rows + rows, pl.ds(begin, HD)]
        moves.append(pltpu.make_async_copy(src, q.at[index], sems.at[index]))
    for move in moves:
        move.start()
    for move in moves:
        move.wait()
    for index in range(blocks):
        query = q[index]
        query_pos = place[4 + index] + lax.broadcasted_iota(jnp.int32, (rows, 1), 0)
        top = None
        for part, ref in enumerate((k0, k1, k2, k3)):
            for begin, width in chunks:
                score = lax.dot_general(
                    query,
                    ref[begin : begin + width, :],
                    (((1,), (1,)), ((), ())),
                    preferred_element_type=jnp.float32,
                )
                lane = begin + lax.broadcasted_iota(jnp.int32, (1, width), 1)
                key_pos = place[part] + lane
                for edge in range(rows, keys, rows):
                    if edge < begin + width:
                        key_pos = key_pos + jnp.where(lane >= edge, rows, 0)
                score = jnp.where(key_pos <= query_pos, score * unit, -1e30)
                scores[:, part * keys + begin : part * keys + begin + width] = score
                for piece in range(0, width, 128):
                    piece = score[:, piece : min(piece + 128, width)]
                    if piece.shape[1] < 128:
                        piece = jnp.concatenate(
                            [piece, jnp.full((rows, 128 - piece.shape[1]), -1e30, jnp.float32)], axis=1
                        )
                    top = piece if top is None else jnp.maximum(top, piece)
        top = jnp.max(top, axis=1, keepdims=True)
        total = jnp.zeros((rows, 128), jnp.float32)
        for begin in range(0, 4 * keys, 128):
            expo = jnp.exp2(scores[:, begin : begin + 128] - top)
            total = total + expo
            weights[index, :, begin : begin + 128] = expo.astype(jnp.bfloat16)
        total = jnp.sum(total, axis=1, keepdims=True)
        denom[index] = jnp.broadcast_to(total, (rows, 128))
        pltpu.make_async_copy(weights.at[index], out.at[index], sems.at[index]).start()
    for index in range(blocks):
        pltpu.make_async_copy(weights.at[index], out.at[index], sems.at[index]).wait()


def score(place, gathered, keys):
    rows = keys[0].shape[0] // 8
    blocks = gathered.shape[0] // (2 * rows)
    count = sum(part.shape[0] for part in keys)
    vmem = pl.BlockSpec(memory_space=pltpu.VMEM)
    return pl.pallas_call(
        score_kernel,
        in_specs=[pl.BlockSpec(memory_space=pltpu.SMEM), pl.BlockSpec(memory_space=pltpu.HBM)] + [vmem] * 4,
        out_specs=[pl.BlockSpec(memory_space=pltpu.HBM), vmem],
        out_shape=[
            pltpu.HBM((blocks, rows, count), jnp.bfloat16),
            jax.ShapeDtypeStruct((blocks, rows, 128), jnp.float32),
        ],
        scratch_shapes=[
            pltpu.VMEM((rows, count), jnp.float32),
            pltpu.VMEM((blocks, rows, count), jnp.bfloat16),
            pltpu.VMEM((blocks, rows, HD), jnp.bfloat16),
            pltpu.SemaphoreType.DMA((blocks,)),
        ],
        compiler_params=pltpu.CompilerParams(vmem_limit_bytes=32 << 20),
        cost_estimate=pl.CostEstimate(
            flops=2 * blocks * rows * count * HD,
            bytes_accessed=8_000_000,
            transcendentals=blocks * rows * count,
        ),
        name="score",
    )(place, *in_hbm(gathered), *keys)


def attend_kernel(place, weights_in, denom, v_own, v_other, out, weights, sems):
    blocks, rows, _ = out.shape
    half = v_own.shape[0] // 2
    moves = [
        pltpu.make_async_copy(weights_in.at[index], weights.at[index], sems.at[index]) for index in range(blocks)
    ]
    for move in moves:
        move.start()
    for index, move in enumerate(moves):
        move.wait()
        total = jnp.zeros((rows, HD), jnp.float32)
        for part in range(4):
            begin = pl.multiple_of(place[9 + part // 2] * half, 16)
            ref = v_other if part % 2 else v_own
            total = total + jnp.dot(
                weights[index, :, part * half : (part + 1) * half],
                ref[pl.ds(begin, half), :],
                preferred_element_type=jnp.float32,
            )
        out[index] = (total / denom[index]).astype(jnp.bfloat16)


def attend(place, weights, denom, v_own, v_other):
    blocks, rows, keys = weights.shape
    vmem = pl.BlockSpec(memory_space=pltpu.VMEM)
    return pl.pallas_call(
        attend_kernel,
        in_specs=[pl.BlockSpec(memory_space=pltpu.SMEM), pl.BlockSpec(memory_space=pltpu.HBM), vmem, vmem, vmem],
        out_specs=vmem,
        out_shape=jax.ShapeDtypeStruct((blocks, rows, HD), jnp.bfloat16),
        scratch_shapes=[pltpu.VMEM((blocks, rows, keys), jnp.bfloat16), pltpu.SemaphoreType.DMA((blocks,))],
        compiler_params=pltpu.CompilerParams(vmem_limit_bytes=16 << 20),
        cost_estimate=pl.CostEstimate(
            flops=2 * blocks * rows * keys * HD, bytes_accessed=7_000_000, transcendentals=0
        ),
        name="attend",
    )(place, *in_hbm(weights), denom, v_own, v_other)


def exchange(value, axes):
    return lax.all_to_all(value, axes, 0, 0, tiled=True)


def swap_cores(value):
    return lax.ppermute(value, "c", [(0, 1), (1, 0)])


def shards(residual, gate_first, gate_second, hyena_value, short_taps, long_taps, norm_gain, queries, attn_keys):
    rows, chans = residual.shape
    heads = chans // HD
    count = 32
    width = chans * 16

    core = lax.axis_index("c")
    head = lax.axis_index("h")
    side = lax.axis_index("zh")
    group = side * 16 + lax.axis_index("s") * 8 + core
    place = [side * 16 + core, side * 16 + 1 - core, (1 - side) * 16 + core, (1 - side) * 16 + 1 - core]
    place = place + [group + owner * 2 for owner in range(heads)]
    place = jnp.concatenate([jnp.stack(place) * rows, jnp.stack([head, side, 1 - side])]).astype(jnp.int32)

    last, keys_by_head, queries_twice = pack(gate_first, hyena_value, gate_second, attn_keys, queries)
    keys_near = exchange(keys_by_head.reshape(8, rows, HD), ("s", "h"))
    queries_all = lax.all_gather(queries_twice, "h", axis=0, tiled=True)
    halo = lax.ppermute(last, ROWS_AXES, [(source, source + 1) for source in range(count - 1)])
    early_parts = early(last, gate_second, residual, short_taps, long_taps)
    stream, squares = late(halo, *early_parts)
    keys_near, squares = lax.optimization_barrier((keys_near, squares))
    gathered = exchange(squares, CHAN_AXES)
    packed = normalize(width, gathered, stream, norm_gain.reshape(1, chans))
    values_own = exchange(packed.reshape(16, rows, HD), PEERS)

    keys_far = lax.ppermute(keys_near, "zh", [(0, 1)])
    parts = [keys_near, swap_cores(keys_near), keys_far, swap_cores(keys_far)]
    weights, denom = score(place, queries_all, [part.reshape(8 * rows, HD) for part in parts])
    values_own, denom = lax.optimization_barrier((values_own, denom))
    values_other = swap_cores(values_own)
    result = attend(
        place, weights, denom, values_own.reshape(16 * rows, HD), values_other.reshape(16 * rows, HD)
    )
    attended = exchange(result, "h").transpose(1, 0, 2).reshape(rows, chans)
    return stream, attended


def solution(mesh):
    inner = Mesh(mesh.devices.reshape(2, 2, 4, 2, 4, 4), ROWS_AXES + CHAN_AXES)
    both = P(ROWS_AXES, CHAN_AXES)
    return jax.shard_map(
        shards,
        mesh=inner,
        in_specs=(both, both, both, both, P(None, None, CHAN_AXES), P(None, CHAN_AXES), P(CHAN_AXES), both, both),
        out_specs=(both, both),
        check_vma=False,
    )
```

```python
import functools
import math

import jax
import jax.numpy as jnp
from jax import lax
from jax.experimental import pallas as pl
from jax.experimental.pallas import tpu as pltpu
from jax.sharding import Mesh, PartitionSpec as P

HD = 128
ROWS_AXES = ("zh", "s", "h", "c")
CHAN_AXES = ("x", "zl")
PEERS = ("zh", "s", "h")
HIGHEST = lax.Precision.HIGHEST


def shift_copies(prod, copies):
    length = prod.shape[0]
    for lag in range(8):
        copies[lag, 8:length, :] = prod[8 - lag : length - lag, :]


def lag_sums(weights, copies, base, pairs):
    totals = {}
    for group in range(weights.shape[0] // 8):
        wanted = [tile for tile, other in pairs if other == group]
        rows = weights[group * 8 : group * 8 + 8, :].astype(jnp.float32)
        for lag in range(8):
            weight = jnp.broadcast_to(rows[lag : lag + 1, :], rows.shape)
            for tile in wanted:
                begin = base + 8 * (tile - group)
                term = weight * copies[lag, begin : begin + 8, :]
                totals[tile] = totals[tile] + term if tile in totals else term
    return [totals[tile] for tile in sorted(totals)]


def featurize(taps, index, ext, begin, count):
    total = taps[index, 0:1, :] * ext[begin : begin + count, :]
    total = total + taps[index, 1:2, :] * ext[begin - 1 : begin - 1 + count, :]
    return total + taps[index, 2:3, :] * ext[begin - 2 : begin - 2 + count, :]


def head_lanes(head):
    return pl.ds(pl.multiple_of(head * HD, HD), HD)


def early_kernel(
    packed, gs, res, taps_in, long_in, partial, feat, res_out, edge, taps_out, long_out,
    gs_v, ext, prod, copies, sems,
):
    rows, chans = gs.shape
    loads = [(taps_in, taps_out), (long_in, long_out), (gs, gs_v), (res, res_out)]
    moves = [pltpu.make_async_copy(src, dst, sems.at[i]) for i, (src, dst) in enumerate(loads)]
    for move in moves:
        move.start()
    for move in moves:
        move.wait()
    tiles = rows // 8
    pairs = [(tile, group) for group in range(long_in.shape[0] // 8) for tile in range(group, tiles)]
    top = lax.broadcasted_iota(jnp.int32, (rows, HD), 0) < 2
    ext[0:8, :] = jnp.zeros((8, HD), jnp.float32)
    prod[0:8, :] = jnp.zeros((8, HD), jnp.float32)

    def one_head(head, carry):
        lanes = head_lanes(head)
        taps = taps_out[:, :, lanes]

        def feature(index, raw):
            wide = raw.astype(jnp.float32)
            ext[8:, :] = wide
            edge[index, :, lanes] = wide[0:8, :]
            return featurize(taps, index, ext, 8, rows)

        first = feature(0, packed[0:rows, lanes])
        product = (first * feature(2, packed[rows : 2 * rows, lanes])).astype(jnp.bfloat16).astype(jnp.float32)
        feat[:, lanes] = feature(1, gs_v[:, lanes])
        prod[8:, :] = jnp.where(top, 0.0, product)
        shift_copies(prod, copies)
        totals = lag_sums(long_out[:, lanes], copies, 8, pairs)
        partial[:, lanes] = jnp.concatenate(totals, axis=0)
        return carry

    lax.fori_loop(0, chans // HD, one_head, 0)


def in_hbm(*arrays):
    return [pltpu.with_memory_space_constraint(array, pltpu.HBM) for array in arrays]


def early(packed, gs, res, taps, long_taps):
    rows, chans = gs.shape
    hbm = pl.BlockSpec(memory_space=pltpu.HBM)
    vmem = pl.BlockSpec(memory_space=pltpu.VMEM)
    return pl.pallas_call(
        early_kernel,
        in_specs=[vmem] + [hbm] * 4,
        out_specs=[vmem] * 6,
        out_shape=[
            jax.ShapeDtypeStruct((rows, chans), jnp.float32),
            jax.ShapeDtypeStruct((rows, chans), jnp.float32),
            jax.ShapeDtypeStruct((rows, chans), jnp.bfloat16),
            jax.ShapeDtypeStruct((3, 8, chans), jnp.float32),
            jax.ShapeDtypeStruct(taps.shape, jnp.float32),
            jax.ShapeDtypeStruct(long_taps.shape, jnp.bfloat16),
        ],
        scratch_shapes=[
            pltpu.VMEM((rows, chans), jnp.bfloat16),
            pltpu.VMEM((rows + 8, HD), jnp.float32),
            pltpu.VMEM((rows + 8, HD), jnp.float32),
            pltpu.VMEM((8, rows + 8, HD), jnp.float32),
            pltpu.SemaphoreType.DMA((4,)),
        ],
        compiler_params=pltpu.CompilerParams(vmem_limit_bytes=32 << 20),
        cost_estimate=pl.CostEstimate(flops=6_000_000_000, bytes_accessed=2_000_000, transcendentals=0),
        name="early",
    )(packed, *in_hbm(gs, res, taps, long_taps))


def late_kernel(halo, partial, feat, res, edge, taps_in, long_in, stream, squares, ext, prod, copies):
    rows, chans = res.shape
    tiles = rows // 8
    pairs = [(tile, group) for group in range(long_in.shape[0] // 8) for tile in range(min(group + 2, tiles))]
    inside = lax.broadcasted_iota(jnp.int32, (rows, HD), 0) < rows - 6
    prod[0:8, :] = jnp.zeros((8, HD), jnp.float32)
    prod[rows + 8 :, :] = jnp.zeros((8, HD), jnp.float32)
    total = jnp.zeros((8, rows), jnp.float32)

    def one_head(head, total):
        lanes = head_lanes(head)
        taps = taps_in[:, :, lanes]

        def feature(index, begin):
            ext[0:rows, :] = halo[begin : begin + rows, lanes].astype(jnp.float32)
            ext[rows : rows + 8, :] = edge[index, :, lanes]
            return featurize(taps, index, ext, 8, rows)

        first = feature(0, 0)
        product = (first * feature(2, rows)).astype(jnp.bfloat16).astype(jnp.float32)
        prod[8 : rows + 8, :] = jnp.where(inside, product, 0.0)
        shift_copies(prod, copies)
        totals = lag_sums(long_in[:, lanes], copies, rows, pairs)
        filtered = partial[:, lanes] + jnp.concatenate(totals, axis=0)
        ext[0:8, :] = halo[2 * rows : 2 * rows + 8, lanes].astype(jnp.float32)
        ext[8:16, :] = edge[1, :, lanes]
        gate = jnp.concatenate([featurize(taps, 1, ext, 8, 8), feat[8:, lanes]], axis=0)
        out = (res[:, lanes].astype(jnp.float32) + gate * filtered).astype(jnp.bfloat16)
        stream[:, lanes] = out
        wide = out.astype(jnp.float32)
        total = total + lax.dot_general(
            jnp.ones((8, HD), jnp.float32),
            wide * wide,
            (((1,), (1,)), ((), ())),
            precision=HIGHEST,
            preferred_element_type=jnp.float32,
        )
        return total

    total = lax.fori_loop(0, chans // HD, one_head, total)
    for peer in range(squares.shape[0]):
        squares[peer] = total[0:1, :]


def late(halo, partial, feat, res, edge, taps, long_taps):
    rows, chans = res.shape
    vmem = pl.BlockSpec(memory_space=pltpu.VMEM)
    return pl.pallas_call(
        late_kernel,
        in_specs=[vmem] * 7,
        out_specs=[vmem] * 2,
        out_shape=[
            jax.ShapeDtypeStruct((rows, chans), jnp.bfloat16),
            jax.ShapeDtypeStruct((16, 1, rows), jnp.float32),
        ],
        scratch_shapes=[
            pltpu.VMEM((rows + 8, HD), jnp.float32),
            pltpu.VMEM((rows + 16, HD), jnp.float32),
            pltpu.VMEM((8, rows + 16, HD), jnp.float32),
        ],
        compiler_params=pltpu.CompilerParams(vmem_limit_bytes=32 << 20),
        cost_estimate=pl.CostEstimate(flops=30_000_000_000, bytes_accessed=2_000_000, transcendentals=0),
        name="late",
    )(halo, partial, feat, res, edge, taps, long_taps)


def pack_kernel(gf, hv, gs, keys, halo, keys_out, sems):
    rows = gf.shape[0]
    pairs = []
    for copy in range(keys_out.shape[0]):
        for head in range(keys_out.shape[1]):
            pairs.append((keys.at[:, head * HD : (head + 1) * HD], keys_out.at[copy, head]))
    pairs += [
        (gf, halo.at[0:rows]),
        (hv, halo.at[rows : 2 * rows]),
        (gs.at[rows - 8 : rows], halo.at[2 * rows : 2 * rows + 8]),
    ]
    moves = [pltpu.make_async_copy(src, dst, sems.at[i]) for i, (src, dst) in enumerate(pairs)]
    for move in moves:
        move.start()
    for move in moves:
        move.wait()


def pack(gf, hv, gs, keys):
    rows, chans = gf.shape
    heads = chans // HD
    vmem = pl.BlockSpec(memory_space=pltpu.VMEM)
    hbm = pl.BlockSpec(memory_space=pltpu.HBM)
    return pl.pallas_call(
        pack_kernel,
        in_specs=[hbm] * 4,
        out_specs=[vmem, vmem],
        out_shape=[
            jax.ShapeDtypeStruct((2 * rows + 8, chans), jnp.bfloat16),
            jax.ShapeDtypeStruct((2, heads, rows, HD), jnp.bfloat16),
        ],
        scratch_shapes=[pltpu.SemaphoreType.DMA((2 * heads + 3,))],
        compiler_params=pltpu.CompilerParams(vmem_limit_bytes=16 << 20),
        cost_estimate=pl.CostEstimate(flops=0, bytes_accessed=600_000, transcendentals=0),
        name="pack",
    )(*in_hbm(gf, hv, gs, keys))


def normalize_kernel(width, gathered, stream, gain, packed):
    total = gathered[0]
    for peer in range(1, gathered.shape[0]):
        total = total + gathered[peer]
    total = jnp.broadcast_to(total, (8, total.shape[1]))
    total = lax.dot_general(
        jnp.where(lax.broadcasted_iota(jnp.int32, total.shape, 0) == 0, total, 0.0),
        jnp.ones((8, HD), jnp.float32),
        (((0,), (0,)), ((), ())),
        precision=HIGHEST,
        preferred_element_type=jnp.float32,
    )
    inverse = 1.0 / jnp.sqrt(total / width + 1e-06)
    for head in range(packed.shape[1]):
        lanes = slice(head * HD, (head + 1) * HD)
        value = stream[:, lanes].astype(jnp.float32) * inverse * gain[:, lanes]
        value = value.astype(jnp.bfloat16)
        for copy in range(packed.shape[0]):
            packed[copy, head] = value


def normalize(width, gathered, stream, gain):
    rows, chans = stream.shape
    vmem = pl.BlockSpec(memory_space=pltpu.VMEM)
    return pl.pallas_call(
        functools.partial(normalize_kernel, width),
        in_specs=[vmem] * 3,
        out_specs=vmem,
        out_shape=jax.ShapeDtypeStruct((4, chans // HD, rows, HD), jnp.bfloat16),
        cost_estimate=pl.CostEstimate(flops=1_000_000, bytes_accessed=800_000, transcendentals=20_000),
        name="normalize",
    )(gathered, stream, gain)


def score_kernel(place, q0, q1, q2, q3, k0, k1, k2, k3, out, denom, scores, weights, sems):
    rows = q0.shape[0]
    keys = k0.shape[0]
    unit = math.log2(math.e) / math.sqrt(HD)
    chunks = [(begin, min(256, keys - begin)) for begin in range(0, keys, 256)]
    for index, query_ref in enumerate((q0, q1, q2, q3)):
        query = query_ref[...]
        query_pos = place[4 + index] + lax.broadcasted_iota(jnp.int32, (rows, 1), 0)
        top = None
        for part, ref in enumerate((k0, k1, k2, k3)):
            for begin, width in chunks:
                score = lax.dot_general(
                    query,
                    ref[begin : begin + width, :],
                    (((1,), (1,)), ((), ())),
                    preferred_element_type=jnp.float32,
                )
                lane = begin + lax.broadcasted_iota(jnp.int32, (1, width), 1)
                key_pos = place[part] + lane
                for edge in range(rows, keys, rows):
                    if edge < begin + width:
                        key_pos = key_pos + jnp.where(lane >= edge, rows, 0)
                score = jnp.where(key_pos <= query_pos, score * unit, -1e30)
                scores[:, part * keys + begin : part * keys + begin + width] = score
                for piece in range(0, width, 128):
                    piece = score[:, piece : min(piece + 128, width)]
                    if piece.shape[1] < 128:
                        piece = jnp.concatenate(
                            [piece, jnp.full((rows, 128 - piece.shape[1]), -1e30, jnp.float32)], axis=1
                        )
                    top = piece if top is None else jnp.maximum(top, piece)
        top = jnp.max(top, axis=1, keepdims=True)
        total = jnp.zeros((rows, 128), jnp.float32)
        for begin in range(0, 4 * keys, 128):
            expo = jnp.exp2(scores[:, begin : begin + 128] - top)
            total = total + expo
            weights[index, :, begin : begin + 128] = expo.astype(jnp.bfloat16)
        total = jnp.sum(total, axis=1, keepdims=True)
        denom[index] = jnp.broadcast_to(total, (rows, 128))
        pltpu.make_async_copy(weights.at[index], out.at[index], sems.at[index]).start()
    for index in range(4):
        pltpu.make_async_copy(weights.at[index], out.at[index], sems.at[index]).wait()


def score(place, queries, keys):
    rows = queries[0].shape[0]
    blocks = len(queries)
    count = sum(part.shape[0] for part in keys)
    vmem = pl.BlockSpec(memory_space=pltpu.VMEM)
    return pl.pallas_call(
        score_kernel,
        in_specs=[pl.BlockSpec(memory_space=pltpu.SMEM)] + [vmem] * 8,
        out_specs=[pl.BlockSpec(memory_space=pltpu.HBM), vmem],
        out_shape=[
            pltpu.HBM((blocks, rows, count), jnp.bfloat16),
            jax.ShapeDtypeStruct((blocks, rows, 128), jnp.float32),
        ],
        scratch_shapes=[
            pltpu.VMEM((rows, count), jnp.float32),
            pltpu.VMEM((blocks, rows, count), jnp.bfloat16),
            pltpu.SemaphoreType.DMA((blocks,)),
        ],
        compiler_params=pltpu.CompilerParams(vmem_limit_bytes=32 << 20),
        cost_estimate=pl.CostEstimate(
            flops=2 * blocks * rows * count * HD,
            bytes_accessed=8_000_000,
            transcendentals=blocks * rows * count,
        ),
        name="score",
    )(place, *queries, *keys)


def attend_kernel(place, weights_in, denom, v_own, v_other, out, weights, sems):
    blocks, rows, _ = out.shape
    half = v_own.shape[0] // 2
    moves = [
        pltpu.make_async_copy(weights_in.at[index], weights.at[index], sems.at[index]) for index in range(blocks)
    ]
    for move in moves:
        move.start()
    for index, move in enumerate(moves):
        move.wait()
        total = jnp.zeros((rows, HD), jnp.float32)
        for part in range(4):
            begin = pl.multiple_of(place[12 + part // 2] * half, 16)
            ref = v_other if part % 2 else v_own
            total = total + jnp.dot(
                weights[index, :, part * half : (part + 1) * half],
                ref[pl.ds(begin, half), :],
                preferred_element_type=jnp.float32,
            )
        out[place[8 + index]] = (total / denom[index]).astype(jnp.bfloat16)


def attend(place, weights, denom, v_own, v_other):
    blocks, rows, keys = weights.shape
    vmem = pl.BlockSpec(memory_space=pltpu.VMEM)
    return pl.pallas_call(
        attend_kernel,
        in_specs=[pl.BlockSpec(memory_space=pltpu.SMEM), pl.BlockSpec(memory_space=pltpu.HBM), vmem, vmem, vmem],
        out_specs=vmem,
        out_shape=jax.ShapeDtypeStruct((blocks, rows, HD), jnp.bfloat16),
        scratch_shapes=[pltpu.VMEM((blocks, rows, keys), jnp.bfloat16), pltpu.SemaphoreType.DMA((blocks,))],
        compiler_params=pltpu.CompilerParams(vmem_limit_bytes=16 << 20),
        cost_estimate=pl.CostEstimate(
            flops=2 * blocks * rows * keys * HD, bytes_accessed=7_000_000, transcendentals=0
        ),
        name="attend",
    )(place, *in_hbm(weights), denom, v_own, v_other)


def exchange(value, axes):
    return lax.all_to_all(value, axes, 0, 0, tiled=True)


def swap_cores(value):
    return lax.ppermute(value, "c", [(0, 1), (1, 0)])


def shards(residual, gate_first, gate_second, hyena_value, short_taps, long_taps, norm_gain, queries, attn_keys):
    rows, chans = residual.shape
    heads = chans // HD
    count = 32
    width = chans * 16

    core = lax.axis_index("c")
    head = lax.axis_index("h")
    side = lax.axis_index("zh")
    group = side * 16 + lax.axis_index("s") * 8 + core
    owners = [head ^ flip for flip in range(heads)]
    place = [side * 16 + core, side * 16 + 1 - core, (1 - side) * 16 + core, (1 - side) * 16 + 1 - core]
    place = place + [group + owner * 2 for owner in owners]
    place = jnp.concatenate([jnp.stack(place) * rows, jnp.stack(owners + [side, 1 - side])]).astype(jnp.int32)

    last, keys_by_head = pack(gate_first, hyena_value, gate_second, attn_keys)
    keys_near = exchange(keys_by_head.reshape(8, rows, HD), ("s", "h"))
    halo = lax.ppermute(last, ROWS_AXES, [(source, source + 1) for source in range(count - 1)])
    early_parts = early(last, gate_second, residual, short_taps, long_taps)
    stream, squares = late(halo, *early_parts)

    blocks = [lax.dynamic_slice_in_dim(queries, owner * HD, HD, 1) for owner in owners]
    blocks, squares = lax.optimization_barrier((blocks, squares))
    for flip in range(1, heads):
        blocks[flip] = lax.ppermute(blocks[flip], "h", [(source, source ^ flip) for source in range(heads)])
    keys_near, blocks, squares = lax.optimization_barrier((keys_near, blocks, squares))
    keys_far = lax.ppermute(keys_near, "zh", [(0, 1)])
    gathered = exchange(squares, CHAN_AXES)
    packed = normalize(width, gathered, stream, norm_gain.reshape(1, chans))
    packed, keys_far = lax.optimization_barrier((packed, keys_far))
    values_own = exchange(packed.reshape(16, rows, HD), PEERS)

    parts = [keys_near, swap_cores(keys_near), keys_far, swap_cores(keys_far)]
    weights, denom = score(place, blocks, [part.reshape(8 * rows, HD) for part in parts])
    values_own, denom = lax.optimization_barrier((values_own, denom))
    values_other = swap_cores(values_own)
    result = attend(
        place, weights, denom, values_own.reshape(16 * rows, HD), values_other.reshape(16 * rows, HD)
    )
    attended = exchange(result, "h").transpose(1, 0, 2).reshape(rows, chans)
    return stream, attended


def solution(mesh):
    inner = Mesh(mesh.devices.reshape(2, 2, 4, 2, 4, 4), ROWS_AXES + CHAN_AXES)
    both = P(ROWS_AXES, CHAN_AXES)
    return jax.shard_map(
        shards,
        mesh=inner,
        in_specs=(both, both, both, both, P(None, None, CHAN_AXES), P(None, CHAN_AXES), P(CHAN_AXES), both, both),
        out_specs=(both, both),
        check_vma=False,
    )
```

```python
import functools
import math

import jax
import jax.numpy as jnp
from jax import lax
from jax.experimental import pallas as pl
from jax.experimental.pallas import tpu as pltpu
from jax.sharding import Mesh, PartitionSpec as P

HD = 128
ROWS_AXES = ("zh", "s", "h", "c")
CHAN_AXES = ("x", "zl")
PEERS = ("zh", "s", "h")
HIGHEST = lax.Precision.HIGHEST


def shift_copies(prod, copies):
    length = prod.shape[0]
    for lag in range(8):
        copies[lag, 8:length, :] = prod[8 - lag : length - lag, :]


def lag_sums(weights, copies, base, pairs):
    totals = {}
    for group in range(weights.shape[0] // 8):
        wanted = [tile for tile, other in pairs if other == group]
        rows = weights[group * 8 : group * 8 + 8, :].astype(jnp.float32)
        for lag in range(8):
            weight = jnp.broadcast_to(rows[lag : lag + 1, :], rows.shape)
            for tile in wanted:
                begin = base + 8 * (tile - group)
                term = weight * copies[lag, begin : begin + 8, :]
                totals[tile] = totals[tile] + term if tile in totals else term
    return [totals[tile] for tile in sorted(totals)]


def featurize(taps, index, ext, begin, count):
    total = taps[index, 0:1, :] * ext[begin : begin + count, :]
    total = total + taps[index, 1:2, :] * ext[begin - 1 : begin - 1 + count, :]
    return total + taps[index, 2:3, :] * ext[begin - 2 : begin - 2 + count, :]


def head_lanes(head):
    return pl.ds(pl.multiple_of(head * HD, HD), HD)


def early_kernel(
    packed, gs, res, taps_in, long_in, partial, feat, res_out, edge, taps_out, long_out,
    gs_v, ext, prod, copies, sems,
):
    rows, chans = gs.shape
    loads = [(taps_in, taps_out), (long_in, long_out), (gs, gs_v), (res, res_out)]
    moves = [pltpu.make_async_copy(src, dst, sems.at[i]) for i, (src, dst) in enumerate(loads)]
    for move in moves:
        move.start()
    for move in moves:
        move.wait()
    tiles = rows // 8
    pairs = [(tile, group) for group in range(long_in.shape[0] // 8) for tile in range(group, tiles)]
    top = lax.broadcasted_iota(jnp.int32, (rows, HD), 0) < 2
    ext[0:8, :] = jnp.zeros((8, HD), jnp.float32)
    prod[0:8, :] = jnp.zeros((8, HD), jnp.float32)

    def one_head(head, carry):
        lanes = head_lanes(head)
        taps = taps_out[:, :, lanes]

        def feature(index, raw):
            wide = raw.astype(jnp.float32)
            ext[8:, :] = wide
            edge[index, :, lanes] = wide[0:8, :]
            return featurize(taps, index, ext, 8, rows)

        first = feature(0, packed[0:rows, lanes])
        product = (first * feature(2, packed[rows : 2 * rows, lanes])).astype(jnp.bfloat16).astype(jnp.float32)
        feat[:, lanes] = feature(1, gs_v[:, lanes])
        prod[8:, :] = jnp.where(top, 0.0, product)
        shift_copies(prod, copies)
        totals = lag_sums(long_out[:, lanes], copies, 8, pairs)
        partial[:, lanes] = jnp.concatenate(totals, axis=0)
        return carry

    lax.fori_loop(0, chans // HD, one_head, 0)


def in_hbm(*arrays):
    return [pltpu.with_memory_space_constraint(array, pltpu.HBM) for array in arrays]


def early(packed, gs, res, taps, long_taps):
    rows, chans = gs.shape
    hbm = pl.BlockSpec(memory_space=pltpu.HBM)
    vmem = pl.BlockSpec(memory_space=pltpu.VMEM)
    return pl.pallas_call(
        early_kernel,
        in_specs=[vmem] + [hbm] * 4,
        out_specs=[vmem] * 6,
        out_shape=[
            jax.ShapeDtypeStruct((rows, chans), jnp.float32),
            jax.ShapeDtypeStruct((rows, chans), jnp.float32),
            jax.ShapeDtypeStruct((rows, chans), jnp.bfloat16),
            jax.ShapeDtypeStruct((3, 8, chans), jnp.float32),
            jax.ShapeDtypeStruct(taps.shape, jnp.float32),
            jax.ShapeDtypeStruct(long_taps.shape, jnp.bfloat16),
        ],
        scratch_shapes=[
            pltpu.VMEM((rows, chans), jnp.bfloat16),
            pltpu.VMEM((rows + 8, HD), jnp.float32),
            pltpu.VMEM((rows + 8, HD), jnp.float32),
            pltpu.VMEM((8, rows + 8, HD), jnp.float32),
            pltpu.SemaphoreType.DMA((4,)),
        ],
        compiler_params=pltpu.CompilerParams(vmem_limit_bytes=32 << 20),
        cost_estimate=pl.CostEstimate(flops=6_000_000_000, bytes_accessed=2_000_000, transcendentals=0),
        name="early",
    )(packed, *in_hbm(gs, res, taps, long_taps))


def late_kernel(halo, partial, feat, res, edge, taps_in, long_in, stream, squares, ext, prod, copies):
    rows, chans = res.shape
    tiles = rows // 8
    pairs = [(tile, group) for group in range(long_in.shape[0] // 8) for tile in range(min(group + 2, tiles))]
    inside = lax.broadcasted_iota(jnp.int32, (rows, HD), 0) < rows - 6
    prod[0:8, :] = jnp.zeros((8, HD), jnp.float32)
    prod[rows + 8 :, :] = jnp.zeros((8, HD), jnp.float32)
    total = jnp.zeros((8, rows), jnp.float32)

    def one_head(head, total):
        lanes = head_lanes(head)
        taps = taps_in[:, :, lanes]

        def feature(index, begin):
            ext[0:rows, :] = halo[begin : begin + rows, lanes].astype(jnp.float32)
            ext[rows : rows + 8, :] = edge[index, :, lanes]
            return featurize(taps, index, ext, 8, rows)

        first = feature(0, 0)
        product = (first * feature(2, rows)).astype(jnp.bfloat16).astype(jnp.float32)
        prod[8 : rows + 8, :] = jnp.where(inside, product, 0.0)
        shift_copies(prod, copies)
        totals = lag_sums(long_in[:, lanes], copies, rows, pairs)
        filtered = partial[:, lanes] + jnp.concatenate(totals, axis=0)
        ext[0:8, :] = halo[2 * rows : 2 * rows + 8, lanes].astype(jnp.float32)
        ext[8:16, :] = edge[1, :, lanes]
        gate = jnp.concatenate([featurize(taps, 1, ext, 8, 8), feat[8:, lanes]], axis=0)
        out = (res[:, lanes].astype(jnp.float32) + gate * filtered).astype(jnp.bfloat16)
        stream[:, lanes] = out
        wide = out.astype(jnp.float32)
        total = total + lax.dot_general(
            jnp.ones((8, HD), jnp.float32),
            wide * wide,
            (((1,), (1,)), ((), ())),
            precision=HIGHEST,
            preferred_element_type=jnp.float32,
        )
        return total

    total = lax.fori_loop(0, chans // HD, one_head, total)
    for peer in range(squares.shape[0]):
        squares[peer] = total[0:1, :]


def late(halo, partial, feat, res, edge, taps, long_taps):
    rows, chans = res.shape
    vmem = pl.BlockSpec(memory_space=pltpu.VMEM)
    return pl.pallas_call(
        late_kernel,
        in_specs=[vmem] * 7,
        out_specs=[vmem] * 2,
        out_shape=[
            jax.ShapeDtypeStruct((rows, chans), jnp.bfloat16),
            jax.ShapeDtypeStruct((16, 1, rows), jnp.float32),
        ],
        scratch_shapes=[
            pltpu.VMEM((rows + 8, HD), jnp.float32),
            pltpu.VMEM((rows + 16, HD), jnp.float32),
            pltpu.VMEM((8, rows + 16, HD), jnp.float32),
        ],
        compiler_params=pltpu.CompilerParams(vmem_limit_bytes=32 << 20),
        cost_estimate=pl.CostEstimate(flops=30_000_000_000, bytes_accessed=2_000_000, transcendentals=0),
        name="late",
    )(halo, partial, feat, res, edge, taps, long_taps)


def pack_kernel(gf, hv, gs, keys, queries, halo, blocks, sems):
    rows = gf.shape[0]
    pairs = []
    for copy in range(blocks.shape[0]):
        for head in range(blocks.shape[1]):
            for kind, source in enumerate((keys, queries)):
                pairs.append((source.at[:, head * HD : (head + 1) * HD], blocks.at[copy, head, kind]))
    pairs += [
        (gf, halo.at[0:rows]),
        (hv, halo.at[rows : 2 * rows]),
        (gs.at[rows - 8 : rows], halo.at[2 * rows : 2 * rows + 8]),
    ]
    moves = [pltpu.make_async_copy(src, dst, sems.at[i]) for i, (src, dst) in enumerate(pairs)]
    for move in moves:
        move.start()
    for move in moves:
        move.wait()


def pack(gf, hv, gs, keys, queries):
    rows, chans = gf.shape
    heads = chans // HD
    vmem = pl.BlockSpec(memory_space=pltpu.VMEM)
    hbm = pl.BlockSpec(memory_space=pltpu.HBM)
    return pl.pallas_call(
        pack_kernel,
        in_specs=[hbm] * 5,
        out_specs=[vmem, vmem],
        out_shape=[
            jax.ShapeDtypeStruct((2 * rows + 8, chans), jnp.bfloat16),
            jax.ShapeDtypeStruct((2, heads, 2, rows, HD), jnp.bfloat16),
        ],
        scratch_shapes=[pltpu.SemaphoreType.DMA((4 * heads + 3,))],
        compiler_params=pltpu.CompilerParams(vmem_limit_bytes=16 << 20),
        cost_estimate=pl.CostEstimate(flops=0, bytes_accessed=600_000, transcendentals=0),
        name="pack",
    )(*in_hbm(gf, hv, gs, keys, queries))


def normalize_kernel(width, gathered, stream, gain, packed):
    total = gathered[0]
    for peer in range(1, gathered.shape[0]):
        total = total + gathered[peer]
    total = jnp.broadcast_to(total, (8, total.shape[1]))
    total = lax.dot_general(
        jnp.where(lax.broadcasted_iota(jnp.int32, total.shape, 0) == 0, total, 0.0),
        jnp.ones((8, HD), jnp.float32),
        (((0,), (0,)), ((), ())),
        precision=HIGHEST,
        preferred_element_type=jnp.float32,
    )
    inverse = 1.0 / jnp.sqrt(total / width + 1e-06)
    for head in range(packed.shape[1]):
        lanes = slice(head * HD, (head + 1) * HD)
        value = stream[:, lanes].astype(jnp.float32) * inverse * gain[:, lanes]
        value = value.astype(jnp.bfloat16)
        for copy in range(packed.shape[0]):
            packed[copy, head] = value


def normalize(width, gathered, stream, gain):
    rows, chans = stream.shape
    vmem = pl.BlockSpec(memory_space=pltpu.VMEM)
    return pl.pallas_call(
        functools.partial(normalize_kernel, width),
        in_specs=[vmem] * 3,
        out_specs=vmem,
        out_shape=jax.ShapeDtypeStruct((4, chans // HD, rows, HD), jnp.bfloat16),
        cost_estimate=pl.CostEstimate(flops=1_000_000, bytes_accessed=800_000, transcendentals=20_000),
        name="normalize",
    )(gathered, stream, gain)


def score_kernel(place, q, k0, k1, k2, k3, out, denom, keys, scores, weights, sems):
    rows = keys.shape[1] // 16
    count = keys.shape[1]
    block = scores.shape[0]
    unit = math.log2(math.e) / math.sqrt(HD)
    for part, ref in enumerate((k0, k1, k2, k3)):
        begin = pl.multiple_of(place[6 + part // 2], 64)
        keys[part % 2, pl.ds(begin, count // 2), :] = ref[...]
    chunks = [(begin, min(256, count - begin)) for begin in range(0, count, 256)]
    line = lax.broadcasted_iota(jnp.int32, (block, 1), 0)
    for index in range(q.shape[0] // block):
        query = q[index * block : (index + 1) * block, :]
        query_pos = line + place[2 + index * (block // rows)]
        for step in range(1, block // rows):
            moved = place[2 + index * (block // rows) + step] - step * rows
            query_pos = jnp.where(line >= step * rows, line + moved, query_pos)
        top = None
        for part in range(2):
            for begin, width in chunks:
                score = lax.dot_general(
                    query,
                    keys[part, begin : begin + width, :],
                    (((1,), (1,)), ((), ())),
                    preferred_element_type=jnp.float32,
                )
                lane = begin + lax.broadcasted_iota(jnp.int32, (1, width), 1)
                key_pos = place[part] + lane
                for edge in range(rows, count, rows):
                    if edge < begin + width:
                        key_pos = key_pos + jnp.where(lane >= edge, rows, 0)
                score = jnp.where(key_pos <= query_pos, score * unit, -1e30)
                scores[:, part * count + begin : part * count + begin + width] = score
                for piece in range(0, width, 128):
                    piece = score[:, piece : piece + 128]
                    top = piece if top is None else jnp.maximum(top, piece)
        top = jnp.max(top, axis=1, keepdims=True)
        total = jnp.zeros((block, 128), jnp.float32)
        for begin in range(0, 2 * count, 128):
            expo = jnp.exp2(scores[:, begin : begin + 128] - top)
            total = total + expo
            weights[index * block : (index + 1) * block, begin : begin + 128] = expo.astype(jnp.bfloat16)
        total = jnp.sum(total, axis=1, keepdims=True)
        denom[index * block : (index + 1) * block, :] = jnp.broadcast_to(total, (block, 128))
        lines = pl.ds(index * block, block)
        pltpu.make_async_copy(weights.at[lines], out.at[lines], sems.at[index]).start()
    for index in range(q.shape[0] // block):
        lines = pl.ds(index * block, block)
        pltpu.make_async_copy(weights.at[lines], out.at[lines], sems.at[index]).wait()


def score(place, q, keys):
    lines = q.shape[0]
    count = sum(part.shape[0] for part in keys)
    block = lines // 2
    vmem = pl.BlockSpec(memory_space=pltpu.VMEM)
    return pl.pallas_call(
        score_kernel,
        in_specs=[pl.BlockSpec(memory_space=pltpu.SMEM)] + [vmem] * 5,
        out_specs=[pl.BlockSpec(memory_space=pltpu.HBM), vmem],
        out_shape=[
            pltpu.HBM((lines, count), jnp.bfloat16),
            jax.ShapeDtypeStruct((lines, 128), jnp.float32),
        ],
        scratch_shapes=[
            pltpu.VMEM((2, count // 2, HD), jnp.bfloat16),
            pltpu.VMEM((block, count), jnp.float32),
            pltpu.VMEM((lines, count), jnp.bfloat16),
            pltpu.SemaphoreType.DMA((2,)),
        ],
        compiler_params=pltpu.CompilerParams(vmem_limit_bytes=32 << 20),
        cost_estimate=pl.CostEstimate(
            flops=2 * lines * count * HD, bytes_accessed=8_000_000, transcendentals=lines * count
        ),
        name="score",
    )(place, q, *keys)


def attend_kernel(weights_in, denom, v_own, v_other, out, weights, sems):
    keys = v_own.shape[0]
    cuts = [0, 1152, keys, keys + 1152, 2 * keys]
    moves = []
    for index, (begin, end) in enumerate(zip(cuts, cuts[1:])):
        moves.append(
            pltpu.make_async_copy(weights_in.at[:, begin:end], weights.at[:, begin:end], sems.at[index])
        )
    for move in moves:
        move.start()
    total = jnp.zeros(out.shape, jnp.float32)
    for move, begin, end in zip(moves, cuts, cuts[1:]):
        move.wait()
        ref, first = (v_own, begin) if begin < keys else (v_other, begin - keys)
        total = total + jnp.dot(
            weights[:, begin:end], ref[first : first + end - begin, :], preferred_element_type=jnp.float32
        )
    out[...] = (total / denom[...]).astype(jnp.bfloat16)


def attend(weights, denom, v_own, v_other):
    lines, count = weights.shape
    vmem = pl.BlockSpec(memory_space=pltpu.VMEM)
    return pl.pallas_call(
        attend_kernel,
        in_specs=[pl.BlockSpec(memory_space=pltpu.HBM), vmem, vmem, vmem],
        out_specs=vmem,
        out_shape=jax.ShapeDtypeStruct((lines, HD), jnp.bfloat16),
        scratch_shapes=[pltpu.VMEM((lines, count), jnp.bfloat16), pltpu.SemaphoreType.DMA((4,))],
        compiler_params=pltpu.CompilerParams(vmem_limit_bytes=16 << 20),
        cost_estimate=pl.CostEstimate(
            flops=2 * lines * count * HD, bytes_accessed=7_000_000, transcendentals=0
        ),
        name="attend",
    )(*in_hbm(weights), denom, v_own, v_other)


def exchange(value, axes):
    return lax.all_to_all(value, axes, 0, 0, tiled=True)


def swap_cores(value):
    return lax.ppermute(value, "c", [(0, 1), (1, 0)])


def shards(residual, gate_first, gate_second, hyena_value, short_taps, long_taps, norm_gain, queries, attn_keys):
    rows, chans = residual.shape
    heads = chans // HD
    count = 32
    width = chans * 16

    core = lax.axis_index("c")
    side = lax.axis_index("zh")
    group = side * 16 + lax.axis_index("s") * 8 + core
    place = [core, 1 - core] + [group + owner * 2 for owner in range(heads)]
    place = (jnp.stack(place + [side * 8, (1 - side) * 8]) * rows).astype(jnp.int32)

    last, blocks = pack(gate_first, hyena_value, gate_second, attn_keys, queries)
    blocks = exchange(blocks.reshape(8, 2, rows, HD), ("s", "h"))
    halo = lax.ppermute(last, ROWS_AXES, [(source, source + 1) for source in range(count - 1)])
    early_parts = early(last, gate_second, residual, short_taps, long_taps)
    stream, squares = late(halo, *early_parts)

    blocks, squares = lax.optimization_barrier((blocks, squares))
    keys_near = blocks[:, 0]
    my_queries = lax.dynamic_slice_in_dim(blocks, lax.axis_index("s") * heads, heads, 0)[:, 1]
    keys_far = lax.ppermute(keys_near, "zh", [(0, 1)])
    gathered = exchange(squares, CHAN_AXES)
    packed = normalize(width, gathered, stream, norm_gain.reshape(1, chans))
    packed, keys_far = lax.optimization_barrier((packed, keys_far))
    values_own = exchange(packed.reshape(16, rows, HD), PEERS)

    parts = [keys_near, swap_cores(keys_near), keys_far, swap_cores(keys_far)]
    weights, denom = score(
        place, my_queries.reshape(heads * rows, HD), [part.reshape(8 * rows, HD) for part in parts]
    )
    values_own, denom = lax.optimization_barrier((values_own, denom))
    values_other = swap_cores(values_own)
    result = attend(
        weights, denom, values_own.reshape(16 * rows, HD), values_other.reshape(16 * rows, HD)
    )
    attended = exchange(result.reshape(heads, rows, HD), "h").transpose(1, 0, 2).reshape(rows, chans)
    return stream, attended


def solution(mesh):
    inner = Mesh(mesh.devices.reshape(2, 2, 4, 2, 4, 4), ROWS_AXES + CHAN_AXES)
    both = P(ROWS_AXES, CHAN_AXES)
    return jax.shard_map(
        shards,
        mesh=inner,
        in_specs=(both, both, both, both, P(None, None, CHAN_AXES), P(None, CHAN_AXES), P(CHAN_AXES), both, both),
        out_specs=(both, both),
        check_vma=False,
    )
```

```python
import functools
import math

import jax
import jax.numpy as jnp
from jax import lax
from jax.experimental import pallas as pl
from jax.experimental.pallas import tpu as pltpu
from jax.sharding import Mesh, PartitionSpec as P

HD = 128
ROWS_AXES = ("zh", "s", "h", "c")
CHAN_AXES = ("x", "zl")
PEERS = ("zh", "s", "h")
HIGHEST = lax.Precision.HIGHEST


def shift_copies(prod, copies):
    length = prod.shape[0]
    for lag in range(8):
        copies[lag, 8:length, :] = prod[8 - lag : length - lag, :]


def lag_sums(weights, copies, base, pairs):
    totals = {}
    for group in range(weights.shape[0] // 8):
        wanted = [tile for tile, other in pairs if other == group]
        rows = weights[group * 8 : group * 8 + 8, :].astype(jnp.float32)
        for lag in range(8):
            weight = jnp.broadcast_to(rows[lag : lag + 1, :], rows.shape)
            for tile in wanted:
                begin = base + 8 * (tile - group)
                term = weight * copies[lag, begin : begin + 8, :]
                totals[tile] = totals[tile] + term if tile in totals else term
    return [totals[tile] for tile in sorted(totals)]


def featurize(taps, index, ext, begin, count):
    total = taps[index, 0:1, :] * ext[begin : begin + count, :]
    total = total + taps[index, 1:2, :] * ext[begin - 1 : begin - 1 + count, :]
    return total + taps[index, 2:3, :] * ext[begin - 2 : begin - 2 + count, :]


def head_lanes(head):
    return pl.ds(pl.multiple_of(head * HD, HD), HD)


def early_kernel(
    packed, gs, res, taps_in, long_in, partial, feat, res_out, edge, taps_out, long_out,
    gs_v, ext, prod, copies, sems,
):
    rows, chans = gs.shape
    loads = [(taps_in, taps_out), (long_in, long_out), (gs, gs_v), (res, res_out)]
    moves = [pltpu.make_async_copy(src, dst, sems.at[i]) for i, (src, dst) in enumerate(loads)]
    for move in moves:
        move.start()
    for move in moves:
        move.wait()
    tiles = rows // 8
    pairs = [(tile, group) for group in range(long_in.shape[0] // 8) for tile in range(group, tiles)]
    top = lax.broadcasted_iota(jnp.int32, (rows, HD), 0) < 2
    ext[0:8, :] = jnp.zeros((8, HD), jnp.float32)
    prod[0:8, :] = jnp.zeros((8, HD), jnp.float32)

    def one_head(head, carry):
        lanes = head_lanes(head)
        taps = taps_out[:, :, lanes]

        def feature(index, raw):
            wide = raw.astype(jnp.float32)
            ext[8:, :] = wide
            edge[index, :, lanes] = wide[0:8, :]
            return featurize(taps, index, ext, 8, rows)

        first = feature(0, packed[0:rows, lanes])
        product = (first * feature(2, packed[rows : 2 * rows, lanes])).astype(jnp.bfloat16).astype(jnp.float32)
        feat[:, lanes] = feature(1, gs_v[:, lanes])
        prod[8:, :] = jnp.where(top, 0.0, product)
        shift_copies(prod, copies)
        totals = lag_sums(long_out[:, lanes], copies, 8, pairs)
        partial[:, lanes] = jnp.concatenate(totals, axis=0)
        return carry

    lax.fori_loop(0, chans // HD, one_head, 0)


def in_hbm(*arrays):
    return [pltpu.with_memory_space_constraint(array, pltpu.HBM) for array in arrays]


def early(packed, gs, res, taps, long_taps):
    rows, chans = gs.shape
    hbm = pl.BlockSpec(memory_space=pltpu.HBM)
    vmem = pl.BlockSpec(memory_space=pltpu.VMEM)
    return pl.pallas_call(
        early_kernel,
        in_specs=[vmem] + [hbm] * 4,
        out_specs=[vmem] * 6,
        out_shape=[
            jax.ShapeDtypeStruct((rows, chans), jnp.float32),
            jax.ShapeDtypeStruct((rows, chans), jnp.float32),
            jax.ShapeDtypeStruct((rows, chans), jnp.bfloat16),
            jax.ShapeDtypeStruct((3, 8, chans), jnp.float32),
            jax.ShapeDtypeStruct(taps.shape, jnp.float32),
            jax.ShapeDtypeStruct(long_taps.shape, jnp.bfloat16),
        ],
        scratch_shapes=[
            pltpu.VMEM((rows, chans), jnp.bfloat16),
            pltpu.VMEM((rows + 8, HD), jnp.float32),
            pltpu.VMEM((rows + 8, HD), jnp.float32),
            pltpu.VMEM((8, rows + 8, HD), jnp.float32),
            pltpu.SemaphoreType.DMA((4,)),
        ],
        compiler_params=pltpu.CompilerParams(vmem_limit_bytes=32 << 20),
        cost_estimate=pl.CostEstimate(flops=6_000_000_000, bytes_accessed=2_000_000, transcendentals=0),
        name="early",
    )(packed, *in_hbm(gs, res, taps, long_taps))


def late_kernel(halo, partial, feat, res, edge, taps_in, long_in, stream, squares, ext, prod, copies):
    rows, chans = res.shape
    tiles = rows // 8
    pairs = [(tile, group) for group in range(long_in.shape[0] // 8) for tile in range(min(group + 2, tiles))]
    inside = lax.broadcasted_iota(jnp.int32, (rows, HD), 0) < rows - 6
    prod[0:8, :] = jnp.zeros((8, HD), jnp.float32)
    prod[rows + 8 :, :] = jnp.zeros((8, HD), jnp.float32)
    total = jnp.zeros((8, rows), jnp.float32)

    def one_head(head, total):
        lanes = head_lanes(head)
        taps = taps_in[:, :, lanes]

        def feature(index, begin):
            ext[0:rows, :] = halo[begin : begin + rows, lanes].astype(jnp.float32)
            ext[rows : rows + 8, :] = edge[index, :, lanes]
            return featurize(taps, index, ext, 8, rows)

        first = feature(0, 0)
        product = (first * feature(2, rows)).astype(jnp.bfloat16).astype(jnp.float32)
        prod[8 : rows + 8, :] = jnp.where(inside, product, 0.0)
        shift_copies(prod, copies)
        totals = lag_sums(long_in[:, lanes], copies, rows, pairs)
        filtered = partial[:, lanes] + jnp.concatenate(totals, axis=0)
        ext[0:8, :] = halo[2 * rows : 2 * rows + 8, lanes].astype(jnp.float32)
        ext[8:16, :] = edge[1, :, lanes]
        gate = jnp.concatenate([featurize(taps, 1, ext, 8, 8), feat[8:, lanes]], axis=0)
        out = (res[:, lanes].astype(jnp.float32) + gate * filtered).astype(jnp.bfloat16)
        stream[:, lanes] = out
        wide = out.astype(jnp.float32)
        total = total + lax.dot_general(
            jnp.ones((8, HD), jnp.float32),
            wide * wide,
            (((1,), (1,)), ((), ())),
            precision=HIGHEST,
            preferred_element_type=jnp.float32,
        )
        return total

    total = lax.fori_loop(0, chans // HD, one_head, total)
    for peer in range(squares.shape[0]):
        squares[peer] = total[0:1, :]


def late(halo, partial, feat, res, edge, taps, long_taps):
    rows, chans = res.shape
    vmem = pl.BlockSpec(memory_space=pltpu.VMEM)
    return pl.pallas_call(
        late_kernel,
        in_specs=[vmem] * 7,
        out_specs=[vmem] * 2,
        out_shape=[
            jax.ShapeDtypeStruct((rows, chans), jnp.bfloat16),
            jax.ShapeDtypeStruct((16, 1, rows), jnp.float32),
        ],
        scratch_shapes=[
            pltpu.VMEM((rows + 8, HD), jnp.float32),
            pltpu.VMEM((rows + 16, HD), jnp.float32),
            pltpu.VMEM((8, rows + 16, HD), jnp.float32),
        ],
        compiler_params=pltpu.CompilerParams(vmem_limit_bytes=32 << 20),
        cost_estimate=pl.CostEstimate(flops=30_000_000_000, bytes_accessed=2_000_000, transcendentals=0),
        name="late",
    )(halo, partial, feat, res, edge, taps, long_taps)


def pack_kernel(gf, hv, gs, keys, halo, blocks, sems):
    rows = gf.shape[0]
    pairs = []
    for copy in range(blocks.shape[0]):
        for head in range(blocks.shape[1]):
            pairs.append((keys.at[:, head * HD : (head + 1) * HD], blocks.at[copy, head]))
    pairs += [
        (gf, halo.at[0:rows]),
        (hv, halo.at[rows : 2 * rows]),
        (gs.at[rows - 8 : rows], halo.at[2 * rows : 2 * rows + 8]),
    ]
    moves = [pltpu.make_async_copy(src, dst, sems.at[i]) for i, (src, dst) in enumerate(pairs)]
    for move in moves:
        move.start()
    for move in moves:
        move.wait()


def pack(gf, hv, gs, keys):
    rows, chans = gf.shape
    heads = chans // HD
    vmem = pl.BlockSpec(memory_space=pltpu.VMEM)
    hbm = pl.BlockSpec(memory_space=pltpu.HBM)
    return pl.pallas_call(
        pack_kernel,
        in_specs=[hbm] * 4,
        out_specs=[vmem, vmem],
        out_shape=[
            jax.ShapeDtypeStruct((2 * rows + 8, chans), jnp.bfloat16),
            jax.ShapeDtypeStruct((2, heads, rows, HD), jnp.bfloat16),
        ],
        scratch_shapes=[pltpu.SemaphoreType.DMA((2 * heads + 3,))],
        compiler_params=pltpu.CompilerParams(vmem_limit_bytes=16 << 20),
        cost_estimate=pl.CostEstimate(flops=0, bytes_accessed=600_000, transcendentals=0),
        name="pack",
    )(*in_hbm(gf, hv, gs, keys))


def normalize_kernel(width, gathered, stream, gain, packed):
    total = gathered[0]
    for peer in range(1, gathered.shape[0]):
        total = total + gathered[peer]
    total = jnp.broadcast_to(total, (8, total.shape[1]))
    total = lax.dot_general(
        jnp.where(lax.broadcasted_iota(jnp.int32, total.shape, 0) == 0, total, 0.0),
        jnp.ones((8, HD), jnp.float32),
        (((0,), (0,)), ((), ())),
        precision=HIGHEST,
        preferred_element_type=jnp.float32,
    )
    inverse = 1.0 / jnp.sqrt(total / width + 1e-06)
    for head in range(packed.shape[1]):
        lanes = slice(head * HD, (head + 1) * HD)
        value = stream[:, lanes].astype(jnp.float32) * inverse * gain[:, lanes]
        value = value.astype(jnp.bfloat16)
        for copy in range(packed.shape[0]):
            packed[copy, head] = value


def normalize(width, gathered, stream, gain):
    rows, chans = stream.shape
    vmem = pl.BlockSpec(memory_space=pltpu.VMEM)
    return pl.pallas_call(
        functools.partial(normalize_kernel, width),
        in_specs=[vmem] * 3,
        out_specs=vmem,
        out_shape=jax.ShapeDtypeStruct((4, chans // HD, rows, HD), jnp.bfloat16),
        compiler_params=pltpu.CompilerParams(vmem_limit_bytes=8 << 20),
        cost_estimate=pl.CostEstimate(flops=1_000_000, bytes_accessed=800_000, transcendentals=20_000),
        name="normalize",
    )(gathered, *in_hbm(stream), gain)


def score_kernel(place, q0, q1, q2, q3, k0, k1, k2, k3, out, denom, q, keys, scores, weights, sems):
    rows = keys.shape[1] // 16
    count = keys.shape[1]
    block = scores.shape[0]
    unit = math.log2(math.e) / math.sqrt(HD)
    for part, ref in enumerate((k0, k1, k2, k3)):
        begin = pl.multiple_of(place[6 + part // 2], 64)
        keys[part % 2, pl.ds(begin, count // 2), :] = ref[...]
    for flip, ref in enumerate((q0, q1, q2, q3)):
        begin = pl.multiple_of(place[8 + flip], 8)
        q[pl.ds(begin, rows), :] = ref[...].astype(jnp.float32)
    chunks = [(begin, min(256, count - begin)) for begin in range(0, count, 256)]
    line = lax.broadcasted_iota(jnp.int32, (block, 1), 0)
    for index in range(q.shape[0] // block):
        query = q[index * block : (index + 1) * block, :].astype(jnp.bfloat16)
        query_pos = line + place[2 + index * (block // rows)]
        for step in range(1, block // rows):
            moved = place[2 + index * (block // rows) + step] - step * rows
            query_pos = jnp.where(line >= step * rows, line + moved, query_pos)
        top = None
        for part in range(2):
            for begin, width in chunks:
                score = lax.dot_general(
                    query,
                    keys[part, begin : begin + width, :],
                    (((1,), (1,)), ((), ())),
                    preferred_element_type=jnp.float32,
                )
                lane = begin + lax.broadcasted_iota(jnp.int32, (1, width), 1)
                key_pos = place[part] + lane
                for edge in range(rows, count, rows):
                    if edge < begin + width:
                        key_pos = key_pos + jnp.where(lane >= edge, rows, 0)
                score = jnp.where(key_pos <= query_pos, score * unit, -1e30)
                scores[:, part * count + begin : part * count + begin + width] = score
                for piece in range(0, width, 128):
                    piece = score[:, piece : piece + 128]
                    top = piece if top is None else jnp.maximum(top, piece)
        top = jnp.max(top, axis=1, keepdims=True)
        total = jnp.zeros((block, 128), jnp.float32)
        for begin in range(0, 2 * count, 128):
            expo = jnp.exp2(scores[:, begin : begin + 128] - top)
            total = total + expo
            weights[index * block : (index + 1) * block, begin : begin + 128] = expo.astype(jnp.bfloat16)
        total = jnp.sum(total, axis=1, keepdims=True)
        denom[index * block : (index + 1) * block, :] = jnp.broadcast_to(total, (block, 128))
        lines = pl.ds(index * block, block)
        pltpu.make_async_copy(weights.at[lines], out.at[lines], sems.at[index]).start()
    for index in range(q.shape[0] // block):
        lines = pl.ds(index * block, block)
        pltpu.make_async_copy(weights.at[lines], out.at[lines], sems.at[index]).wait()


def score(place, queries, keys):
    lines = sum(part.shape[0] for part in queries)
    count = sum(part.shape[0] for part in keys)
    block = lines // 2
    vmem = pl.BlockSpec(memory_space=pltpu.VMEM)
    return pl.pallas_call(
        score_kernel,
        in_specs=[pl.BlockSpec(memory_space=pltpu.SMEM)] + [vmem] * 8,
        out_specs=[pl.BlockSpec(memory_space=pltpu.HBM), vmem],
        out_shape=[
            pltpu.HBM((lines, count), jnp.bfloat16),
            jax.ShapeDtypeStruct((lines, 128), jnp.float32),
        ],
        scratch_shapes=[
            pltpu.VMEM((lines, HD), jnp.float32),
            pltpu.VMEM((2, count // 2, HD), jnp.bfloat16),
            pltpu.VMEM((block, count), jnp.float32),
            pltpu.VMEM((lines, count), jnp.bfloat16),
            pltpu.SemaphoreType.DMA((2,)),
        ],
        compiler_params=pltpu.CompilerParams(vmem_limit_bytes=32 << 20),
        cost_estimate=pl.CostEstimate(
            flops=2 * lines * count * HD, bytes_accessed=8_000_000, transcendentals=lines * count
        ),
        name="score",
    )(place, *queries, *keys)


def attend_kernel(half, weights_in, *refs):
    if half:
        denom, before, values, out, weights, sems = refs
    else:
        values, out, weights, sems = refs
    keys = values.shape[0]
    cuts = [0] + list(range(keys % 512 + 512, keys + 1, 512))
    moves = []
    for index, (begin, end) in enumerate(zip(cuts, cuts[1:])):
        src = weights_in.at[:, half * keys + begin : half * keys + end]
        moves.append(pltpu.make_async_copy(src, weights.at[:, begin:end], sems.at[index]))
    moves[0].start()
    moves[1].start()
    total = before[...] if half else jnp.zeros(out.shape, jnp.float32)
    for index, (begin, end) in enumerate(zip(cuts, cuts[1:])):
        moves[index].wait()
        if index + 2 < len(moves):
            moves[index + 2].start()
        total = total + jnp.dot(
            weights[:, begin:end], values[begin:end, :], preferred_element_type=jnp.float32
        )
    out[...] = (total / denom[...]).astype(jnp.bfloat16) if half else total


def attend(half, weights, *args):
    lines, count = weights.shape
    keys = count // 2
    vmem = pl.BlockSpec(memory_space=pltpu.VMEM)
    return pl.pallas_call(
        functools.partial(attend_kernel, half),
        in_specs=[pl.BlockSpec(memory_space=pltpu.HBM)] + [vmem] * len(args),
        out_specs=vmem,
        out_shape=jax.ShapeDtypeStruct((lines, HD), jnp.bfloat16 if half else jnp.float32),
        scratch_shapes=[pltpu.VMEM((lines, keys), jnp.bfloat16), pltpu.SemaphoreType.DMA((4,))],
        compiler_params=pltpu.CompilerParams(vmem_limit_bytes=16 << 20),
        cost_estimate=pl.CostEstimate(
            flops=2 * lines * keys * HD, bytes_accessed=3_500_000, transcendentals=0
        ),
        name="attend_other" if half else "attend_own",
    )(*in_hbm(weights), *args)


def exchange(value, axes):
    return lax.all_to_all(value, axes, 0, 0, tiled=True)


def swap_cores(value):
    return lax.ppermute(value, "c", [(0, 1), (1, 0)])


def shards(residual, gate_first, gate_second, hyena_value, short_taps, long_taps, norm_gain, queries, attn_keys):
    rows, chans = residual.shape
    heads = chans // HD
    count = 32
    width = chans * 16

    core = lax.axis_index("c")
    side = lax.axis_index("zh")
    group = side * 16 + lax.axis_index("s") * 8 + core
    head = lax.axis_index("h")
    owners = [head ^ flip for flip in range(heads)]
    place = [core, 1 - core] + [group + owner * 2 for owner in range(heads)]
    place = (jnp.stack(place + [side * 8, (1 - side) * 8] + owners) * rows).astype(jnp.int32)

    last, blocks = pack(gate_first, hyena_value, gate_second, attn_keys)
    keys_near = exchange(blocks.reshape(8, rows, HD), ("s", "h"))
    halo = lax.ppermute(last, ROWS_AXES, [(source, source + 1) for source in range(count - 1)])
    early_parts = early(last, gate_second, residual, short_taps, long_taps)
    stream, squares = late(halo, *early_parts)

    keys_near, squares = lax.optimization_barrier((keys_near, squares))
    gathered = exchange(squares, CHAN_AXES)
    keys_far = lax.ppermute(keys_near, "zh", [(0, 1)])
    packed = normalize(width, gathered, stream, norm_gain.reshape(1, chans))
    heads_of_q = [lax.dynamic_slice_in_dim(queries, owner * HD, HD, 1) for owner in owners]
    packed, keys_far, heads_of_q = lax.optimization_barrier((packed, keys_far, heads_of_q))
    for flip in range(1, heads):
        pairs = [(source, source ^ flip) for source in range(heads)]
        heads_of_q[flip] = lax.ppermute(heads_of_q[flip], "h", pairs)
    values_own = exchange(packed.reshape(16, rows, HD), PEERS)

    parts = [keys_near, swap_cores(keys_near), keys_far, swap_cores(keys_far)]
    weights, denom = score(place, heads_of_q, [part.reshape(8 * rows, HD) for part in parts])
    values_own, denom = lax.optimization_barrier((values_own, denom))
    values_other = swap_cores(values_own)
    result = attend(0, weights, values_own.reshape(16 * rows, HD))
    result = attend(1, weights, denom, result, values_other.reshape(16 * rows, HD))
    attended = exchange(result.reshape(heads, rows, HD), "h").transpose(1, 0, 2).reshape(rows, chans)
    return stream, attended


def solution(mesh):
    inner = Mesh(mesh.devices.reshape(2, 2, 4, 2, 4, 4), ROWS_AXES + CHAN_AXES)
    both = P(ROWS_AXES, CHAN_AXES)
    return jax.shard_map(
        shards,
        mesh=inner,
        in_specs=(both, both, both, both, P(None, None, CHAN_AXES), P(None, CHAN_AXES), P(CHAN_AXES), both, both),
        out_specs=(both, both),
        check_vma=False,
    )
```

```python
import functools
import math

import jax
import jax.numpy as jnp
from jax import lax
from jax.experimental import pallas as pl
from jax.experimental.pallas import tpu as pltpu
from jax.sharding import Mesh, PartitionSpec as P

HD = 128
ROWS_AXES = ("zh", "s", "h", "c")
CHAN_AXES = ("x", "zl")
PEERS = ("zh", "s", "h")
HIGHEST = lax.Precision.HIGHEST


def shift_copies(prod, copies):
    length = prod.shape[0]
    for lag in range(8):
        copies[lag, 8:length, :] = prod[8 - lag : length - lag, :]


def lag_sums(weights, copies, base, pairs):
    totals = {}
    for group in range(weights.shape[0] // 8):
        wanted = [tile for tile, other in pairs if other == group]
        rows = weights[group * 8 : group * 8 + 8, :].astype(jnp.float32)
        for lag in range(8):
            weight = jnp.broadcast_to(rows[lag : lag + 1, :], rows.shape)
            for tile in wanted:
                begin = base + 8 * (tile - group)
                term = weight * copies[lag, begin : begin + 8, :]
                totals[tile] = totals[tile] + term if tile in totals else term
    return [totals[tile] for tile in sorted(totals)]


def featurize(taps, index, ext, begin, count):
    total = taps[index, 0:1, :] * ext[begin : begin + count, :]
    total = total + taps[index, 1:2, :] * ext[begin - 1 : begin - 1 + count, :]
    return total + taps[index, 2:3, :] * ext[begin - 2 : begin - 2 + count, :]


def head_lanes(head):
    return pl.ds(pl.multiple_of(head * HD, HD), HD)


def early_kernel(
    packed, gs, res, taps_in, long_in, keys, queries, partial, feat, res_out, edge, taps_out, long_out, blocks,
    gs_v, ext, prod, copies, sems,
):
    rows, chans = gs.shape
    loads = [(taps_in, taps_out), (long_in, long_out), (gs, gs_v), (res, res_out)]
    moves = [pltpu.make_async_copy(src, dst, sems.at[i]) for i, (src, dst) in enumerate(loads)]
    first = len(moves)
    for copy in range(blocks.shape[0]):
        for head in range(blocks.shape[1]):
            for kind, source in enumerate((keys, queries)):
                src = source.at[:, head * HD : (head + 1) * HD]
                dst = blocks.at[copy, head, kind]
                moves.append(pltpu.make_async_copy(src, dst, sems.at[len(moves)]))
    for move in moves:
        move.start()
    for move in moves[:first]:
        move.wait()
    tiles = rows // 8
    pairs = [(tile, group) for group in range(long_in.shape[0] // 8) for tile in range(group, tiles)]
    top = lax.broadcasted_iota(jnp.int32, (rows, HD), 0) < 2
    ext[0:8, :] = jnp.zeros((8, HD), jnp.float32)
    prod[0:8, :] = jnp.zeros((8, HD), jnp.float32)

    def one_head(head, carry):
        lanes = head_lanes(head)
        taps = taps_out[:, :, lanes]

        def feature(index, raw):
            wide = raw.astype(jnp.float32)
            ext[8:, :] = wide
            edge[index, :, lanes] = wide[0:8, :]
            return featurize(taps, index, ext, 8, rows)

        first = feature(0, packed[0:rows, lanes])
        product = (first * feature(2, packed[rows : 2 * rows, lanes])).astype(jnp.bfloat16).astype(jnp.float32)
        feat[:, lanes] = feature(1, gs_v[:, lanes])
        prod[8:, :] = jnp.where(top, 0.0, product)
        shift_copies(prod, copies)
        totals = lag_sums(long_out[:, lanes], copies, 8, pairs)
        partial[:, lanes] = jnp.concatenate(totals, axis=0)
        return carry

    lax.fori_loop(0, chans // HD, one_head, 0)
    for move in moves[first:]:
        move.wait()


def in_hbm(*arrays):
    return [pltpu.with_memory_space_constraint(array, pltpu.HBM) for array in arrays]


def early(packed, gs, res, taps, long_taps, keys, queries):
    rows, chans = gs.shape
    heads = chans // HD
    hbm = pl.BlockSpec(memory_space=pltpu.HBM)
    vmem = pl.BlockSpec(memory_space=pltpu.VMEM)
    return pl.pallas_call(
        early_kernel,
        in_specs=[vmem] + [hbm] * 6,
        out_specs=[vmem] * 7,
        out_shape=[
            jax.ShapeDtypeStruct((rows, chans), jnp.float32),
            jax.ShapeDtypeStruct((rows, chans), jnp.float32),
            jax.ShapeDtypeStruct((rows, chans), jnp.bfloat16),
            jax.ShapeDtypeStruct((3, 8, chans), jnp.float32),
            jax.ShapeDtypeStruct(taps.shape, jnp.float32),
            jax.ShapeDtypeStruct(long_taps.shape, jnp.bfloat16),
            jax.ShapeDtypeStruct((2, heads, 2, rows, HD), jnp.bfloat16),
        ],
        scratch_shapes=[
            pltpu.VMEM((rows, chans), jnp.bfloat16),
            pltpu.VMEM((rows + 8, HD), jnp.float32),
            pltpu.VMEM((rows + 8, HD), jnp.float32),
            pltpu.VMEM((8, rows + 8, HD), jnp.float32),
            pltpu.SemaphoreType.DMA((4 + 4 * heads,)),
        ],
        compiler_params=pltpu.CompilerParams(vmem_limit_bytes=32 << 20),
        cost_estimate=pl.CostEstimate(flops=6_000_000_000, bytes_accessed=2_000_000, transcendentals=0),
        name="early",
    )(packed, *in_hbm(gs, res, taps, long_taps, keys, queries))


def late_kernel(halo, partial, feat, res, edge, taps_in, long_in, stream, squares, ext, prod, copies):
    rows, chans = res.shape
    tiles = rows // 8
    pairs = [(tile, group) for group in range(long_in.shape[0] // 8) for tile in range(min(group + 2, tiles))]
    inside = lax.broadcasted_iota(jnp.int32, (rows, HD), 0) < rows - 6
    prod[0:8, :] = jnp.zeros((8, HD), jnp.float32)
    prod[rows + 8 :, :] = jnp.zeros((8, HD), jnp.float32)
    total = jnp.zeros((8, rows), jnp.float32)

    def one_head(head, total):
        lanes = head_lanes(head)
        taps = taps_in[:, :, lanes]

        def feature(index, begin):
            ext[0:rows, :] = halo[begin : begin + rows, lanes].astype(jnp.float32)
            ext[rows : rows + 8, :] = edge[index, :, lanes]
            return featurize(taps, index, ext, 8, rows)

        first = feature(0, 0)
        product = (first * feature(2, rows)).astype(jnp.bfloat16).astype(jnp.float32)
        prod[8 : rows + 8, :] = jnp.where(inside, product, 0.0)
        shift_copies(prod, copies)
        totals = lag_sums(long_in[:, lanes], copies, rows, pairs)
        filtered = partial[:, lanes] + jnp.concatenate(totals, axis=0)
        ext[0:8, :] = halo[2 * rows : 2 * rows + 8, lanes].astype(jnp.float32)
        ext[8:16, :] = edge[1, :, lanes]
        gate = jnp.concatenate([featurize(taps, 1, ext, 8, 8), feat[8:, lanes]], axis=0)
        out = (res[:, lanes].astype(jnp.float32) + gate * filtered).astype(jnp.bfloat16)
        stream[:, lanes] = out
        wide = out.astype(jnp.float32)
        total = total + lax.dot_general(
            jnp.ones((8, HD), jnp.float32),
            wide * wide,
            (((1,), (1,)), ((), ())),
            precision=HIGHEST,
            preferred_element_type=jnp.float32,
        )
        return total

    total = lax.fori_loop(0, chans // HD, one_head, total)
    squares[...] = total


def late(halo, partial, feat, res, edge, taps, long_taps):
    rows, chans = res.shape
    vmem = pl.BlockSpec(memory_space=pltpu.VMEM)
    return pl.pallas_call(
        late_kernel,
        in_specs=[vmem] * 7,
        out_specs=[vmem] * 2,
        out_shape=[
            jax.ShapeDtypeStruct((rows, chans), jnp.bfloat16),
            jax.ShapeDtypeStruct((8, rows), jnp.float32),
        ],
        scratch_shapes=[
            pltpu.VMEM((rows + 8, HD), jnp.float32),
            pltpu.VMEM((rows + 16, HD), jnp.float32),
            pltpu.VMEM((8, rows + 16, HD), jnp.float32),
        ],
        compiler_params=pltpu.CompilerParams(vmem_limit_bytes=32 << 20),
        cost_estimate=pl.CostEstimate(flops=30_000_000_000, bytes_accessed=2_000_000, transcendentals=0),
        name="late",
    )(halo, partial, feat, res, edge, taps, long_taps)


def pack_kernel(gf, hv, gs, halo, sems):
    rows = gf.shape[0]
    pairs = [
        (gf, halo.at[0:rows]),
        (hv, halo.at[rows : 2 * rows]),
        (gs.at[rows - 8 : rows], halo.at[2 * rows : 2 * rows + 8]),
    ]
    moves = [pltpu.make_async_copy(src, dst, sems.at[i]) for i, (src, dst) in enumerate(pairs)]
    for move in moves:
        move.start()
    for move in moves:
        move.wait()


def pack(gf, hv, gs):
    rows, chans = gf.shape
    return pl.pallas_call(
        pack_kernel,
        in_specs=[pl.BlockSpec(memory_space=pltpu.HBM)] * 3,
        out_specs=pl.BlockSpec(memory_space=pltpu.VMEM),
        out_shape=jax.ShapeDtypeStruct((2 * rows + 8, chans), jnp.bfloat16),
        scratch_shapes=[pltpu.SemaphoreType.DMA((3,))],
        compiler_params=pltpu.CompilerParams(vmem_limit_bytes=16 << 20),
        cost_estimate=pl.CostEstimate(flops=0, bytes_accessed=600_000, transcendentals=0),
        name="pack",
    )(*in_hbm(gf, hv, gs))


def normalize_kernel(width, part0, part1, part2, part3, stream, gain, packed):
    total = part0[...] + part1[...] + part2[...] + part3[...]
    total = lax.dot_general(
        jnp.where(lax.broadcasted_iota(jnp.int32, total.shape, 0) == 0, total, 0.0),
        jnp.ones((8, HD), jnp.float32),
        (((0,), (0,)), ((), ())),
        precision=HIGHEST,
        preferred_element_type=jnp.float32,
    )
    inverse = 1.0 / jnp.sqrt(total / width + 1e-06)
    for head in range(packed.shape[1]):
        lanes = slice(head * HD, (head + 1) * HD)
        value = stream[:, lanes].astype(jnp.float32) * inverse * gain[:, lanes]
        value = value.astype(jnp.bfloat16)
        for copy in range(packed.shape[0]):
            packed[copy, head] = value


def normalize(width, parts, stream, gain):
    rows, chans = stream.shape
    vmem = pl.BlockSpec(memory_space=pltpu.VMEM)
    return pl.pallas_call(
        functools.partial(normalize_kernel, width),
        in_specs=[vmem] * 6,
        out_specs=vmem,
        out_shape=jax.ShapeDtypeStruct((4, chans // HD, rows, HD), jnp.bfloat16),
        compiler_params=pltpu.CompilerParams(vmem_limit_bytes=8 << 20),
        cost_estimate=pl.CostEstimate(flops=1_000_000, bytes_accessed=800_000, transcendentals=20_000),
        name="normalize",
    )(*parts, *in_hbm(stream), gain)


def score_kernel(place, q, k0, k1, k2, k3, out, denom, keys, scores, weights, sems):
    rows = keys.shape[1] // 16
    count = keys.shape[1]
    block = scores.shape[0]
    unit = math.log2(math.e) / math.sqrt(HD)
    for part, ref in enumerate((k0, k1, k2, k3)):
        begin = pl.multiple_of(place[6 + part // 2], 64)
        keys[part % 2, pl.ds(begin, count // 2), :] = ref[...]
    chunks = [(begin, min(256, count - begin)) for begin in range(0, count, 256)]
    line = lax.broadcasted_iota(jnp.int32, (block, 1), 0)
    for index in range(q.shape[0] // block):
        query = q[index * block : (index + 1) * block, :]
        query_pos = line + place[2 + index * (block // rows)]
        for step in range(1, block // rows):
            moved = place[2 + index * (block // rows) + step] - step * rows
            query_pos = jnp.where(line >= step * rows, line + moved, query_pos)
        top = None
        for part in range(2):
            for begin, width in chunks:
                score = lax.dot_general(
                    query,
                    keys[part, begin : begin + width, :],
                    (((1,), (1,)), ((), ())),
                    preferred_element_type=jnp.float32,
                )
                lane = begin + lax.broadcasted_iota(jnp.int32, (1, width), 1)
                key_pos = place[part] + lane
                for edge in range(rows, count, rows):
                    if edge < begin + width:
                        key_pos = key_pos + jnp.where(lane >= edge, rows, 0)
                score = jnp.where(key_pos <= query_pos, score * unit, -1e30)
                scores[:, part * count + begin : part * count + begin + width] = score
                for piece in range(0, width, 128):
                    piece = score[:, piece : piece + 128]
                    top = piece if top is None else jnp.maximum(top, piece)
        top = jnp.max(top, axis=1, keepdims=True)
        total = jnp.zeros((block, 128), jnp.float32)
        for begin in range(0, 2 * count, 128):
            expo = jnp.exp2(scores[:, begin : begin + 128] - top)
            total = total + expo
            weights[index * block : (index + 1) * block, begin : begin + 128] = expo.astype(jnp.bfloat16)
        total = jnp.sum(total, axis=1, keepdims=True)
        denom[index * block : (index + 1) * block, :] = jnp.broadcast_to(total, (block, 128))
        lines = pl.ds(index * block, block)
        pltpu.make_async_copy(weights.at[lines], out.at[lines], sems.at[index]).start()
    for index in range(q.shape[0] // block):
        lines = pl.ds(index * block, block)
        pltpu.make_async_copy(weights.at[lines], out.at[lines], sems.at[index]).wait()


def score(place, q, keys):
    lines = q.shape[0]
    count = sum(part.shape[0] for part in keys)
    block = lines // 2
    vmem = pl.BlockSpec(memory_space=pltpu.VMEM)
    return pl.pallas_call(
        score_kernel,
        in_specs=[pl.BlockSpec(memory_space=pltpu.SMEM)] + [vmem] * 5,
        out_specs=[pl.BlockSpec(memory_space=pltpu.HBM), vmem],
        out_shape=[
            pltpu.HBM((lines, count), jnp.bfloat16),
            jax.ShapeDtypeStruct((lines, 128), jnp.float32),
        ],
        scratch_shapes=[
            pltpu.VMEM((2, count // 2, HD), jnp.bfloat16),
            pltpu.VMEM((block, count), jnp.float32),
            pltpu.VMEM((lines, count), jnp.bfloat16),
            pltpu.SemaphoreType.DMA((2,)),
        ],
        compiler_params=pltpu.CompilerParams(vmem_limit_bytes=32 << 20),
        cost_estimate=pl.CostEstimate(
            flops=2 * lines * count * HD, bytes_accessed=8_000_000, transcendentals=lines * count
        ),
        name="score",
    )(place, q, *keys)


def attend_own_kernel(weights_in, values, out, later, weights, sems):
    keys = values.shape[0]
    cuts = [0, 640, 1152, 1664, keys]
    moves = []
    for half, target in enumerate((weights, later)):
        for begin, end in zip(cuts, cuts[1:]):
            src = weights_in.at[:, half * keys + begin : half * keys + end]
            moves.append(pltpu.make_async_copy(src, target.at[:, begin:end], sems.at[len(moves)]))
    for move in moves[:3]:
        move.start()
    total = jnp.zeros(out.shape, jnp.float32)
    for index, (begin, end) in enumerate(zip(cuts, cuts[1:])):
        moves[index].wait()
        for move in moves[3 + 2 * index : min(5 + 2 * index, len(moves))]:
            move.start()
        total = total + jnp.dot(
            weights[:, begin:end], values[begin:end, :], preferred_element_type=jnp.float32
        )
    out[...] = total
    for move in moves[4:]:
        move.wait()


def attend_other_kernel(weights, denom, before, values, out):
    total = before[...] + jnp.dot(weights[...], values[...], preferred_element_type=jnp.float32)
    out[...] = (total / denom[...]).astype(jnp.bfloat16)


def attend_own(weights, values):
    lines, count = weights.shape
    keys = count // 2
    vmem = pl.BlockSpec(memory_space=pltpu.VMEM)
    return pl.pallas_call(
        attend_own_kernel,
        in_specs=[pl.BlockSpec(memory_space=pltpu.HBM), vmem],
        out_specs=[vmem, vmem],
        out_shape=[
            jax.ShapeDtypeStruct((lines, HD), jnp.float32),
            jax.ShapeDtypeStruct((lines, keys), jnp.bfloat16),
        ],
        scratch_shapes=[pltpu.VMEM((lines, keys), jnp.bfloat16), pltpu.SemaphoreType.DMA((8,))],
        compiler_params=pltpu.CompilerParams(vmem_limit_bytes=16 << 20),
        cost_estimate=pl.CostEstimate(
            flops=2 * lines * keys * HD, bytes_accessed=5_500_000, transcendentals=0
        ),
        name="attend_own",
    )(*in_hbm(weights), values)


def attend_other(weights, denom, before, values):
    lines, keys = weights.shape
    vmem = pl.BlockSpec(memory_space=pltpu.VMEM)
    return pl.pallas_call(
        attend_other_kernel,
        in_specs=[vmem] * 4,
        out_specs=vmem,
        out_shape=jax.ShapeDtypeStruct((lines, HD), jnp.bfloat16),
        compiler_params=pltpu.CompilerParams(vmem_limit_bytes=16 << 20),
        cost_estimate=pl.CostEstimate(
            flops=2 * lines * keys * HD, bytes_accessed=3_500_000, transcendentals=0
        ),
        name="attend_other",
    )(weights, denom, before, values)


def exchange(value, axes):
    return lax.all_to_all(value, axes, 0, 0, tiled=True)


def three_others(value, axis):
    return [
        lax.ppermute(value, axis, [(source, source ^ flip) for source in range(4)]) for flip in range(1, 4)
    ]


def swap_cores(value):
    return lax.ppermute(value, "c", [(0, 1), (1, 0)])


def shards(residual, gate_first, gate_second, hyena_value, short_taps, long_taps, norm_gain, queries, attn_keys):
    rows, chans = residual.shape
    heads = chans // HD
    count = 32
    width = chans * 16

    core = lax.axis_index("c")
    side = lax.axis_index("zh")
    group = side * 16 + lax.axis_index("s") * 8 + core
    place = [core, 1 - core] + [group + owner * 2 for owner in range(heads)]
    place = (jnp.stack(place + [side * 8, (1 - side) * 8]) * rows).astype(jnp.int32)

    last = pack(gate_first, hyena_value, gate_second)
    halo = lax.ppermute(last, ROWS_AXES, [(source, source + 1) for source in range(count - 1)])
    *early_parts, blocks = early(
        last, gate_second, residual, short_taps, long_taps, attn_keys, queries
    )
    blocks = exchange(blocks.reshape(8, 2, rows, HD), ("s", "h"))
    stream, squares = late(halo, *early_parts)
    squares = sum(three_others(squares, "x"), squares)
    parts = [squares] + three_others(squares, "zl")
    packed = normalize(width, parts, stream, norm_gain.reshape(1, chans))
    values_own = exchange(packed.reshape(16, rows, HD), PEERS)

    keys_near = blocks[:, 0]
    my_queries = lax.dynamic_slice_in_dim(blocks, lax.axis_index("s") * heads, heads, 0)[:, 1]
    keys_far = lax.ppermute(keys_near, "zh", [(0, 1)])
    parts = [keys_near, swap_cores(keys_near), keys_far, swap_cores(keys_far)]
    weights, denom = score(
        place, my_queries.reshape(heads * rows, HD), [part.reshape(8 * rows, HD) for part in parts]
    )
    values_own, denom = lax.optimization_barrier((values_own, denom))
    values_other = swap_cores(values_own)
    result, weights_other = attend_own(weights, values_own.reshape(16 * rows, HD))
    result = attend_other(weights_other, denom, result, values_other.reshape(16 * rows, HD))
    attended = exchange(result.reshape(heads, rows, HD), "h").transpose(1, 0, 2).reshape(rows, chans)
    return stream, attended


def solution(mesh):
    inner = Mesh(mesh.devices.reshape(2, 2, 4, 2, 4, 4), ROWS_AXES + CHAN_AXES)
    both = P(ROWS_AXES, CHAN_AXES)
    return jax.shard_map(
        shards,
        mesh=inner,
        in_specs=(both, both, both, both, P(None, None, CHAN_AXES), P(None, CHAN_AXES), P(CHAN_AXES), both, both),
        out_specs=(both, both),
        check_vma=False,
    )
```

```python
import functools
import math

import jax
import jax.numpy as jnp
from jax import lax
from jax.experimental import pallas as pl
from jax.experimental.pallas import tpu as pltpu
from jax.sharding import Mesh, PartitionSpec as P

HD = 128
ROWS_AXES = ("zh", "s", "h", "c")
CHAN_AXES = ("x", "zl")
PEERS = ("zh", "s", "h")
HIGHEST = lax.Precision.HIGHEST


def shift_copies(prod, copies):
    length = prod.shape[0]
    for lag in range(8):
        copies[lag, 8:length, :] = prod[8 - lag : length - lag, :]


def lag_sums(weights, copies, base, pairs):
    totals = {}
    for group in range(weights.shape[0] // 8):
        wanted = [tile for tile, other in pairs if other == group]
        rows = weights[group * 8 : group * 8 + 8, :].astype(jnp.float32)
        for lag in range(8):
            weight = jnp.broadcast_to(rows[lag : lag + 1, :], rows.shape)
            for tile in wanted:
                begin = base + 8 * (tile - group)
                term = weight * copies[lag, begin : begin + 8, :]
                totals[tile] = totals[tile] + term if tile in totals else term
    return [totals[tile] for tile in sorted(totals)]


def featurize(taps, index, ext, begin, count):
    total = taps[index, 0:1, :] * ext[begin : begin + count, :]
    total = total + taps[index, 1:2, :] * ext[begin - 1 : begin - 1 + count, :]
    return total + taps[index, 2:3, :] * ext[begin - 2 : begin - 2 + count, :]


def head_lanes(head):
    return pl.ds(pl.multiple_of(head * HD, HD), HD)


def early_kernel(
    packed, gs, res, taps_in, long_in, partial, feat, res_out, edge, taps_out, long_out,
    gs_v, ext, prod, copies, sems,
):
    rows, chans = gs.shape
    loads = [(taps_in, taps_out), (long_in, long_out), (gs, gs_v), (res, res_out)]
    moves = [pltpu.make_async_copy(src, dst, sems.at[i]) for i, (src, dst) in enumerate(loads)]
    for move in moves:
        move.start()
    for move in moves:
        move.wait()
    tiles = rows // 8
    pairs = [(tile, group) for group in range(long_in.shape[0] // 8) for tile in range(group, tiles)]
    top = lax.broadcasted_iota(jnp.int32, (rows, HD), 0) < 2
    ext[0:8, :] = jnp.zeros((8, HD), jnp.float32)
    prod[0:8, :] = jnp.zeros((8, HD), jnp.float32)

    def one_head(head, carry):
        lanes = head_lanes(head)
        taps = taps_out[:, :, lanes]

        def feature(index, raw):
            wide = raw.astype(jnp.float32)
            ext[8:, :] = wide
            edge[index, :, lanes] = wide[0:8, :]
            return featurize(taps, index, ext, 8, rows)

        first = feature(0, packed[0:rows, lanes])
        product = (first * feature(2, packed[rows : 2 * rows, lanes])).astype(jnp.bfloat16).astype(jnp.float32)
        feat[:, lanes] = feature(1, gs_v[:, lanes])
        prod[8:, :] = jnp.where(top, 0.0, product)
        shift_copies(prod, copies)
        totals = lag_sums(long_out[:, lanes], copies, 8, pairs)
        partial[:, lanes] = jnp.concatenate(totals, axis=0)
        return carry

    lax.fori_loop(0, chans // HD, one_head, 0)


def in_hbm(*arrays):
    return [pltpu.with_memory_space_constraint(array, pltpu.HBM) for array in arrays]


def early(packed, gs, res, taps, long_taps):
    rows, chans = gs.shape
    hbm = pl.BlockSpec(memory_space=pltpu.HBM)
    vmem = pl.BlockSpec(memory_space=pltpu.VMEM)
    return pl.pallas_call(
        early_kernel,
        in_specs=[vmem] + [hbm] * 4,
        out_specs=[vmem] * 6,
        out_shape=[
            jax.ShapeDtypeStruct((rows, chans), jnp.float32),
            jax.ShapeDtypeStruct((rows, chans), jnp.float32),
            jax.ShapeDtypeStruct((rows, chans), jnp.bfloat16),
            jax.ShapeDtypeStruct((3, 8, chans), jnp.float32),
            jax.ShapeDtypeStruct(taps.shape, jnp.float32),
            jax.ShapeDtypeStruct(long_taps.shape, jnp.bfloat16),
        ],
        scratch_shapes=[
            pltpu.VMEM((rows, chans), jnp.bfloat16),
            pltpu.VMEM((rows + 8, HD), jnp.float32),
            pltpu.VMEM((rows + 8, HD), jnp.float32),
            pltpu.VMEM((8, rows + 8, HD), jnp.float32),
            pltpu.SemaphoreType.DMA((4,)),
        ],
        compiler_params=pltpu.CompilerParams(vmem_limit_bytes=32 << 20),
        cost_estimate=pl.CostEstimate(flops=20_000_000, bytes_accessed=2_000_000, transcendentals=0),
        name="early",
    )(packed, *in_hbm(gs, res, taps, long_taps))


def late_kernel(halo, partial, feat, res, edge, taps_in, long_in, stream, squares, ext, prod, copies):
    rows, chans = res.shape
    tiles = rows // 8
    pairs = [(tile, group) for group in range(long_in.shape[0] // 8) for tile in range(min(group + 2, tiles))]
    inside = lax.broadcasted_iota(jnp.int32, (rows, HD), 0) < rows - 6
    prod[0:8, :] = jnp.zeros((8, HD), jnp.float32)
    prod[rows + 8 :, :] = jnp.zeros((8, HD), jnp.float32)
    total = jnp.zeros((8, rows), jnp.float32)

    def one_head(head, total):
        lanes = head_lanes(head)
        taps = taps_in[:, :, lanes]

        def feature(index, begin):
            ext[0:rows, :] = halo[begin : begin + rows, lanes].astype(jnp.float32)
            ext[rows : rows + 8, :] = edge[index, :, lanes]
            return featurize(taps, index, ext, 8, rows)

        first = feature(0, 0)
        product = (first * feature(2, rows)).astype(jnp.bfloat16).astype(jnp.float32)
        prod[8 : rows + 8, :] = jnp.where(inside, product, 0.0)
        shift_copies(prod, copies)
        totals = lag_sums(long_in[:, lanes], copies, rows, pairs)
        filtered = partial[:, lanes] + jnp.concatenate(totals, axis=0)
        ext[0:8, :] = halo[2 * rows : 2 * rows + 8, lanes].astype(jnp.float32)
        ext[8:16, :] = edge[1, :, lanes]
        gate = jnp.concatenate([featurize(taps, 1, ext, 8, 8), feat[8:, lanes]], axis=0)
        out = (res[:, lanes].astype(jnp.float32) + gate * filtered).astype(jnp.bfloat16)
        stream[:, lanes] = out
        wide = out.astype(jnp.float32)
        total = total + lax.dot_general(
            jnp.ones((8, HD), jnp.float32),
            wide * wide,
            (((1,), (1,)), ((), ())),
            precision=HIGHEST,
            preferred_element_type=jnp.float32,
        )
        return total

    total = lax.fori_loop(0, chans // HD, one_head, total)
    for peer in range(squares.shape[0]):
        squares[peer] = total[0:1, :]


def late(halo, partial, feat, res, edge, taps, long_taps):
    rows, chans = res.shape
    vmem = pl.BlockSpec(memory_space=pltpu.VMEM)
    return pl.pallas_call(
        late_kernel,
        in_specs=[vmem] * 7,
        out_specs=[vmem] * 2,
        out_shape=[
            jax.ShapeDtypeStruct((rows, chans), jnp.bfloat16),
            jax.ShapeDtypeStruct((16, 1, rows), jnp.float32),
        ],
        scratch_shapes=[
            pltpu.VMEM((rows + 8, HD), jnp.float32),
            pltpu.VMEM((rows + 16, HD), jnp.float32),
            pltpu.VMEM((8, rows + 16, HD), jnp.float32),
        ],
        compiler_params=pltpu.CompilerParams(vmem_limit_bytes=32 << 20),
        cost_estimate=pl.CostEstimate(flops=30_000_000_000, bytes_accessed=2_000_000, transcendentals=0),
        name="late",
    )(halo, partial, feat, res, edge, taps, long_taps)


def pack_kernel(gf, hv, gs, keys, queries, halo, blocks, whole, sems):
    rows = gf.shape[0]
    pairs = [
        (keys, whole.at[0]),
        (queries, whole.at[1]),
        (gf, halo.at[0:rows]),
        (hv, halo.at[rows : 2 * rows]),
        (gs.at[rows - 8 : rows], halo.at[2 * rows : 2 * rows + 8]),
    ]
    for kind in range(2):
        for copy in range(blocks.shape[0]):
            for head in range(blocks.shape[1]):
                src = whole.at[kind, :, head * HD : (head + 1) * HD]
                pairs.append((src, blocks.at[copy, head, kind]))
    moves = [pltpu.make_async_copy(src, dst, sems.at[i]) for i, (src, dst) in enumerate(pairs)]
    half = (len(moves) - 5) // 2
    for move in moves[:5]:
        move.start()
    moves[0].wait()
    for move in moves[5 : 5 + half]:
        move.start()
    moves[1].wait()
    for move in moves[5 + half :]:
        move.start()
    for move in moves[2:]:
        move.wait()


def pack(gf, hv, gs, keys, queries):
    rows, chans = gf.shape
    heads = chans // HD
    vmem = pl.BlockSpec(memory_space=pltpu.VMEM)
    hbm = pl.BlockSpec(memory_space=pltpu.HBM)
    return pl.pallas_call(
        pack_kernel,
        in_specs=[hbm] * 5,
        out_specs=[vmem, hbm],
        out_shape=[
            jax.ShapeDtypeStruct((2 * rows + 8, chans), jnp.bfloat16),
            pltpu.HBM((2, heads, 2, rows, HD), jnp.bfloat16),
        ],
        scratch_shapes=[pltpu.VMEM((2, rows, chans), jnp.bfloat16), pltpu.SemaphoreType.DMA((4 * heads + 5,))],
        compiler_params=pltpu.CompilerParams(vmem_limit_bytes=16 << 20),
        cost_estimate=pl.CostEstimate(flops=0, bytes_accessed=600_000, transcendentals=0),
        name="pack",
    )(*in_hbm(gf, hv, gs, keys, queries))


def normalize_kernel(width, gathered, stream, gain, packed):
    total = gathered[0]
    for peer in range(1, gathered.shape[0]):
        total = total + gathered[peer]
    total = jnp.broadcast_to(total, (8, total.shape[1]))
    total = lax.dot_general(
        jnp.where(lax.broadcasted_iota(jnp.int32, total.shape, 0) == 0, total, 0.0),
        jnp.ones((8, HD), jnp.float32),
        (((0,), (0,)), ((), ())),
        precision=HIGHEST,
        preferred_element_type=jnp.float32,
    )
    inverse = 1.0 / jnp.sqrt(total / width + 1e-06)
    for head in range(packed.shape[1]):
        lanes = slice(head * HD, (head + 1) * HD)
        value = stream[:, lanes].astype(jnp.float32) * inverse * gain[:, lanes]
        value = value.astype(jnp.bfloat16)
        for copy in range(packed.shape[0]):
            packed[copy, head] = value


def normalize(width, gathered, stream, gain):
    rows, chans = stream.shape
    vmem = pl.BlockSpec(memory_space=pltpu.VMEM)
    return pl.pallas_call(
        functools.partial(normalize_kernel, width),
        in_specs=[vmem] * 3,
        out_specs=vmem,
        out_shape=jax.ShapeDtypeStruct((4, chans // HD, rows, HD), jnp.bfloat16),
        compiler_params=pltpu.CompilerParams(vmem_limit_bytes=8 << 20),
        cost_estimate=pl.CostEstimate(flops=1_000_000, bytes_accessed=800_000, transcendentals=20_000),
        name="normalize",
    )(gathered, *in_hbm(stream), gain)


def score_kernel(place, q, k0, k1, k2, k3, out, denom, keys, scores, weights, sems):
    rows = keys.shape[1] // 16
    count = keys.shape[1]
    block = scores.shape[0]
    unit = math.log2(math.e) / math.sqrt(HD)
    for part, ref in enumerate((k0, k1, k2, k3)):
        begin = pl.multiple_of(place[6 + part // 2], 64)
        keys[part % 2, pl.ds(begin, count // 2), :] = ref[...]
    chunks = [(begin, min(256, count - begin)) for begin in range(0, count, 256)]
    line = lax.broadcasted_iota(jnp.int32, (block, 1), 0)
    for index in range(q.shape[0] // block):
        query = q[index * block : (index + 1) * block, :]
        query_pos = line + place[2 + index * (block // rows)]
        for step in range(1, block // rows):
            moved = place[2 + index * (block // rows) + step] - step * rows
            query_pos = jnp.where(line >= step * rows, line + moved, query_pos)
        top = None
        for part in range(2):
            for begin, width in chunks:
                score = lax.dot_general(
                    query,
                    keys[part, begin : begin + width, :],
                    (((1,), (1,)), ((), ())),
                    preferred_element_type=jnp.float32,
                )
                lane = begin + lax.broadcasted_iota(jnp.int32, (1, width), 1)
                key_pos = place[part] + lane
                for edge in range(rows, count, rows):
                    if edge < begin + width:
                        key_pos = key_pos + jnp.where(lane >= edge, rows, 0)
                score = jnp.where(key_pos <= query_pos, score * unit, -1e30)
                scores[:, part * count + begin : part * count + begin + width] = score
                for piece in range(0, width, 128):
                    piece = score[:, piece : piece + 128]
                    top = piece if top is None else jnp.maximum(top, piece)
        top = jnp.max(top, axis=1, keepdims=True)
        total = jnp.zeros((block, 128), jnp.float32)
        for begin in range(0, 2 * count, 128):
            expo = jnp.exp2(scores[:, begin : begin + 128] - top)
            total = total + expo
            weights[index * block : (index + 1) * block, begin : begin + 128] = expo.astype(jnp.bfloat16)
        total = jnp.sum(total, axis=1, keepdims=True)
        denom[index * block : (index + 1) * block, :] = jnp.broadcast_to(total, (block, 128))
        lines = pl.ds(index * block, block)
        pltpu.make_async_copy(weights.at[lines], out.at[lines], sems.at[index]).start()
    for index in range(q.shape[0] // block):
        lines = pl.ds(index * block, block)
        pltpu.make_async_copy(weights.at[lines], out.at[lines], sems.at[index]).wait()


def score(place, q, keys):
    lines = q.shape[0]
    count = sum(part.shape[0] for part in keys)
    block = lines // 2
    vmem = pl.BlockSpec(memory_space=pltpu.VMEM)
    return pl.pallas_call(
        score_kernel,
        in_specs=[pl.BlockSpec(memory_space=pltpu.SMEM)] + [vmem] * 5,
        out_specs=[pl.BlockSpec(memory_space=pltpu.HBM), vmem],
        out_shape=[
            pltpu.HBM((lines, count), jnp.bfloat16),
            jax.ShapeDtypeStruct((lines, 128), jnp.float32),
        ],
        scratch_shapes=[
            pltpu.VMEM((2, count // 2, HD), jnp.bfloat16),
            pltpu.VMEM((block, count), jnp.float32),
            pltpu.VMEM((lines, count), jnp.bfloat16),
            pltpu.SemaphoreType.DMA((2,)),
        ],
        compiler_params=pltpu.CompilerParams(vmem_limit_bytes=32 << 20),
        cost_estimate=pl.CostEstimate(
            flops=2 * lines * count * HD, bytes_accessed=8_000_000, transcendentals=lines * count
        ),
        name="score",
    )(place, q, *keys)


def attend_own_kernel(weights_in, values, out, later, weights, sems):
    keys = values.shape[0]
    cuts = [0, 640, 1152, 1664, keys]
    moves = []
    for half, target in enumerate((weights, later)):
        for begin, end in zip(cuts, cuts[1:]):
            src = weights_in.at[:, half * keys + begin : half * keys + end]
            moves.append(pltpu.make_async_copy(src, target.at[:, begin:end], sems.at[len(moves)]))
    for move in moves[:3]:
        move.start()
    total = jnp.zeros(out.shape, jnp.float32)
    for index, (begin, end) in enumerate(zip(cuts, cuts[1:])):
        moves[index].wait()
        for move in moves[3 + 2 * index : min(5 + 2 * index, len(moves))]:
            move.start()
        total = total + jnp.dot(
            weights[:, begin:end], values[begin:end, :], preferred_element_type=jnp.float32
        )
    out[...] = total
    for move in moves[4:]:
        move.wait()


def attend_other_kernel(weights, denom, before, values, out):
    total = before[...] + jnp.dot(weights[...], values[...], preferred_element_type=jnp.float32)
    out[...] = (total / denom[...]).astype(jnp.bfloat16)


def attend_own(weights, values):
    lines, count = weights.shape
    keys = count // 2
    vmem = pl.BlockSpec(memory_space=pltpu.VMEM)
    return pl.pallas_call(
        attend_own_kernel,
        in_specs=[pl.BlockSpec(memory_space=pltpu.HBM), vmem],
        out_specs=[vmem, vmem],
        out_shape=[
            jax.ShapeDtypeStruct((lines, HD), jnp.float32),
            jax.ShapeDtypeStruct((lines, keys), jnp.bfloat16),
        ],
        scratch_shapes=[pltpu.VMEM((lines, keys), jnp.bfloat16), pltpu.SemaphoreType.DMA((8,))],
        compiler_params=pltpu.CompilerParams(vmem_limit_bytes=16 << 20),
        cost_estimate=pl.CostEstimate(
            flops=2 * lines * keys * HD, bytes_accessed=5_500_000, transcendentals=0
        ),
        name="attend_own",
    )(*in_hbm(weights), values)


def attend_other(weights, denom, before, values):
    lines, keys = weights.shape
    vmem = pl.BlockSpec(memory_space=pltpu.VMEM)
    return pl.pallas_call(
        attend_other_kernel,
        in_specs=[vmem] * 4,
        out_specs=vmem,
        out_shape=jax.ShapeDtypeStruct((lines, HD), jnp.bfloat16),
        compiler_params=pltpu.CompilerParams(vmem_limit_bytes=16 << 20),
        cost_estimate=pl.CostEstimate(
            flops=2 * lines * keys * HD, bytes_accessed=3_500_000, transcendentals=0
        ),
        name="attend_other",
    )(weights, denom, before, values)


def exchange(value, axes):
    return lax.all_to_all(value, axes, 0, 0, tiled=True)


def swap_cores(value):
    return lax.ppermute(value, "c", [(0, 1), (1, 0)])


def shards(residual, gate_first, gate_second, hyena_value, short_taps, long_taps, norm_gain, queries, attn_keys):
    rows, chans = residual.shape
    heads = chans // HD
    count = 32
    width = chans * 16

    core = lax.axis_index("c")
    side = lax.axis_index("zh")
    group = side * 16 + lax.axis_index("s") * 8 + core
    place = [core, 1 - core] + [group + owner * 2 for owner in range(heads)]
    place = (jnp.stack(place + [side * 8, (1 - side) * 8]) * rows).astype(jnp.int32)

    last, blocks = pack(gate_first, hyena_value, gate_second, attn_keys, queries)
    blocks = exchange(blocks.reshape(8, 2, rows, HD), ("s", "h"))
    halo = lax.ppermute(last, ROWS_AXES, [(source, source + 1) for source in range(count - 1)])
    early_parts = early(last, gate_second, residual, short_taps, long_taps)
    stream, squares = late(halo, *early_parts)

    blocks, squares = lax.optimization_barrier((blocks, squares))
    keys_near = blocks[:, 0]
    my_queries = lax.dynamic_slice_in_dim(blocks, lax.axis_index("s") * heads, heads, 0)[:, 1]
    keys_far = lax.ppermute(keys_near, "zh", [(0, 1)])
    gathered = exchange(squares, CHAN_AXES)
    packed = normalize(width, gathered, stream, norm_gain.reshape(1, chans))
    packed, keys_far = lax.optimization_barrier((packed, keys_far))
    values_own = exchange(packed.reshape(16, rows, HD), PEERS)

    parts = [keys_near, swap_cores(keys_near), keys_far, swap_cores(keys_far)]
    weights, denom = score(
        place, my_queries.reshape(heads * rows, HD), [part.reshape(8 * rows, HD) for part in parts]
    )
    values_own, denom = lax.optimization_barrier((values_own, denom))
    values_other = swap_cores(values_own)
    result, weights_other = attend_own(weights, values_own.reshape(16 * rows, HD))
    result = attend_other(weights_other, denom, result, values_other.reshape(16 * rows, HD))
    attended = exchange(result.reshape(heads, rows, HD), "h").transpose(1, 0, 2).reshape(rows, chans)
    return stream, attended


def solution(mesh):
    inner = Mesh(mesh.devices.reshape(2, 2, 4, 2, 4, 4), ROWS_AXES + CHAN_AXES)
    both = P(ROWS_AXES, CHAN_AXES)
    return jax.shard_map(
        shards,
        mesh=inner,
        in_specs=(both, both, both, both, P(None, None, CHAN_AXES), P(None, CHAN_AXES), P(CHAN_AXES), both, both),
        out_specs=(both, both),
        check_vma=False,
    )
```

```python
import functools
import math

import jax
import jax.numpy as jnp
from jax import lax
from jax.experimental import pallas as pl
from jax.experimental.pallas import tpu as pltpu
from jax.sharding import Mesh, PartitionSpec as P

HD = 128
ROWS_AXES = ("zh", "s", "h", "c")
CHAN_AXES = ("x", "zl")
HIGHEST = lax.Precision.HIGHEST


def shift_copies(prod, copies):
    length = prod.shape[0]
    for lag in range(8):
        copies[lag, 8:length, :] = prod[8 - lag : length - lag, :]


def lag_sums(weights, copies, base, pairs):
    totals = {}
    for group in range(weights.shape[0] // 8):
        wanted = [tile for tile, other in pairs if other == group]
        rows = weights[group * 8 : group * 8 + 8, :].astype(jnp.float32)
        for lag in range(8):
            weight = jnp.broadcast_to(rows[lag : lag + 1, :], rows.shape)
            for tile in wanted:
                begin = base + 8 * (tile - group)
                term = weight * copies[lag, begin : begin + 8, :]
                totals[tile] = totals[tile] + term if tile in totals else term
    return [totals[tile] for tile in sorted(totals)]


def featurize(taps, index, ext, begin, count):
    total = taps[index, 0:1, :] * ext[begin : begin + count, :]
    total = total + taps[index, 1:2, :] * ext[begin - 1 : begin - 1 + count, :]
    return total + taps[index, 2:3, :] * ext[begin - 2 : begin - 2 + count, :]


def head_lanes(head):
    return pl.ds(pl.multiple_of(head * HD, HD), HD)


def early_kernel(
    packed, gs, res, taps_in, long_in, partial, feat, res_out, edge, taps_out, long_out,
    gs_v, ext, prod, copies, sems,
):
    rows, chans = gs.shape
    loads = [(taps_in, taps_out), (long_in, long_out), (gs, gs_v), (res, res_out)]
    moves = [pltpu.make_async_copy(src, dst, sems.at[i]) for i, (src, dst) in enumerate(loads)]
    for move in moves:
        move.start()
    for move in moves:
        move.wait()
    tiles = rows // 8
    pairs = [(tile, group) for group in range(long_in.shape[0] // 8) for tile in range(group, tiles)]
    top = lax.broadcasted_iota(jnp.int32, (rows, HD), 0) < 2
    ext[0:8, :] = jnp.zeros((8, HD), jnp.float32)
    prod[0:8, :] = jnp.zeros((8, HD), jnp.float32)

    def one_head(head, carry):
        lanes = head_lanes(head)
        taps = taps_out[:, :, lanes]

        def feature(index, raw):
            wide = raw.astype(jnp.float32)
            ext[8:, :] = wide
            edge[index, :, lanes] = wide[0:8, :]
            return featurize(taps, index, ext, 8, rows)

        first = feature(0, packed[0:rows, lanes])
        product = (first * feature(2, packed[rows : 2 * rows, lanes])).astype(jnp.bfloat16).astype(jnp.float32)
        feat[:, lanes] = feature(1, gs_v[:, lanes])
        prod[8:, :] = jnp.where(top, 0.0, product)
        shift_copies(prod, copies)
        totals = lag_sums(long_out[:, lanes], copies, 8, pairs)
        partial[:, lanes] = jnp.concatenate(totals, axis=0)
        return carry

    lax.fori_loop(0, chans // HD, one_head, 0)


def in_hbm(*arrays):
    return [pltpu.with_memory_space_constraint(array, pltpu.HBM) for array in arrays]


def early(packed, gs, res, taps, long_taps):
    rows, chans = gs.shape
    hbm = pl.BlockSpec(memory_space=pltpu.HBM)
    vmem = pl.BlockSpec(memory_space=pltpu.VMEM)
    return pl.pallas_call(
        early_kernel,
        in_specs=[vmem] + [hbm] * 4,
        out_specs=[vmem] * 6,
        out_shape=[
            jax.ShapeDtypeStruct((rows, chans), jnp.float32),
            jax.ShapeDtypeStruct((rows, chans), jnp.float32),
            jax.ShapeDtypeStruct((rows, chans), jnp.bfloat16),
            jax.ShapeDtypeStruct((3, 8, chans), jnp.float32),
            jax.ShapeDtypeStruct(taps.shape, jnp.float32),
            jax.ShapeDtypeStruct(long_taps.shape, jnp.bfloat16),
        ],
        scratch_shapes=[
            pltpu.VMEM((rows, chans), jnp.bfloat16),
            pltpu.VMEM((rows + 8, HD), jnp.float32),
            pltpu.VMEM((rows + 8, HD), jnp.float32),
            pltpu.VMEM((8, rows + 8, HD), jnp.float32),
            pltpu.SemaphoreType.DMA((4,)),
        ],
        compiler_params=pltpu.CompilerParams(vmem_limit_bytes=32 << 20),
        cost_estimate=pl.CostEstimate(flops=20_000_000, bytes_accessed=2_000_000, transcendentals=0),
        name="early",
    )(packed, *in_hbm(gs, res, taps, long_taps))


def late_kernel(halo, partial, feat, res, edge, taps_in, long_in, stream, squares, ext, prod, copies):
    rows, chans = res.shape
    tiles = rows // 8
    pairs = [(tile, group) for group in range(long_in.shape[0] // 8) for tile in range(min(group + 2, tiles))]
    inside = lax.broadcasted_iota(jnp.int32, (rows, HD), 0) < rows - 6
    prod[0:8, :] = jnp.zeros((8, HD), jnp.float32)
    prod[rows + 8 :, :] = jnp.zeros((8, HD), jnp.float32)
    total = jnp.zeros((8, rows), jnp.float32)

    def one_head(head, total):
        lanes = head_lanes(head)
        taps = taps_in[:, :, lanes]

        def feature(index, begin):
            ext[0:rows, :] = halo[begin : begin + rows, lanes].astype(jnp.float32)
            ext[rows : rows + 8, :] = edge[index, :, lanes]
            return featurize(taps, index, ext, 8, rows)

        first = feature(0, 0)
        product = (first * feature(2, rows)).astype(jnp.bfloat16).astype(jnp.float32)
        prod[8 : rows + 8, :] = jnp.where(inside, product, 0.0)
        shift_copies(prod, copies)
        totals = lag_sums(long_in[:, lanes], copies, rows, pairs)
        filtered = partial[:, lanes] + jnp.concatenate(totals, axis=0)
        ext[0:8, :] = halo[2 * rows : 2 * rows + 8, lanes].astype(jnp.float32)
        ext[8:16, :] = edge[1, :, lanes]
        gate = jnp.concatenate([featurize(taps, 1, ext, 8, 8), feat[8:, lanes]], axis=0)
        out = (res[:, lanes].astype(jnp.float32) + gate * filtered).astype(jnp.bfloat16)
        stream[:, lanes] = out
        wide = out.astype(jnp.float32)
        total = total + lax.dot_general(
            jnp.ones((8, HD), jnp.float32),
            wide * wide,
            (((1,), (1,)), ((), ())),
            precision=HIGHEST,
            preferred_element_type=jnp.float32,
        )
        return total

    total = lax.fori_loop(0, chans // HD, one_head, total)
    squares[...] = total


def late(halo, partial, feat, res, edge, taps, long_taps):
    rows, chans = res.shape
    vmem = pl.BlockSpec(memory_space=pltpu.VMEM)
    return pl.pallas_call(
        late_kernel,
        in_specs=[vmem] * 7,
        out_specs=[vmem] * 2,
        out_shape=[
            jax.ShapeDtypeStruct((rows, chans), jnp.bfloat16),
            jax.ShapeDtypeStruct((8, rows), jnp.float32),
        ],
        scratch_shapes=[
            pltpu.VMEM((rows + 8, HD), jnp.float32),
            pltpu.VMEM((rows + 16, HD), jnp.float32),
            pltpu.VMEM((8, rows + 16, HD), jnp.float32),
        ],
        compiler_params=pltpu.CompilerParams(vmem_limit_bytes=32 << 20),
        cost_estimate=pl.CostEstimate(flops=30_000_000_000, bytes_accessed=2_000_000, transcendentals=0),
        name="late",
    )(halo, partial, feat, res, edge, taps, long_taps)


def pack_kernel(gf, hv, gs, keys, queries, halo, blocks, whole, sems):
    rows = gf.shape[0]
    pairs = [
        (keys, whole.at[0]),
        (queries, whole.at[1]),
        (gf, halo.at[0:rows]),
        (hv, halo.at[rows : 2 * rows]),
        (gs.at[rows - 8 : rows], halo.at[2 * rows : 2 * rows + 8]),
    ]
    for kind in range(2):
        for copy in range(blocks.shape[0]):
            for head in range(blocks.shape[1]):
                src = whole.at[kind, :, head * HD : (head + 1) * HD]
                pairs.append((src, blocks.at[copy, head, kind]))
    moves = [pltpu.make_async_copy(src, dst, sems.at[i]) for i, (src, dst) in enumerate(pairs)]
    half = (len(moves) - 5) // 2
    for move in moves[:5]:
        move.start()
    moves[0].wait()
    for move in moves[5 : 5 + half]:
        move.start()
    moves[1].wait()
    for move in moves[5 + half :]:
        move.start()
    for move in moves[2:]:
        move.wait()


def pack(gf, hv, gs, keys, queries):
    rows, chans = gf.shape
    heads = chans // HD
    vmem = pl.BlockSpec(memory_space=pltpu.VMEM)
    hbm = pl.BlockSpec(memory_space=pltpu.HBM)
    return pl.pallas_call(
        pack_kernel,
        in_specs=[hbm] * 5,
        out_specs=[vmem, hbm],
        out_shape=[
            jax.ShapeDtypeStruct((2 * rows + 8, chans), jnp.bfloat16),
            pltpu.HBM((2, heads, 2, rows, HD), jnp.bfloat16),
        ],
        scratch_shapes=[pltpu.VMEM((2, rows, chans), jnp.bfloat16), pltpu.SemaphoreType.DMA((4 * heads + 5,))],
        compiler_params=pltpu.CompilerParams(vmem_limit_bytes=16 << 20),
        cost_estimate=pl.CostEstimate(flops=0, bytes_accessed=600_000, transcendentals=0),
        name="pack",
    )(*in_hbm(gf, hv, gs, keys, queries))


def normalize_kernel(width, gathered, near, far, gain, packed):
    total = gathered[0]
    for peer in range(1, gathered.shape[0]):
        total = total + gathered[peer]
    total = jnp.broadcast_to(total, (8, total.shape[1]))
    total = lax.dot_general(
        jnp.where(lax.broadcasted_iota(jnp.int32, total.shape, 0) == 0, total, 0.0),
        jnp.ones((8, HD), jnp.float32),
        (((0,), (0,)), ((), ())),
        precision=HIGHEST,
        preferred_element_type=jnp.float32,
    )
    inverse = 1.0 / jnp.sqrt(total / width + 1e-06)
    rows = near.shape[0]
    for head in range(packed.shape[1]):
        lanes = slice(head * HD, (head + 1) * HD)
        for kind, ref in enumerate((near, far)):
            scale = inverse[kind * rows : (kind + 1) * rows, :]
            value = (ref[:, lanes].astype(jnp.float32) * scale * gain[:, lanes]).astype(jnp.bfloat16)
            for copy in range(packed.shape[0]):
                packed[copy, head, kind] = value


def normalize(width, gathered, near, far, gain):
    rows, chans = near.shape
    vmem = pl.BlockSpec(memory_space=pltpu.VMEM)
    return pl.pallas_call(
        functools.partial(normalize_kernel, width),
        in_specs=[vmem] * 4,
        out_specs=vmem,
        out_shape=jax.ShapeDtypeStruct((2, chans // HD, 2, rows, HD), jnp.bfloat16),
        compiler_params=pltpu.CompilerParams(vmem_limit_bytes=8 << 20),
        cost_estimate=pl.CostEstimate(flops=1_000_000, bytes_accessed=800_000, transcendentals=20_000),
        name="normalize",
    )(gathered, *in_hbm(near), far, gain)


def score_kernel(place, q, k0, k1, k2, k3, out, denom, keys, scores, weights, sems):
    rows = keys.shape[1] // 16
    count = keys.shape[1]
    block = scores.shape[0]
    unit = math.log2(math.e) / math.sqrt(HD)
    for part, ref in enumerate((k0, k1, k2, k3)):
        for peer in range(8):
            begin = (peer * 2 + part // 2) * rows
            keys[part % 2, begin : begin + rows, :] = ref[peer]
    chunks = [(begin, min(256, count - begin)) for begin in range(0, count, 256)]
    line = lax.broadcasted_iota(jnp.int32, (block, 1), 0)
    for index in range(q.shape[0] // block):
        query = q[index * block : (index + 1) * block, :]
        query_pos = line + place[2 + index * (block // rows)]
        for step in range(1, block // rows):
            moved = place[2 + index * (block // rows) + step] - step * rows
            query_pos = jnp.where(line >= step * rows, line + moved, query_pos)
        top = None
        for part in range(2):
            for begin, width in chunks:
                score = lax.dot_general(
                    query,
                    keys[part, begin : begin + width, :],
                    (((1,), (1,)), ((), ())),
                    preferred_element_type=jnp.float32,
                )
                lane = begin + lax.broadcasted_iota(jnp.int32, (1, width), 1)
                odd = begin // rows % 2
                key_pos = lane + place[6 + 2 * part + odd]
                for edge in range((begin // rows + 1) * rows, begin + width, rows):
                    odd = 1 - odd
                    key_pos = jnp.where(lane >= edge, lane + place[6 + 2 * part + odd], key_pos)
                score = jnp.where(key_pos <= query_pos, score * unit, -1e30)
                scores[:, part * count + begin : part * count + begin + width] = score
                for piece in range(0, width, 128):
                    piece = score[:, piece : piece + 128]
                    top = piece if top is None else jnp.maximum(top, piece)
        top = jnp.max(top, axis=1, keepdims=True)
        total = jnp.zeros((block, 128), jnp.float32)
        for begin in range(0, 2 * count, 128):
            expo = jnp.exp2(scores[:, begin : begin + 128] - top)
            total = total + expo
            weights[index * block : (index + 1) * block, begin : begin + 128] = expo.astype(jnp.bfloat16)
        total = jnp.sum(total, axis=1, keepdims=True)
        denom[index * block : (index + 1) * block, :] = jnp.broadcast_to(total, (block, 128))
        lines = pl.ds(index * block, block)
        pltpu.make_async_copy(weights.at[lines], out.at[lines], sems.at[index]).start()
    for index in range(q.shape[0] // block):
        lines = pl.ds(index * block, block)
        pltpu.make_async_copy(weights.at[lines], out.at[lines], sems.at[index]).wait()


def score(place, q, keys):
    lines = q.shape[0]
    count = sum(part.shape[0] * part.shape[1] for part in keys)
    block = lines // 2
    vmem = pl.BlockSpec(memory_space=pltpu.VMEM)
    return pl.pallas_call(
        score_kernel,
        in_specs=[pl.BlockSpec(memory_space=pltpu.SMEM)] + [vmem] * 5,
        out_specs=[pl.BlockSpec(memory_space=pltpu.HBM), vmem],
        out_shape=[
            pltpu.HBM((lines, count), jnp.bfloat16),
            jax.ShapeDtypeStruct((lines, 128), jnp.float32),
        ],
        scratch_shapes=[
            pltpu.VMEM((2, count // 2, HD), jnp.bfloat16),
            pltpu.VMEM((block, count), jnp.float32),
            pltpu.VMEM((lines, count), jnp.bfloat16),
            pltpu.SemaphoreType.DMA((2,)),
        ],
        compiler_params=pltpu.CompilerParams(vmem_limit_bytes=32 << 20),
        cost_estimate=pl.CostEstimate(
            flops=2 * lines * count * HD, bytes_accessed=8_000_000, transcendentals=lines * count
        ),
        name="score",
    )(place, q, *keys)


def attend_own_kernel(weights_in, values, out, later, weights, sems):
    keys = values.shape[0]
    cuts = [0, 640, 1152, 1664, keys]
    moves = []
    for half, target in enumerate((weights, later)):
        for begin, end in zip(cuts, cuts[1:]):
            src = weights_in.at[:, half * keys + begin : half * keys + end]
            moves.append(pltpu.make_async_copy(src, target.at[:, begin:end], sems.at[len(moves)]))
    for move in moves[:3]:
        move.start()
    total = jnp.zeros(out.shape, jnp.float32)
    for index, (begin, end) in enumerate(zip(cuts, cuts[1:])):
        moves[index].wait()
        for move in moves[3 + 2 * index : min(5 + 2 * index, len(moves))]:
            move.start()
        total = total + jnp.dot(
            weights[:, begin:end], values[begin:end, :], preferred_element_type=jnp.float32
        )
    out[...] = total
    for move in moves[4:]:
        move.wait()


def attend_other_kernel(weights, denom, before, values, out):
    total = before[...] + jnp.dot(weights[...], values[...], preferred_element_type=jnp.float32)
    out[...] = (total / denom[...]).astype(jnp.bfloat16)


def attend_own(weights, values):
    lines, count = weights.shape
    keys = count // 2
    vmem = pl.BlockSpec(memory_space=pltpu.VMEM)
    return pl.pallas_call(
        attend_own_kernel,
        in_specs=[pl.BlockSpec(memory_space=pltpu.HBM), vmem],
        out_specs=[vmem, vmem],
        out_shape=[
            jax.ShapeDtypeStruct((lines, HD), jnp.float32),
            jax.ShapeDtypeStruct((lines, keys), jnp.bfloat16),
        ],
        scratch_shapes=[pltpu.VMEM((lines, keys), jnp.bfloat16), pltpu.SemaphoreType.DMA((8,))],
        compiler_params=pltpu.CompilerParams(vmem_limit_bytes=16 << 20),
        cost_estimate=pl.CostEstimate(
            flops=2 * lines * keys * HD, bytes_accessed=5_500_000, transcendentals=0
        ),
        name="attend_own",
    )(*in_hbm(weights), values)


def attend_other(weights, denom, before, values):
    lines, keys = weights.shape
    vmem = pl.BlockSpec(memory_space=pltpu.VMEM)
    return pl.pallas_call(
        attend_other_kernel,
        in_specs=[vmem] * 4,
        out_specs=vmem,
        out_shape=jax.ShapeDtypeStruct((lines, HD), jnp.bfloat16),
        compiler_params=pltpu.CompilerParams(vmem_limit_bytes=16 << 20),
        cost_estimate=pl.CostEstimate(
            flops=2 * lines * keys * HD, bytes_accessed=3_500_000, transcendentals=0
        ),
        name="attend_other",
    )(weights, denom, before, values)


def exchange(value, axes):
    return lax.all_to_all(value, axes, 0, 0, tiled=True)


def swap_cores(value):
    return lax.ppermute(value, "c", [(0, 1), (1, 0)])


def shards(residual, gate_first, gate_second, hyena_value, short_taps, long_taps, norm_gain, queries, attn_keys):
    rows, chans = residual.shape
    heads = chans // HD
    count = 32
    width = chans * 16

    core = lax.axis_index("c")
    side = lax.axis_index("zh")
    group = side * 16 + lax.axis_index("s") * 8 + core
    place = [core, 1 - core] + [group + owner * 2 for owner in range(heads)]
    for sender in (core, 1 - core):
        place += [sender + side * 16, sender - 1 + (1 - side) * 16]
    place = (jnp.stack(place) * rows).astype(jnp.int32)

    last, blocks = pack(gate_first, hyena_value, gate_second, attn_keys, queries)
    blocks = exchange(blocks.reshape(8, 2, rows, HD), ("s", "h"))
    halo = lax.ppermute(last, ROWS_AXES, [(source, source + 1) for source in range(count - 1)])
    early_parts = early(last, gate_second, residual, short_taps, long_taps)
    stream, squares = late(halo, *early_parts)

    far_stream, far_squares = [lax.ppermute(value, "zh", [(0, 1)]) for value in (stream, squares)]
    squares = jnp.concatenate([squares[0:1], far_squares[0:1]], axis=1)
    squares = jnp.broadcast_to(squares, (16, 1, 2 * rows))
    blocks, squares, far_stream = lax.optimization_barrier((blocks, squares, far_stream))
    gathered = exchange(squares, CHAN_AXES)
    packed = normalize(width, gathered, stream, far_stream, norm_gain.reshape(1, chans))
    blocks, packed = lax.optimization_barrier((blocks, packed))
    values_own = exchange(packed.reshape(8, 2 * rows, HD), ("s", "h"))

    keys_near = blocks[:, 0]
    my_queries = lax.dynamic_slice_in_dim(blocks, lax.axis_index("s") * heads, heads, 0)[:, 1]
    keys_far = lax.ppermute(keys_near, "zh", [(0, 1)])
    parts = [keys_near, swap_cores(keys_near), keys_far, swap_cores(keys_far)]
    weights, denom = score(place, my_queries.reshape(heads * rows, HD), parts)
    values_own, denom = lax.optimization_barrier((values_own, denom))
    values_other = swap_cores(values_own)
    result, weights_other = attend_own(weights, values_own.reshape(16 * rows, HD))
    result = attend_other(weights_other, denom, result, values_other.reshape(16 * rows, HD))
    attended = exchange(result.reshape(heads, rows, HD), "h").transpose(1, 0, 2).reshape(rows, chans)
    return stream, attended


def solution(mesh):
    inner = Mesh(mesh.devices.reshape(2, 2, 4, 2, 4, 4), ROWS_AXES + CHAN_AXES)
    both = P(ROWS_AXES, CHAN_AXES)
    return jax.shard_map(
        shards,
        mesh=inner,
        in_specs=(both, both, both, both, P(None, None, CHAN_AXES), P(None, CHAN_AXES), P(CHAN_AXES), both, both),
        out_specs=(both, both),
        check_vma=False,
    )
```

```python
import functools
import math

import jax
import jax.numpy as jnp
from jax import lax
from jax.experimental import pallas as pl
from jax.experimental.pallas import tpu as pltpu
from jax.sharding import Mesh, PartitionSpec as P

HD = 128
ROWS_AXES = ("zh", "s", "h", "c")
CHAN_AXES = ("x", "zl")
HIGHEST = lax.Precision.HIGHEST


def shift_copies(prod, copies):
    length = prod.shape[0]
    for lag in range(8):
        copies[lag, 8:length, :] = prod[8 - lag : length - lag, :]


def lag_sums(weights, copies, base, pairs):
    totals = {}
    for group in range(weights.shape[0] // 8):
        wanted = [tile for tile, other in pairs if other == group]
        rows = weights[group * 8 : group * 8 + 8, :].astype(jnp.float32)
        for lag in range(8):
            weight = jnp.broadcast_to(rows[lag : lag + 1, :], rows.shape)
            for tile in wanted:
                begin = base + 8 * (tile - group)
                term = weight * copies[lag, begin : begin + 8, :]
                totals[tile] = totals[tile] + term if tile in totals else term
    return [totals[tile] for tile in sorted(totals)]


def featurize(taps, index, ext, begin, count):
    total = taps[index, 0:1, :] * ext[begin : begin + count, :]
    total = total + taps[index, 1:2, :] * ext[begin - 1 : begin - 1 + count, :]
    return total + taps[index, 2:3, :] * ext[begin - 2 : begin - 2 + count, :]


def head_lanes(head):
    return pl.ds(pl.multiple_of(head * HD, HD), HD)


def early_kernel(
    packed, gs, res, taps_in, long_in, partial, feat, res_out, edge, taps_out, long_out,
    gs_v, ext, prod, copies, sems,
):
    rows, chans = gs.shape
    loads = [(taps_in, taps_out), (long_in, long_out), (gs, gs_v), (res, res_out)]
    moves = [pltpu.make_async_copy(src, dst, sems.at[i]) for i, (src, dst) in enumerate(loads)]
    for move in moves:
        move.start()
    for move in moves:
        move.wait()
    tiles = rows // 8
    pairs = [(tile, group) for group in range(long_in.shape[0] // 8) for tile in range(group, tiles)]
    top = lax.broadcasted_iota(jnp.int32, (rows, HD), 0) < 2
    ext[0:8, :] = jnp.zeros((8, HD), jnp.float32)
    prod[0:8, :] = jnp.zeros((8, HD), jnp.float32)

    def one_head(head, carry):
        lanes = head_lanes(head)
        taps = taps_out[:, :, lanes]

        def feature(index, raw):
            wide = raw.astype(jnp.float32)
            ext[8:, :] = wide
            edge[index, :, lanes] = wide[0:8, :]
            return featurize(taps, index, ext, 8, rows)

        first = feature(0, packed[0:rows, lanes])
        product = (first * feature(2, packed[rows : 2 * rows, lanes])).astype(jnp.bfloat16).astype(jnp.float32)
        feat[:, lanes] = feature(1, gs_v[:, lanes])
        prod[8:, :] = jnp.where(top, 0.0, product)
        shift_copies(prod, copies)
        totals = lag_sums(long_out[:, lanes], copies, 8, pairs)
        partial[:, lanes] = jnp.concatenate(totals, axis=0)
        return carry

    lax.fori_loop(0, chans // HD, one_head, 0)


def in_hbm(*arrays):
    return [pltpu.with_memory_space_constraint(array, pltpu.HBM) for array in arrays]


def early(packed, gs, res, taps, long_taps):
    rows, chans = gs.shape
    hbm = pl.BlockSpec(memory_space=pltpu.HBM)
    vmem = pl.BlockSpec(memory_space=pltpu.VMEM)
    return pl.pallas_call(
        early_kernel,
        in_specs=[vmem] + [hbm] * 4,
        out_specs=[vmem] * 6,
        out_shape=[
            jax.ShapeDtypeStruct((rows, chans), jnp.float32),
            jax.ShapeDtypeStruct((rows, chans), jnp.float32),
            jax.ShapeDtypeStruct((rows, chans), jnp.bfloat16),
            jax.ShapeDtypeStruct((3, 8, chans), jnp.float32),
            jax.ShapeDtypeStruct(taps.shape, jnp.float32),
            jax.ShapeDtypeStruct(long_taps.shape, jnp.bfloat16),
        ],
        scratch_shapes=[
            pltpu.VMEM((rows, chans), jnp.bfloat16),
            pltpu.VMEM((rows + 8, HD), jnp.float32),
            pltpu.VMEM((rows + 8, HD), jnp.float32),
            pltpu.VMEM((8, rows + 8, HD), jnp.float32),
            pltpu.SemaphoreType.DMA((4,)),
        ],
        compiler_params=pltpu.CompilerParams(vmem_limit_bytes=32 << 20),
        cost_estimate=pl.CostEstimate(flops=20_000_000, bytes_accessed=2_000_000, transcendentals=0),
        name="early",
    )(packed, *in_hbm(gs, res, taps, long_taps))


def late_kernel(halo, partial, feat, res, edge, taps_in, long_in, stream, squares, ext, prod, copies):
    rows, chans = res.shape
    tiles = rows // 8
    pairs = [(tile, group) for group in range(long_in.shape[0] // 8) for tile in range(min(group + 2, tiles))]
    inside = lax.broadcasted_iota(jnp.int32, (rows, HD), 0) < rows - 6
    prod[0:8, :] = jnp.zeros((8, HD), jnp.float32)
    prod[rows + 8 :, :] = jnp.zeros((8, HD), jnp.float32)
    total = jnp.zeros((8, rows), jnp.float32)

    def one_head(head, total):
        lanes = head_lanes(head)
        taps = taps_in[:, :, lanes]

        def feature(index, begin):
            ext[0:rows, :] = halo[begin : begin + rows, lanes].astype(jnp.float32)
            ext[rows : rows + 8, :] = edge[index, :, lanes]
            return featurize(taps, index, ext, 8, rows)

        first = feature(0, 0)
        product = (first * feature(2, rows)).astype(jnp.bfloat16).astype(jnp.float32)
        prod[8 : rows + 8, :] = jnp.where(inside, product, 0.0)
        shift_copies(prod, copies)
        totals = lag_sums(long_in[:, lanes], copies, rows, pairs)
        filtered = partial[:, lanes] + jnp.concatenate(totals, axis=0)
        ext[0:8, :] = halo[2 * rows : 2 * rows + 8, lanes].astype(jnp.float32)
        ext[8:16, :] = edge[1, :, lanes]
        gate = jnp.concatenate([featurize(taps, 1, ext, 8, 8), feat[8:, lanes]], axis=0)
        out = (res[:, lanes].astype(jnp.float32) + gate * filtered).astype(jnp.bfloat16)
        stream[:, lanes] = out
        wide = out.astype(jnp.float32)
        total = total + lax.dot_general(
            jnp.ones((8, HD), jnp.float32),
            wide * wide,
            (((1,), (1,)), ((), ())),
            precision=HIGHEST,
            preferred_element_type=jnp.float32,
        )
        return total

    total = lax.fori_loop(0, chans // HD, one_head, total)
    squares[...] = total


def late(halo, partial, feat, res, edge, taps, long_taps):
    rows, chans = res.shape
    vmem = pl.BlockSpec(memory_space=pltpu.VMEM)
    return pl.pallas_call(
        late_kernel,
        in_specs=[vmem] * 7,
        out_specs=[vmem] * 2,
        out_shape=[
            jax.ShapeDtypeStruct((rows, chans), jnp.bfloat16),
            jax.ShapeDtypeStruct((8, rows), jnp.float32),
        ],
        scratch_shapes=[
            pltpu.VMEM((rows + 8, HD), jnp.float32),
            pltpu.VMEM((rows + 16, HD), jnp.float32),
            pltpu.VMEM((8, rows + 16, HD), jnp.float32),
        ],
        compiler_params=pltpu.CompilerParams(vmem_limit_bytes=32 << 20),
        cost_estimate=pl.CostEstimate(flops=30_000_000_000, bytes_accessed=2_000_000, transcendentals=0),
        name="late",
    )(halo, partial, feat, res, edge, taps, long_taps)


def pack_kernel(gf, hv, gs, keys, queries, halo, blocks, whole, sems):
    rows = gf.shape[0]
    pairs = [
        (keys, whole.at[0]),
        (queries, whole.at[1]),
        (gf, halo.at[0:rows]),
        (hv, halo.at[rows : 2 * rows]),
        (gs.at[rows - 8 : rows], halo.at[2 * rows : 2 * rows + 8]),
    ]
    for kind in range(2):
        for copy in range(blocks.shape[0]):
            for head in range(blocks.shape[1]):
                src = whole.at[kind, :, head * HD : (head + 1) * HD]
                pairs.append((src, blocks.at[copy, head, kind]))
    moves = [pltpu.make_async_copy(src, dst, sems.at[i]) for i, (src, dst) in enumerate(pairs)]
    half = (len(moves) - 5) // 2
    for move in moves[:5]:
        move.start()
    moves[0].wait()
    for move in moves[5 : 5 + half]:
        move.start()
    moves[1].wait()
    for move in moves[5 + half :]:
        move.start()
    for move in moves[2:]:
        move.wait()


def pack(gf, hv, gs, keys, queries):
    rows, chans = gf.shape
    heads = chans // HD
    vmem = pl.BlockSpec(memory_space=pltpu.VMEM)
    hbm = pl.BlockSpec(memory_space=pltpu.HBM)
    return pl.pallas_call(
        pack_kernel,
        in_specs=[hbm] * 5,
        out_specs=[vmem, hbm],
        out_shape=[
            jax.ShapeDtypeStruct((2 * rows + 8, chans), jnp.bfloat16),
            pltpu.HBM((2, heads, 2, rows, HD), jnp.bfloat16),
        ],
        scratch_shapes=[pltpu.VMEM((2, rows, chans), jnp.bfloat16), pltpu.SemaphoreType.DMA((4 * heads + 5,))],
        compiler_params=pltpu.CompilerParams(vmem_limit_bytes=16 << 20),
        cost_estimate=pl.CostEstimate(flops=0, bytes_accessed=600_000, transcendentals=0),
        name="pack",
    )(*in_hbm(gf, hv, gs, keys, queries))


def normalize_kernel(width, gathered, near, far, gain, packed):
    total = gathered[0]
    for peer in range(1, gathered.shape[0]):
        total = total + gathered[peer]
    total = jnp.broadcast_to(total, (8, total.shape[1]))
    total = lax.dot_general(
        jnp.where(lax.broadcasted_iota(jnp.int32, total.shape, 0) == 0, total, 0.0),
        jnp.ones((8, HD), jnp.float32),
        (((0,), (0,)), ((), ())),
        precision=HIGHEST,
        preferred_element_type=jnp.float32,
    )
    inverse = 1.0 / jnp.sqrt(total / width + 1e-06)
    rows = near.shape[0]
    for head in range(packed.shape[1]):
        lanes = slice(head * HD, (head + 1) * HD)
        for kind, ref in enumerate((near, far)):
            scale = inverse[kind * rows : (kind + 1) * rows, :]
            value = (ref[:, lanes].astype(jnp.float32) * scale * gain[:, lanes]).astype(jnp.bfloat16)
            for copy in range(packed.shape[0]):
                packed[copy, head, kind] = value


def normalize(width, gathered, near, far, gain):
    rows, chans = near.shape
    vmem = pl.BlockSpec(memory_space=pltpu.VMEM)
    return pl.pallas_call(
        functools.partial(normalize_kernel, width),
        in_specs=[vmem] * 4,
        out_specs=vmem,
        out_shape=jax.ShapeDtypeStruct((2, chans // HD, 2, rows, HD), jnp.bfloat16),
        compiler_params=pltpu.CompilerParams(vmem_limit_bytes=8 << 20),
        cost_estimate=pl.CostEstimate(flops=1_000_000, bytes_accessed=800_000, transcendentals=20_000),
        name="normalize",
    )(gathered, *in_hbm(near), far, gain)


def score_kernel(place, q, k0, k1, k2, k3, out, denom, keys, scores, weights, sems):
    rows = keys.shape[1] // 16
    count = keys.shape[1]
    block = scores.shape[0]
    unit = math.log2(math.e) / math.sqrt(HD)
    for part, ref in enumerate((k0, k1, k2, k3)):
        for peer in range(8):
            begin = (peer * 2 + part // 2) * rows
            keys[part % 2, begin : begin + rows, :] = ref[peer]
    chunks = [(begin, min(256, count - begin)) for begin in range(0, count, 256)]
    line = lax.broadcasted_iota(jnp.int32, (block, 1), 0)
    for index in range(q.shape[0] // block):
        query = q[index * block : (index + 1) * block, :]
        query_pos = line + place[2 + index * (block // rows)]
        for step in range(1, block // rows):
            moved = place[2 + index * (block // rows) + step] - step * rows
            query_pos = jnp.where(line >= step * rows, line + moved, query_pos)
        top = None
        for part in range(2):
            for begin, width in chunks:
                score = lax.dot_general(
                    query,
                    keys[part, begin : begin + width, :],
                    (((1,), (1,)), ((), ())),
                    preferred_element_type=jnp.float32,
                )
                lane = begin + lax.broadcasted_iota(jnp.int32, (1, width), 1)
                odd = begin // rows % 2
                key_pos = lane + place[6 + 2 * part + odd]
                for edge in range((begin // rows + 1) * rows, begin + width, rows):
                    odd = 1 - odd
                    key_pos = jnp.where(lane >= edge, lane + place[6 + 2 * part + odd], key_pos)
                score = jnp.where(key_pos <= query_pos, score * unit, -1e30)
                scores[:, part * count + begin : part * count + begin + width] = score
                for piece in range(0, width, 128):
                    piece = score[:, piece : piece + 128]
                    top = piece if top is None else jnp.maximum(top, piece)
        top = jnp.max(top, axis=1, keepdims=True)
        total = jnp.zeros((block, 128), jnp.float32)
        for begin in range(0, 2 * count, 128):
            expo = jnp.exp2(scores[:, begin : begin + 128] - top)
            total = total + expo
            weights[index * block : (index + 1) * block, begin : begin + 128] = expo.astype(jnp.bfloat16)
        total = jnp.sum(total, axis=1, keepdims=True)
        denom[index * block : (index + 1) * block, :] = jnp.broadcast_to(total, (block, 128))
        lines = pl.ds(index * block, block)
        pltpu.make_async_copy(weights.at[lines], out.at[lines], sems.at[index]).start()
    for index in range(q.shape[0] // block):
        lines = pl.ds(index * block, block)
        pltpu.make_async_copy(weights.at[lines], out.at[lines], sems.at[index]).wait()


def score(place, q, keys):
    lines = q.shape[0]
    count = sum(part.shape[0] * part.shape[1] for part in keys)
    block = lines // 2
    vmem = pl.BlockSpec(memory_space=pltpu.VMEM)
    return pl.pallas_call(
        score_kernel,
        in_specs=[pl.BlockSpec(memory_space=pltpu.SMEM)] + [vmem] * 5,
        out_specs=[pl.BlockSpec(memory_space=pltpu.HBM), vmem],
        out_shape=[
            pltpu.HBM((lines, count), jnp.bfloat16),
            jax.ShapeDtypeStruct((lines, 128), jnp.float32),
        ],
        scratch_shapes=[
            pltpu.VMEM((2, count // 2, HD), jnp.bfloat16),
            pltpu.VMEM((block, count), jnp.float32),
            pltpu.VMEM((lines, count), jnp.bfloat16),
            pltpu.SemaphoreType.DMA((2,)),
        ],
        compiler_params=pltpu.CompilerParams(vmem_limit_bytes=32 << 20),
        cost_estimate=pl.CostEstimate(
            flops=2 * lines * count * HD, bytes_accessed=8_000_000, transcendentals=lines * count
        ),
        name="score",
    )(place, q, *keys)


def attend_own_kernel(weights_in, values, out, later, weights, sems):
    keys = values.shape[0]
    cuts = [0, 640, 1152, 1664, keys]
    moves = []
    for half, target in enumerate((weights, later)):
        for begin, end in zip(cuts, cuts[1:]):
            src = weights_in.at[:, half * keys + begin : half * keys + end]
            moves.append(pltpu.make_async_copy(src, target.at[:, begin:end], sems.at[len(moves)]))
    for move in moves[:3]:
        move.start()
    total = jnp.zeros(out.shape, jnp.float32)
    for index, (begin, end) in enumerate(zip(cuts, cuts[1:])):
        moves[index].wait()
        for move in moves[3 + 2 * index : min(5 + 2 * index, len(moves))]:
            move.start()
        total = total + jnp.dot(
            weights[:, begin:end], values[begin:end, :], preferred_element_type=jnp.float32
        )
    out[...] = total
    for move in moves[4:]:
        move.wait()


def attend_other_kernel(weights, denom, before, values, out):
    total = before[...] + jnp.dot(weights[...], values[...], preferred_element_type=jnp.float32)
    out[...] = (total / denom[...]).astype(jnp.bfloat16)


def attend_own(weights, values):
    lines, count = weights.shape
    keys = count // 2
    vmem = pl.BlockSpec(memory_space=pltpu.VMEM)
    return pl.pallas_call(
        attend_own_kernel,
        in_specs=[pl.BlockSpec(memory_space=pltpu.HBM), vmem],
        out_specs=[vmem, vmem],
        out_shape=[
            jax.ShapeDtypeStruct((lines, HD), jnp.float32),
            jax.ShapeDtypeStruct((lines, keys), jnp.bfloat16),
        ],
        scratch_shapes=[pltpu.VMEM((lines, keys), jnp.bfloat16), pltpu.SemaphoreType.DMA((8,))],
        compiler_params=pltpu.CompilerParams(vmem_limit_bytes=16 << 20),
        cost_estimate=pl.CostEstimate(
            flops=2 * lines * keys * HD, bytes_accessed=5_500_000, transcendentals=0
        ),
        name="attend_own",
    )(*in_hbm(weights), values)


def attend_other(weights, denom, before, values):
    lines, keys = weights.shape
    vmem = pl.BlockSpec(memory_space=pltpu.VMEM)
    return pl.pallas_call(
        attend_other_kernel,
        in_specs=[vmem] * 4,
        out_specs=vmem,
        out_shape=jax.ShapeDtypeStruct((lines, HD), jnp.bfloat16),
        compiler_params=pltpu.CompilerParams(vmem_limit_bytes=16 << 20),
        cost_estimate=pl.CostEstimate(
            flops=2 * lines * keys * HD, bytes_accessed=3_500_000, transcendentals=0
        ),
        name="attend_other",
    )(weights, denom, before, values)


def exchange(value, axes):
    return lax.all_to_all(value, axes, 0, 0, tiled=True)


def swap_cores(value):
    return lax.ppermute(value, "c", [(0, 1), (1, 0)])


def shards(residual, gate_first, gate_second, hyena_value, short_taps, long_taps, norm_gain, queries, attn_keys):
    rows, chans = residual.shape
    heads = chans // HD
    count = 32
    width = chans * 16

    core = lax.axis_index("c")
    side = lax.axis_index("zh")
    group = side * 16 + lax.axis_index("s") * 8 + core
    place = [core, 1 - core] + [group + owner * 2 for owner in range(heads)]
    for sender in (core, 1 - core):
        place += [sender + side * 16, sender - 1 + (1 - side) * 16]
    place = (jnp.stack(place) * rows).astype(jnp.int32)

    last, blocks = pack(gate_first, hyena_value, gate_second, attn_keys, queries)
    blocks = exchange(blocks.reshape(8, 2, rows, HD), ("s", "h"))
    halo = lax.ppermute(last, ROWS_AXES, [(source, source + 1) for source in range(count - 1)])
    early_parts = early(last, gate_second, residual, short_taps, long_taps)
    stream, squares = late(halo, *early_parts)

    far_stream, far_squares = [lax.ppermute(value, "zh", [(0, 1)]) for value in (stream, squares)]
    squares = jnp.concatenate([squares[0:1], far_squares[0:1]], axis=1)
    squares = jnp.broadcast_to(squares, (16, 1, 2 * rows))
    blocks, squares, far_stream = lax.optimization_barrier((blocks, squares, far_stream))
    gathered = exchange(squares, CHAN_AXES)
    packed = normalize(width, gathered, stream, far_stream, norm_gain.reshape(1, chans))
    keys_near = blocks[:, 0]
    my_queries = lax.dynamic_slice_in_dim(blocks, lax.axis_index("s") * heads, heads, 0)[:, 1]
    keys_far = lax.ppermute(keys_near, "zh", [(0, 1)])
    packed, keys_far = lax.optimization_barrier((packed, keys_far))
    values_own = exchange(packed.reshape(8, 2 * rows, HD), ("s", "h"))

    parts = [keys_near, swap_cores(keys_near), keys_far, swap_cores(keys_far)]
    weights, denom = score(place, my_queries.reshape(heads * rows, HD), parts)
    values_own, denom = lax.optimization_barrier((values_own, denom))
    values_other = swap_cores(values_own)
    result, weights_other = attend_own(weights, values_own.reshape(16 * rows, HD))
    result = attend_other(weights_other, denom, result, values_other.reshape(16 * rows, HD))
    attended = exchange(result.reshape(heads, rows, HD), "h").transpose(1, 0, 2).reshape(rows, chans)
    return stream, attended


def solution(mesh):
    inner = Mesh(mesh.devices.reshape(2, 2, 4, 2, 4, 4), ROWS_AXES + CHAN_AXES)
    both = P(ROWS_AXES, CHAN_AXES)
    return jax.shard_map(
        shards,
        mesh=inner,
        in_specs=(both, both, both, both, P(None, None, CHAN_AXES), P(None, CHAN_AXES), P(CHAN_AXES), both, both),
        out_specs=(both, both),
        check_vma=False,
    )
```

```python
import functools
import math

import jax
import jax.numpy as jnp
from jax import lax
from jax.experimental import pallas as pl
from jax.experimental.pallas import tpu as pltpu
from jax.sharding import Mesh, PartitionSpec as P

HD = 128
ROWS_AXES = ("zh", "s", "h", "c")
CHAN_AXES = ("x", "zl")
HIGHEST = lax.Precision.HIGHEST


def shift_copies(prod, copies):
    length = prod.shape[0]
    for lag in range(8):
        copies[lag, 8:length, :] = prod[8 - lag : length - lag, :]


def lag_sums(weights, copies, base, pairs):
    totals = {}
    for group in range(weights.shape[0] // 8):
        wanted = [tile for tile, other in pairs if other == group]
        rows = weights[group * 8 : group * 8 + 8, :].astype(jnp.float32)
        for lag in range(8):
            weight = jnp.broadcast_to(rows[lag : lag + 1, :], rows.shape)
            for tile in wanted:
                begin = base + 8 * (tile - group)
                term = weight * copies[lag, begin : begin + 8, :]
                totals[tile] = totals[tile] + term if tile in totals else term
    return [totals[tile] for tile in sorted(totals)]


def featurize(taps, index, ext, begin, count):
    total = taps[index, 0:1, :] * ext[begin : begin + count, :]
    total = total + taps[index, 1:2, :] * ext[begin - 1 : begin - 1 + count, :]
    return total + taps[index, 2:3, :] * ext[begin - 2 : begin - 2 + count, :]


def head_lanes(head):
    return slice(head * HD, (head + 1) * HD)


def early_kernel(
    packed, gs, res, taps_in, long_in, partial, feat, res_out, edge, taps_out, long_out,
    gs_v, exts, prods, all_copies, sems,
):
    rows, chans = gs.shape
    loads = [(taps_in, taps_out), (long_in, long_out), (gs, gs_v), (res, res_out)]
    moves = [pltpu.make_async_copy(src, dst, sems.at[i]) for i, (src, dst) in enumerate(loads)]
    for move in moves:
        move.start()
    for move in moves:
        move.wait()
    tiles = rows // 8
    pairs = [(tile, group) for group in range(long_in.shape[0] // 8) for tile in range(group, tiles)]
    top = lax.broadcasted_iota(jnp.int32, (rows, HD), 0) < 2

    def one_head(head):
        lanes = head_lanes(head)
        ext, prod, copies = exts.at[head], prods.at[head], all_copies.at[head]
        ext[0:8, :] = jnp.zeros((8, HD), jnp.float32)
        prod[0:8, :] = jnp.zeros((8, HD), jnp.float32)
        taps = taps_out[:, :, lanes]

        def feature(index, raw):
            wide = raw.astype(jnp.float32)
            ext[8:, :] = wide
            edge[index, :, lanes] = wide[0:8, :]
            return featurize(taps, index, ext, 8, rows)

        first = feature(0, packed[0:rows, lanes])
        product = (first * feature(2, packed[rows : 2 * rows, lanes])).astype(jnp.bfloat16).astype(jnp.float32)
        feat[:, lanes] = feature(1, gs_v[:, lanes])
        prod[8:, :] = jnp.where(top, 0.0, product)
        shift_copies(prod, copies)
        totals = lag_sums(long_out[:, lanes], copies, 8, pairs)
        partial[:, lanes] = jnp.concatenate(totals, axis=0)

    for head in range(chans // HD):
        one_head(head)


def in_hbm(*arrays):
    return [pltpu.with_memory_space_constraint(array, pltpu.HBM) for array in arrays]


def early(packed, gs, res, taps, long_taps):
    rows, chans = gs.shape
    heads = chans // HD
    hbm = pl.BlockSpec(memory_space=pltpu.HBM)
    vmem = pl.BlockSpec(memory_space=pltpu.VMEM)
    return pl.pallas_call(
        early_kernel,
        in_specs=[vmem] + [hbm] * 4,
        out_specs=[vmem] * 6,
        out_shape=[
            jax.ShapeDtypeStruct((rows, chans), jnp.float32),
            jax.ShapeDtypeStruct((rows, chans), jnp.float32),
            jax.ShapeDtypeStruct((rows, chans), jnp.bfloat16),
            jax.ShapeDtypeStruct((3, 8, chans), jnp.float32),
            jax.ShapeDtypeStruct(taps.shape, jnp.float32),
            jax.ShapeDtypeStruct(long_taps.shape, jnp.bfloat16),
        ],
        scratch_shapes=[
            pltpu.VMEM((rows, chans), jnp.bfloat16),
            pltpu.VMEM((heads, rows + 8, HD), jnp.float32),
            pltpu.VMEM((heads, rows + 8, HD), jnp.float32),
            pltpu.VMEM((heads, 8, rows + 8, HD), jnp.float32),
            pltpu.SemaphoreType.DMA((4,)),
        ],
        compiler_params=pltpu.CompilerParams(vmem_limit_bytes=32 << 20),
        cost_estimate=pl.CostEstimate(flops=20_000_000, bytes_accessed=2_000_000, transcendentals=0),
        name="early",
    )(packed, *in_hbm(gs, res, taps, long_taps))


def late_kernel(halo, partial, feat, res, edge, taps_in, long_in, stream, squares, exts, prods, all_copies):
    rows, chans = res.shape
    tiles = rows // 8
    pairs = [(tile, group) for group in range(long_in.shape[0] // 8) for tile in range(min(group + 2, tiles))]
    inside = lax.broadcasted_iota(jnp.int32, (rows, HD), 0) < rows - 6
    total = jnp.zeros((8, rows), jnp.float32)

    def one_head(head, total):
        lanes = head_lanes(head)
        ext, prod, copies = exts.at[head], prods.at[head], all_copies.at[head]
        prod[0:8, :] = jnp.zeros((8, HD), jnp.float32)
        prod[rows + 8 :, :] = jnp.zeros((8, HD), jnp.float32)
        taps = taps_in[:, :, lanes]

        def feature(index, begin):
            ext[0:rows, :] = halo[begin : begin + rows, lanes].astype(jnp.float32)
            ext[rows : rows + 8, :] = edge[index, :, lanes]
            return featurize(taps, index, ext, 8, rows)

        first = feature(0, 0)
        product = (first * feature(2, rows)).astype(jnp.bfloat16).astype(jnp.float32)
        prod[8 : rows + 8, :] = jnp.where(inside, product, 0.0)
        shift_copies(prod, copies)
        totals = lag_sums(long_in[:, lanes], copies, rows, pairs)
        filtered = partial[:, lanes] + jnp.concatenate(totals, axis=0)
        ext[0:8, :] = halo[2 * rows : 2 * rows + 8, lanes].astype(jnp.float32)
        ext[8:16, :] = edge[1, :, lanes]
        gate = jnp.concatenate([featurize(taps, 1, ext, 8, 8), feat[8:, lanes]], axis=0)
        out = (res[:, lanes].astype(jnp.float32) + gate * filtered).astype(jnp.bfloat16)
        stream[:, lanes] = out
        wide = out.astype(jnp.float32)
        total = total + lax.dot_general(
            jnp.ones((8, HD), jnp.float32),
            wide * wide,
            (((1,), (1,)), ((), ())),
            precision=HIGHEST,
            preferred_element_type=jnp.float32,
        )
        return total

    for head in range(chans // HD):
        total = one_head(head, total)
    squares[...] = total


def late(halo, partial, feat, res, edge, taps, long_taps):
    rows, chans = res.shape
    heads = chans // HD
    vmem = pl.BlockSpec(memory_space=pltpu.VMEM)
    return pl.pallas_call(
        late_kernel,
        in_specs=[vmem] * 7,
        out_specs=[vmem] * 2,
        out_shape=[
            jax.ShapeDtypeStruct((rows, chans), jnp.bfloat16),
            jax.ShapeDtypeStruct((8, rows), jnp.float32),
        ],
        scratch_shapes=[
            pltpu.VMEM((heads, rows + 8, HD), jnp.float32),
            pltpu.VMEM((heads, rows + 16, HD), jnp.float32),
            pltpu.VMEM((heads, 8, rows + 16, HD), jnp.float32),
        ],
        compiler_params=pltpu.CompilerParams(vmem_limit_bytes=32 << 20),
        cost_estimate=pl.CostEstimate(flops=30_000_000_000, bytes_accessed=2_000_000, transcendentals=0),
        name="late",
    )(halo, partial, feat, res, edge, taps, long_taps)


def pack_kernel(gf, hv, gs, keys, queries, halo, blocks, whole, sems):
    rows = gf.shape[0]
    pairs = [
        (keys, whole.at[0]),
        (queries, whole.at[1]),
        (gf, halo.at[0:rows]),
        (hv, halo.at[rows : 2 * rows]),
        (gs.at[rows - 8 : rows], halo.at[2 * rows : 2 * rows + 8]),
    ]
    for kind in range(2):
        for copy in range(blocks.shape[0]):
            for head in range(blocks.shape[1]):
                src = whole.at[kind, :, head * HD : (head + 1) * HD]
                pairs.append((src, blocks.at[copy, head, kind]))
    moves = [pltpu.make_async_copy(src, dst, sems.at[i]) for i, (src, dst) in enumerate(pairs)]
    half = (len(moves) - 5) // 2
    for move in moves[:5]:
        move.start()
    moves[0].wait()
    for move in moves[5 : 5 + half]:
        move.start()
    moves[1].wait()
    for move in moves[5 + half :]:
        move.start()
    for move in moves[2:]:
        move.wait()


def pack(gf, hv, gs, keys, queries):
    rows, chans = gf.shape
    heads = chans // HD
    vmem = pl.BlockSpec(memory_space=pltpu.VMEM)
    hbm = pl.BlockSpec(memory_space=pltpu.HBM)
    return pl.pallas_call(
        pack_kernel,
        in_specs=[hbm] * 5,
        out_specs=[vmem, hbm],
        out_shape=[
            jax.ShapeDtypeStruct((2 * rows + 8, chans), jnp.bfloat16),
            pltpu.HBM((2, heads, 2, rows, HD), jnp.bfloat16),
        ],
        scratch_shapes=[pltpu.VMEM((2, rows, chans), jnp.bfloat16), pltpu.SemaphoreType.DMA((4 * heads + 5,))],
        compiler_params=pltpu.CompilerParams(vmem_limit_bytes=16 << 20),
        cost_estimate=pl.CostEstimate(flops=0, bytes_accessed=600_000, transcendentals=0),
        name="pack",
    )(*in_hbm(gf, hv, gs, keys, queries))


def normalize_kernel(width, gathered, near, far, gain, packed):
    total = gathered[0]
    for peer in range(1, gathered.shape[0]):
        total = total + gathered[peer]
    total = jnp.broadcast_to(total, (8, total.shape[1]))
    total = lax.dot_general(
        jnp.where(lax.broadcasted_iota(jnp.int32, total.shape, 0) == 0, total, 0.0),
        jnp.ones((8, HD), jnp.float32),
        (((0,), (0,)), ((), ())),
        precision=HIGHEST,
        preferred_element_type=jnp.float32,
    )
    inverse = 1.0 / jnp.sqrt(total / width + 1e-06)
    rows = near.shape[0]
    for head in range(packed.shape[1]):
        lanes = slice(head * HD, (head + 1) * HD)
        for kind, ref in enumerate((near, far)):
            scale = inverse[kind * rows : (kind + 1) * rows, :]
            value = (ref[:, lanes].astype(jnp.float32) * scale * gain[:, lanes]).astype(jnp.bfloat16)
            for copy in range(packed.shape[0]):
                packed[copy, head, kind] = value


def normalize(width, gathered, near, far, gain):
    rows, chans = near.shape
    vmem = pl.BlockSpec(memory_space=pltpu.VMEM)
    return pl.pallas_call(
        functools.partial(normalize_kernel, width),
        in_specs=[vmem] * 4,
        out_specs=vmem,
        out_shape=jax.ShapeDtypeStruct((2, chans // HD, 2, rows, HD), jnp.bfloat16),
        compiler_params=pltpu.CompilerParams(vmem_limit_bytes=8 << 20),
        cost_estimate=pl.CostEstimate(flops=1_000_000, bytes_accessed=800_000, transcendentals=20_000),
        name="normalize",
    )(gathered, *in_hbm(near), far, gain)


def score_kernel(place, q, k0, k1, k2, k3, out, denom, keys, scores, weights, sems):
    rows = keys.shape[1] // 16
    count = keys.shape[1]
    block = scores.shape[0]
    unit = math.log2(math.e) / math.sqrt(HD)
    for part, ref in enumerate((k0, k1, k2, k3)):
        for peer in range(8):
            begin = (peer * 2 + part // 2) * rows
            keys[part % 2, begin : begin + rows, :] = ref[peer]
    chunks = [(begin, min(256, count - begin)) for begin in range(0, count, 256)]
    line = lax.broadcasted_iota(jnp.int32, (block, 1), 0)
    for index in range(q.shape[0] // block):
        query = q[index * block : (index + 1) * block, :]
        query_pos = line + place[2 + index * (block // rows)]
        for step in range(1, block // rows):
            moved = place[2 + index * (block // rows) + step] - step * rows
            query_pos = jnp.where(line >= step * rows, line + moved, query_pos)
        top = None
        for part in range(2):
            for begin, width in chunks:
                score = lax.dot_general(
                    query,
                    keys[part, begin : begin + width, :],
                    (((1,), (1,)), ((), ())),
                    preferred_element_type=jnp.float32,
                )
                lane = begin + lax.broadcasted_iota(jnp.int32, (1, width), 1)
                odd = begin // rows % 2
                key_pos = lane + place[6 + 2 * part + odd]
                for edge in range((begin // rows + 1) * rows, begin + width, rows):
                    odd = 1 - odd
                    key_pos = jnp.where(lane >= edge, lane + place[6 + 2 * part + odd], key_pos)
                score = jnp.where(key_pos <= query_pos, score * unit, -1e30)
                scores[:, part * count + begin : part * count + begin + width] = score
                for piece in range(0, width, 128):
                    piece = score[:, piece : piece + 128]
                    top = piece if top is None else jnp.maximum(top, piece)
        top = jnp.max(top, axis=1, keepdims=True)
        total = jnp.zeros((block, 128), jnp.float32)
        for begin in range(0, 2 * count, 128):
            expo = jnp.exp2(scores[:, begin : begin + 128] - top)
            total = total + expo
            weights[index * block : (index + 1) * block, begin : begin + 128] = expo.astype(jnp.bfloat16)
        total = jnp.sum(total, axis=1, keepdims=True)
        denom[index * block : (index + 1) * block, :] = jnp.broadcast_to(total, (block, 128))
        lines = pl.ds(index * block, block)
        pltpu.make_async_copy(weights.at[lines], out.at[lines], sems.at[index]).start()
    for index in range(q.shape[0] // block):
        lines = pl.ds(index * block, block)
        pltpu.make_async_copy(weights.at[lines], out.at[lines], sems.at[index]).wait()


def score(place, q, keys):
    lines = q.shape[0]
    count = sum(part.shape[0] * part.shape[1] for part in keys)
    block = lines // 2
    vmem = pl.BlockSpec(memory_space=pltpu.VMEM)
    return pl.pallas_call(
        score_kernel,
        in_specs=[pl.BlockSpec(memory_space=pltpu.SMEM)] + [vmem] * 5,
        out_specs=[pl.BlockSpec(memory_space=pltpu.HBM), vmem],
        out_shape=[
            pltpu.HBM((lines, count), jnp.bfloat16),
            jax.ShapeDtypeStruct((lines, 128), jnp.float32),
        ],
        scratch_shapes=[
            pltpu.VMEM((2, count // 2, HD), jnp.bfloat16),
            pltpu.VMEM((block, count), jnp.float32),
            pltpu.VMEM((lines, count), jnp.bfloat16),
            pltpu.SemaphoreType.DMA((2,)),
        ],
        compiler_params=pltpu.CompilerParams(vmem_limit_bytes=32 << 20),
        cost_estimate=pl.CostEstimate(
            flops=2 * lines * count * HD, bytes_accessed=8_000_000, transcendentals=lines * count
        ),
        name="score",
    )(place, q, *keys)


def attend_own_kernel(weights_in, values, out, later, weights, sems):
    keys = values.shape[0]
    cuts = [0, 640, 1152, 1664, keys]
    moves = []
    for half, target in enumerate((weights, later)):
        for begin, end in zip(cuts, cuts[1:]):
            src = weights_in.at[:, half * keys + begin : half * keys + end]
            moves.append(pltpu.make_async_copy(src, target.at[:, begin:end], sems.at[len(moves)]))
    for move in moves[:3]:
        move.start()
    total = jnp.zeros(out.shape, jnp.float32)
    for index, (begin, end) in enumerate(zip(cuts, cuts[1:])):
        moves[index].wait()
        for move in moves[3 + 2 * index : min(5 + 2 * index, len(moves))]:
            move.start()
        total = total + jnp.dot(
            weights[:, begin:end], values[begin:end, :], preferred_element_type=jnp.float32
        )
    out[...] = total
    for move in moves[4:]:
        move.wait()


def attend_other_kernel(weights, denom, before, values, out):
    total = before[...] + jnp.dot(weights[...], values[...], preferred_element_type=jnp.float32)
    out[...] = (total / denom[...]).astype(jnp.bfloat16)


def attend_own(weights, values):
    lines, count = weights.shape
    keys = count // 2
    vmem = pl.BlockSpec(memory_space=pltpu.VMEM)
    return pl.pallas_call(
        attend_own_kernel,
        in_specs=[pl.BlockSpec(memory_space=pltpu.HBM), vmem],
        out_specs=[vmem, vmem],
        out_shape=[
            jax.ShapeDtypeStruct((lines, HD), jnp.float32),
            jax.ShapeDtypeStruct((lines, keys), jnp.bfloat16),
        ],
        scratch_shapes=[pltpu.VMEM((lines, keys), jnp.bfloat16), pltpu.SemaphoreType.DMA((8,))],
        compiler_params=pltpu.CompilerParams(vmem_limit_bytes=16 << 20),
        cost_estimate=pl.CostEstimate(
            flops=2 * lines * keys * HD, bytes_accessed=5_500_000, transcendentals=0
        ),
        name="attend_own",
    )(*in_hbm(weights), values)


def attend_other(weights, denom, before, values):
    lines, keys = weights.shape
    vmem = pl.BlockSpec(memory_space=pltpu.VMEM)
    return pl.pallas_call(
        attend_other_kernel,
        in_specs=[vmem] * 4,
        out_specs=vmem,
        out_shape=jax.ShapeDtypeStruct((lines, HD), jnp.bfloat16),
        compiler_params=pltpu.CompilerParams(vmem_limit_bytes=16 << 20),
        cost_estimate=pl.CostEstimate(
            flops=2 * lines * keys * HD, bytes_accessed=3_500_000, transcendentals=0
        ),
        name="attend_other",
    )(weights, denom, before, values)


def exchange(value, axes):
    return lax.all_to_all(value, axes, 0, 0, tiled=True)


def swap_cores(value):
    return lax.ppermute(value, "c", [(0, 1), (1, 0)])


def shards(residual, gate_first, gate_second, hyena_value, short_taps, long_taps, norm_gain, queries, attn_keys):
    rows, chans = residual.shape
    heads = chans // HD
    count = 32
    width = chans * 16

    core = lax.axis_index("c")
    side = lax.axis_index("zh")
    group = side * 16 + lax.axis_index("s") * 8 + core
    place = [core, 1 - core] + [group + owner * 2 for owner in range(heads)]
    for sender in (core, 1 - core):
        place += [sender + side * 16, sender - 1 + (1 - side) * 16]
    place = (jnp.stack(place) * rows).astype(jnp.int32)

    last, blocks = pack(gate_first, hyena_value, gate_second, attn_keys, queries)
    blocks = exchange(blocks.reshape(8, 2, rows, HD), ("s", "h"))
    halo = lax.ppermute(last, ROWS_AXES, [(source, source + 1) for source in range(count - 1)])
    early_parts = early(last, gate_second, residual, short_taps, long_taps)
    stream, squares = late(halo, *early_parts)

    far_squares = lax.ppermute(squares, "zh", [(0, 1)])
    far_squares, sent = lax.optimization_barrier((far_squares, stream))
    far_stream = lax.ppermute(sent, "zh", [(0, 1)])
    squares = jnp.concatenate([squares[0:1], far_squares[0:1]], axis=1)
    squares = jnp.broadcast_to(squares, (16, 1, 2 * rows))
    blocks, squares = lax.optimization_barrier((blocks, squares))
    gathered = exchange(squares, CHAN_AXES)
    packed = normalize(width, gathered, stream, far_stream, norm_gain.reshape(1, chans))
    keys_near = blocks[:, 0]
    my_queries = lax.dynamic_slice_in_dim(blocks, lax.axis_index("s") * heads, heads, 0)[:, 1]
    keys_far = lax.ppermute(keys_near, "zh", [(0, 1)])
    packed, keys_far = lax.optimization_barrier((packed, keys_far))
    values_own = exchange(packed.reshape(8, 2 * rows, HD), ("s", "h"))

    parts = [keys_near, swap_cores(keys_near), keys_far, swap_cores(keys_far)]
    weights, denom = score(place, my_queries.reshape(heads * rows, HD), parts)
    values_own, denom = lax.optimization_barrier((values_own, denom))
    values_other = swap_cores(values_own)
    result, weights_other = attend_own(weights, values_own.reshape(16 * rows, HD))
    result = attend_other(weights_other, denom, result, values_other.reshape(16 * rows, HD))
    attended = exchange(result.reshape(heads, rows, HD), "h").transpose(1, 0, 2).reshape(rows, chans)
    return stream, attended


def solution(mesh):
    inner = Mesh(mesh.devices.reshape(2, 2, 4, 2, 4, 4), ROWS_AXES + CHAN_AXES)
    both = P(ROWS_AXES, CHAN_AXES)
    return jax.shard_map(
        shards,
        mesh=inner,
        in_specs=(both, both, both, both, P(None, None, CHAN_AXES), P(None, CHAN_AXES), P(CHAN_AXES), both, both),
        out_specs=(both, both),
        check_vma=False,
    )
```
